32 devices in a mesh: seg: 2 (over x), genome: 16 (over z, y, core).
Axes of the slice: x: 2, y: 2, z: 4, core: 2. Of those that a mesh axis runs over, the one named last changes fastest.
Arguments:
- z_typed: float32 [256, 16384], P(None, ('seg', 'genome')), parts along dimension 1, may hold values from -8 to 8
- diag_inverse: float32 [32, 512, 512], P(('seg', 'genome')), parts along dimension 0
- coupling: float32 [32, 512, 256], P(('seg', 'genome')), parts along dimension 0
- impute_coef: bfloat16 [16384, 1024], P(('seg', 'genome')), parts along dimension 0, may hold values from -0.25 to 0.25
- anchor: int32 [16384], P(('seg', 'genome')), parts along dimension 0, may hold values from 0 to 8191, as said below
Outputs:
- imputed: float32 [256, 16384], P(None, ('seg', 'genome')), parts along dimension 1
The draws below stay inside these ranges and needn't reach their ends.
There are 2 independent parts, one for each index of `seg`. The reference program is written for one: setup_inputs(seed, part) draws one part's arguments, and reference() takes and returns one part's arrays. A program takes and returns all parts, laid end to end along the dimension named above; each array names one. Nothing has to cross between parts.
Inputs may be any that keep to these rules, and one draw needn't show every extreme that they name: The anchor of the untyped variant t lies in typed block t // 512, i.e. in columns (t // 512) * 512 to (t // 512 + 1) * 512 - 1.
All inputs are finite; a program needn't handle non-finite values.
Results may differ from the reference program's by a relative error of at most 0.002.
The reference program's roundings to bfloat16 on the way (of `alpha`) count: a program that leaves them out, or rounds other values in their place, can miss the bound.
Values may be sent and summed in bfloat16 or wider, within the bound.
A program may use at most 192 MiB of HBM per device.

```python
import jax
import jax.numpy as jnp
from jax import lax

TRAITS = 256
TYP_DEV = 512
HALF = 256
UNT_DEV = 512
BLOCKS = 16
TYPED = 8192
UNTYPED = 8192


def draw_diag_inverse(key, part):
    first, second = jax.random.split(key)
    noise = jax.random.normal(first, (BLOCKS, TYP_DEV, TYP_DEV), jnp.float32)
    lower_part = jnp.tril(noise, -1) * (0.3 / TYP_DEV ** 0.5)
    diag_values = jax.random.uniform(second, (BLOCKS, TYP_DEV), jnp.float32, 0.9, 1.1)
    rows_idx = jnp.arange(TYP_DEV)[:, None]
    cols_idx = jnp.arange(TYP_DEV)[None, :]
    on_diag = (rows_idx == cols_idx).astype(jnp.float32)
    return 0.25 * (lower_part + on_diag[None, :, :] * diag_values[:, :, None])


def block_order(one_key):
    return jax.random.permutation(one_key, HALF)


def draw_coupling(key, part):
    first, second, third, fourth = jax.random.split(key, 4)
    block_keys = jax.random.split(first, BLOCKS)
    orders = jax.vmap(block_order)(block_keys).astype(jnp.int32)
    signs = jax.random.randint(second, (BLOCKS, HALF), 0, 2).astype(jnp.float32) * 2.0 - 1.0
    columns = jnp.arange(HALF, dtype=jnp.int32)
    placed = (orders[:, :, None] == columns[None, None, :]).astype(jnp.float32) * signs[:, :, None]
    bottom_noise = jax.random.normal(third, (BLOCKS, HALF, HALF), jnp.float32)
    top_noise = jax.random.normal(fourth, (BLOCKS, TYP_DEV - HALF, HALF), jnp.float32)
    bottom = placed + bottom_noise * (0.05 / HALF ** 0.5)
    top = top_noise * (0.1 / TYP_DEV ** 0.5)
    factor = 0.5 ** (1.0 / BLOCKS) * 0.976 / 0.25
    return jnp.concatenate([top, bottom], axis=1) * factor


def draw_anchor(key, part):
    offsets = jax.random.randint(key, (UNTYPED,), 0, TYP_DEV)
    owners = jnp.arange(UNTYPED, dtype=jnp.int32) // UNT_DEV
    anchors = owners * TYP_DEV + offsets
    anchors = anchors.at[0].set(0)
    anchors = anchors.at[UNTYPED - 1].set(TYPED - 1)
    return anchors.astype(jnp.int32)


def level_of(stream_key, dims, cuts, smallest, top_value):
    def one(dim, blocks):
        heights = jax.random.uniform(jax.random.fold_in(jax.random.fold_in(stream_key, 6), dim), (blocks,), jnp.float32, smallest / len(cuts), top_value / len(cuts))
        return jnp.repeat(jnp.exp(heights), dims[dim] // blocks).reshape((-1,) + (1,) * (len(dims) - dim - 1))

    loudness = one(*cuts[0])
    for cut in cuts[1:]:
        loudness = loudness * one(*cut)
    return loudness


def bell_draw(rng, shape, width, limit, pieces=(), kind=jnp.bfloat16):
    drawn = width * jax.random.normal(rng, shape, jnp.float32)
    if pieces:
        drawn = drawn * level_of(rng, shape, pieces, -0.22, 0.18)
    return jnp.clip(drawn, -limit, limit).astype(kind)


def setup_inputs(seed: int = 0, part: int = 0) -> dict:
    splits = jax.random.split(jax.random.key(seed), 6)
    part_splits = jax.random.split(jax.random.fold_in(splits[5], part), 6)
    return {
        "z_typed": bell_draw(part_splits[0], (TRAITS, TYPED), 1.0, 8.0, ((1, 16),), jnp.float32),
        "diag_inverse": draw_diag_inverse(jax.random.fold_in(jax.random.fold_in(splits[5], part), 71), part),
        "coupling": draw_coupling(jax.random.fold_in(jax.random.fold_in(splits[5], part), 71), part),
        "impute_coef": bell_draw(part_splits[3], (UNTYPED, TYP_DEV + 2 * HALF), (2 * HALF) ** -0.5, 0.25, ((0, 16),)),
        "anchor": draw_anchor(jax.random.fold_in(jax.random.fold_in(splits[5], part), 71), part),
    }


precise = lax.Precision.HIGHEST


def reference(z_typed, diag_inverse, coupling, impute_coef, anchor):
    z_blocks = z_typed.reshape(TRAITS, BLOCKS, TYP_DEV).transpose(1, 0, 2)

    def forward_step(tail_in, inputs):
        z_block, inverse_block, couple = inputs
        projected = jnp.dot(inverse_block, couple, precision=precise)
        rows_now = jnp.dot(z_block, inverse_block.T, precision=precise) - jnp.dot(tail_in, projected.T, precision=precise)
        return rows_now[:, TYP_DEV - HALF:], rows_now

    start_tail = jnp.zeros((TRAITS, HALF), jnp.float32)
    _, all_rows = lax.scan(forward_step, start_tail, (z_blocks, diag_inverse, coupling))

    def backward_step(upper_in, inputs):
        rows_now, inverse_block, couple = inputs
        padded = jnp.concatenate([jnp.zeros((TRAITS, TYP_DEV - HALF), jnp.float32), upper_in], axis=1)
        solved = jnp.dot(rows_now - padded, inverse_block, precision=precise)
        return jnp.dot(solved, couple, precision=precise), solved

    _, all_alpha = lax.scan(backward_step, start_tail, (all_rows, diag_inverse, coupling), reverse=True)
    alpha = all_alpha.transpose(1, 0, 2).reshape(TRAITS, TYPED).astype(jnp.bfloat16)
    alpha_pad = jnp.concatenate([jnp.zeros((TRAITS, HALF), jnp.bfloat16), alpha, jnp.zeros((TRAITS, HALF), jnp.bfloat16)], axis=1)
    span = TYP_DEV + 2 * HALF
    coef_blocks = impute_coef.reshape(BLOCKS, UNT_DEV, span)
    anchor_blocks = anchor.reshape(BLOCKS, UNT_DEV)

    def impute_block(inputs):
        index, coef_block, anchor_block = inputs
        start = (index * TYP_DEV).astype(jnp.int32)
        window = lax.dynamic_slice_in_dim(alpha_pad, start, span, 1)
        columns = start - HALF + jnp.arange(span, dtype=jnp.int32)
        within = jnp.abs(columns[None, :] - anchor_block[:, None]) <= HALF
        masked = jnp.where(within, coef_block, jnp.zeros_like(coef_block))
        return lax.dot_general(window, masked, (((1,), (1,)), ((), ())), preferred_element_type=jnp.float32)

    parts = lax.map(impute_block, (jnp.arange(BLOCKS, dtype=jnp.int32), coef_blocks, anchor_blocks))
    return parts.transpose(1, 0, 2).reshape(TRAITS, UNTYPED)
```

```python
import functools

import jax
import jax.numpy as jnp
from jax import lax
from jax.experimental import pallas as pl
from jax.experimental.pallas import tpu as pltpu
from jax.sharding import PartitionSpec as P

F32 = jnp.float32
BF16 = jnp.bfloat16
NN = (((1,), (0,)), ((), ()))
NT = (((1,), (1,)), ((), ()))


def halves(x):
    high = x.astype(BF16)
    return high, (x - high.astype(F32)).astype(BF16)


def product(a, b, dims):
    return lax.dot_general(a, b, dims, preferred_element_type=F32)


def dot3(a, b, dims):
    return product(a[0], b[0], dims) + (product(a[0], b[1], dims) + product(a[1], b[0], dims))


def stacked(b):
    return jnp.concatenate([b[0], b[0], b[1]], axis=0)


def dot_stacked(x, weights):
    high, low = halves(x)
    return product(jnp.concatenate([high, low, high], axis=1), weights, NN)


def kernel(
    n, group, z_hbm, inverse_hbm, couple_hbm, coef_hbm, anchor_hbm, out_ref,
    z_ref, inverse_ref, couple_ref, coef_ref, anchor_ref, fetched,
    tail_in, tail_out, upper_in, upper_out, enter_f, enter_b, carry_f,
    map_f_in, map_f_out, map_b_in, map_b_out, left_in, right_in, left_out, right_out,
    top_rows, base, enter_rows_w, enter_add_w, enter_base_w, forward_w, backward_w, inv_hi, inv_lo, proj_hi, proj_lo, masked,
    pre_base_out, pre_base_in, pre_slope_out, pre_slope_in, ps, pr,
    own, add_in, add_out, gram_in, gram_out, rs, rr,
    sent, got, es, er,
):
    me = lax.axis_index("genome")
    count = n // group
    g, q = me // group, lax.rem(me, group)
    first, last = me == 0, me == n - 1
    head, tail = q == 0, q == group - 1
    start_group, end_group = g == 0, g == count - 1
    right, left = lax.rem(me + 1, n), lax.rem(me + n - 1, n)
    far_right, far_left = lax.rem(me + group, n), lax.rem(me + n - group, n)
    chunks, rows, half = tail_in.shape
    typed = inverse_ref.shape[0]
    top = typed - half
    traits = chunks * rows
    no = jnp.logical_not
    fetch = [
        pltpu.make_async_copy(src, dst, fetched.at[i])
        for i, (src, dst) in enumerate((
            (inverse_hbm, inverse_ref), (z_hbm, z_ref), (couple_hbm, couple_ref),
            (anchor_hbm, anchor_ref), (coef_hbm, coef_ref)))]
    for copy in fetch:
        copy.start()

    def both(*conditions):
        return functools.reduce(jnp.logical_and, conditions)

    barrier = pltpu.get_barrier_semaphore()
    middle = group // 2
    half_right, half_left = lax.rem(me + middle, n), lax.rem(me + n - middle, n)
    to_end = g == count - 2
    expected = 0
    for other, meets in (
            (left, no(first)), (right, no(last)), (half_left, both(head, no(start_group))),
            (half_right, both(q == middle, no(end_group))),
            (far_left, no(start_group)), (far_right, no(end_group))):
        expected += jnp.where(meets, 1, 0)

        @pl.when(meets)
        def _():
            pl.semaphore_signal(barrier, inc=1, device_id={"genome": other},
                                device_id_type=pl.DeviceIdType.MESH)

    def remote(src, dst, send, recv, other):
        return pltpu.make_async_remote_copy(
            src_ref=src, dst_ref=dst, send_sem=send, recv_sem=recv,
            device_id={"genome": other}, device_id_type=pl.DeviceIdType.MESH)

    def channel(index, src, dst, landing, other):
        return lambda c: remote(src.at[c], dst.at[c], sent.at[index, c], got.at[landing, c], other)

    map_f = channel(0, map_f_out, map_f_in, 0, right)
    local_f = channel(1, tail_out, tail_in, 1, right)
    group_f = channel(2, carry_f, enter_f, 2, far_right)
    head_f = channel(8, carry_f, enter_f, 2, right)
    pass_f_left = channel(3, enter_f, enter_f, 2, left)
    pass_f_right = channel(3, enter_f, enter_f, 2, right)
    map_b = channel(4, map_b_out, map_b_in, 3, left)
    local_b = channel(5, upper_out, upper_in, 4, left)
    group_b = channel(6, upper_out, enter_b, 5, far_left)
    half_b = channel(9, upper_out, enter_b, 5, half_left)
    pass_b = channel(7, enter_b, enter_b, 5, right)
    gives_left, gives_right = q > middle, q + 1 < middle
    gives_b = lax.rem(q + 1, middle) != 0

    def pass_on_f(c):
        @pl.when(gives_left)
        def _():
            pass_f_left(c).start()

        @pl.when(gives_right)
        def _():
            pass_f_right(c).start()

    def pass_on_b(c):
        @pl.when(gives_b)
        def _():
            pass_b(c).start()

    def carry_first(c):
        @pl.when(to_end)
        def _():
            head_f(c).start()

        @pl.when(no(to_end))
        def _():
            group_f(c).start()

    def carry_second(c):
        @pl.when(to_end)
        def _():
            group_f(c).start()

        @pl.when(no(to_end))
        def _():
            head_f(c).start()

    def to_left_gram():
        return remote(gram_out, gram_in, rs.at[0], rr.at[0], left)

    def to_left_add():
        return remote(add_out, add_in, rs.at[1], rr.at[1], left)

    def to_right():
        return remote(left_out, left_in, es.at[0], er.at[0], right)

    def to_left():
        return remote(right_out, right_in, es.at[1], er.at[1], left)

    def ahead(side):
        other = (right, left)[side]
        return (remote(pre_base_out.at[side], pre_base_in.at[side], ps.at[side, 0], pr.at[side, 0], other),
                remote(pre_slope_out.at[side], pre_slope_in.at[side], ps.at[side, 1], pr.at[side, 1], other))

    def each(condition, step):
        @pl.when(condition)
        def _():
            def go(c, _):
                step(c)
                return 0
            lax.fori_loop(0, chunks, go, 0)

    def clear(condition, ref):
        @pl.when(condition)
        def _():
            ref[...] = jnp.zeros_like(ref)

    def unit(condition, ref):
        @pl.when(condition)
        def _():
            row = lax.broadcasted_iota(jnp.int32, (half, half), 0)
            col = lax.broadcasted_iota(jnp.int32, (half, half), 1)
            ref[...] = (row == col).astype(F32).reshape(ref.shape)

    fetch[0].wait()
    hi, lo = halves(inverse_ref[...])
    inv_hi[...] = hi
    inv_lo[...] = lo
    fetch[1].wait()
    z_halves = halves(z_ref[...])
    solved = dot3(z_halves, (inv_hi[pl.ds(top, half), :], inv_lo[pl.ds(top, half), :]), NT)
    tail_out[...] = solved.reshape(chunks, rows, half)
    pl.semaphore_wait(barrier, expected)

    each(both(head, start_group, no(tail)), lambda c: local_f(c).start())

    fetch[2].wait()
    projected = dot3((inv_hi[...], inv_lo[...]), halves(couple_ref[...]), NN)
    hi, lo = halves(projected)
    proj_hi[...] = hi
    proj_lo[...] = lo
    chain = -projected[top:, :]
    chain_t = chain.T
    map_f_out[...] = chain_t.reshape(map_f_out.shape)
    map_b_out[...] = chain.reshape(map_b_out.shape)
    forward_w[...] = stacked(halves(chain_t))
    backward_w[...] = stacked(halves(chain))

    def start_head(c):
        map_f(c).start()
        local_f(c).start()
    each(both(head, no(start_group), no(tail)), start_head)
    each(both(tail, no(end_group), no(head)), lambda c: map_b(c).start())

    clear(head, tail_in)
    clear(tail, upper_in)
    clear(start_group, enter_f)
    clear(both(tail, end_group), gram_in)
    clear(both(tail, end_group), add_in)
    clear(end_group, enter_b)
    clear(first, left_in)
    clear(last, right_in)
    unit(jnp.logical_or(head, start_group), map_f_in)
    unit(jnp.logical_or(tail, end_group), map_b_in)

    def solve_top():
        solved_top = dot3(z_halves, (inv_hi[pl.ds(0, top), :], inv_lo[pl.ds(0, top), :]), NT)
        top_rows[...] = solved_top.reshape(chunks, rows, top)

    @pl.when(end_group)
    def _():
        proj = (proj_hi[...], proj_lo[...])
        projected_t = jnp.concatenate([projected[:top, :].T, -chain_t], axis=1)
        gram_out[...] = dot3(halves(projected_t), proj, NN)

        @pl.when(tail)
        def _():
            to_left_gram().start()

        solve_top()
        own[...] = tail_out[...].reshape(traits, half)
        rows_now = jnp.concatenate([top_rows[...].reshape(traits, top), own[...]], axis=1)
        add_out[...] = dot3(halves(rows_now), proj, NN)

        @pl.when(tail)
        def _():
            to_left_add().start()

    def fold():
        to_left_gram().wait_recv()
        gram = halves(gram_in[...])
        step_map = (forward_w[pl.ds(0, half), :], forward_w[pl.ds(2 * half, half), :])
        gram_out[...] += dot_stacked(dot3(step_map, gram, NN), backward_w[...])

        @pl.when(no(head))
        def _():
            to_left_gram().start()

        to_left_add().wait_recv()
        add_out[...] += dot_stacked(add_in[...] - dot3(halves(own[...]), gram, NN), backward_w[...])

        @pl.when(no(head))
        def _():
            to_left_add().start()

    @pl.when(both(end_group, no(tail), q >= middle))
    def _():
        fold()

    def step(c):
        map_f(c).wait_recv()
        local_f(c).wait_recv()
        moved = dot_stacked(jnp.concatenate([map_f_in[c], tail_in[c]], axis=0), forward_w[...])
        map_f_out[c] = moved[:half // chunks]
        tail_out[c] = tail_out[c] + moved[half // chunks:]

        @pl.when(no(tail))
        def _():
            map_f(c).start()
            local_f(c).start()
    each(both(no(start_group), no(head)), step)

    def step(c):
        local_f(c).wait_recv()
        tail_out[c] = tail_out[c] + dot_stacked(tail_in[c], forward_w[...])

        @pl.when(no(tail))
        def _():
            local_f(c).start()

        @pl.when(both(tail, start_group, no(end_group)))
        def _():
            carry_f[c] = tail_out[c]
            carry_first(c)
    each(both(start_group, no(head)), step)
    each(both(tail, start_group, no(end_group)), carry_second)
    @pl.when(both(end_group, q < middle))
    def _():
        fold()

    @pl.when(no(end_group))
    def _():
        solve_top()

    def step(c):
        map_b(c).wait_recv()
        map_b_out[c] = dot_stacked(map_b_in[c], backward_w[...])

        @pl.when(no(head))
        def _():
            map_b(c).start()
    each(both(no(end_group), no(tail)), step)

    fetch[3].wait()
    fetch[4].wait()

    def make_mask():
        spread = 128
        units = anchor_ref.shape[1]
        nearest = jnp.broadcast_to(anchor_ref[...], (spread, units)).T
        start = me * typed - half
        lanes = lax.broadcasted_iota(jnp.int32, (units, spread), 1)
        for j in range(0, typed + 2 * half, spread):
            within = jnp.abs(lanes + (start + j) - nearest) <= half
            coef = coef_ref[:, j:j + spread].astype(F32)
            masked[:, j:j + spread] = jnp.where(within, coef, 0.0).astype(BF16)

    @pl.when(g >= count // 2)
    def _():
        make_mask()

    def prepare():
        proj = (proj_hi[...], proj_lo[...])
        proj_top = (proj_hi[pl.ds(0, top), :], proj_lo[pl.ds(0, top), :])
        above = top_rows[...].reshape(traits, top) - dot3(
            halves(tail_in[...].reshape(traits, half)), proj_top, NT)
        top_rows[...] = above.reshape(chunks, rows, top)
        all_rows = jnp.concatenate([above, tail_out[...].reshape(traits, half)], axis=1)
        upper_out[...] = dot3(halves(all_rows), proj, NN).reshape(chunks, rows, half)

        @pl.when(no(start_group))
        def _():
            slope_top = -dot3(halves(map_f_in[...].reshape(half, half)), proj_top, NT)
            slope = jnp.concatenate([slope_top, map_f_out[...].reshape(half, half)], axis=1)
            slope_halves = halves(slope)
            enter_rows_w[...] = stacked(slope_halves)
            enter_add_w[...] = stacked(halves(dot3(slope_halves, proj, NN)))

    def prepare_end():
        proj_top = (proj_hi[pl.ds(0, top), :], proj_lo[pl.ds(0, top), :])
        inverse = (inv_hi[...], inv_lo[...])
        gram = halves(gram_in[...])
        low = tail_out[...].reshape(traits, half)
        above = top_rows[...].reshape(traits, top) - dot3(
            halves(tail_in[...].reshape(traits, half)), proj_top, NT)
        below = low - add_in[...] + dot3(halves(low), gram, NN)
        base[...] = dot3(halves(jnp.concatenate([above, below], axis=1)), inverse, NN)
        low = map_f_out[...].reshape(half, half)
        above = -dot3(halves(map_f_in[...].reshape(half, half)), proj_top, NT)
        below = low + dot3(halves(low), gram, NN)
        enter_rows_w[...] = stacked(halves(
            dot3(halves(jnp.concatenate([above, below], axis=1)), inverse, NN)))
        enter_add_w[...] = stacked(halves(gram_out[...]))

    relay = both(no(start_group), no(end_group), tail)

    @pl.when(both(no(relay), no(end_group)))
    def _():
        prepare()

    @pl.when(end_group)
    def _():
        prepare_end()

    @pl.when(relay)
    def _():
        whole = stacked(halves(map_f_out[...].reshape(half, half)))

        def go(c, _):
            group_f(c).wait_recv()
            pass_on_f(c)
            carry_f[c] = tail_out[c] + dot_stacked(enter_f[c], whole)
            carry_first(c)
            return 0
        lax.fori_loop(0, chunks, go, 0)
        each(True, carry_second)
        prepare()

    def step(c):
        group_f(c).wait_recv()
        pass_on_f(c)
    each(both(no(start_group), no(end_group), no(tail)), step)

    @pl.when(both(no(start_group), no(end_group)))
    def _():
        add = dot_stacked(enter_f[...].reshape(traits, half), enter_add_w[...])
        upper_out[...] += add.reshape(chunks, rows, half)

    each(both(tail, no(head), no(end_group)), lambda c: local_b(c).start())

    def step(c):
        local_b(c).wait_recv()
        upper_out[c] = upper_out[c] + dot_stacked(upper_in[c], backward_w[...])

        @pl.when(no(head))
        def _():
            local_b(c).start()
    each(both(no(tail), no(end_group)), step)

    def step(c):
        group_f(c).wait_recv()

        @pl.when(head)
        def _():
            upper_out[c] = add_out[pl.ds(pl.multiple_of(c * rows, rows), rows), :] - dot_stacked(
                enter_f[c], enter_add_w[...])
            group_b(c).start()
        pass_on_f(c)
    each(end_group, step)
    each(both(end_group, head), lambda c: half_b(c).start())

    @pl.when(end_group)
    def _():
        base[...] += dot_stacked(enter_f[...].reshape(traits, half), enter_rows_w[...])

    @pl.when(no(end_group))
    def _():
        all_rows = jnp.concatenate([top_rows[...].reshape(traits, top),
                                    tail_out[...].reshape(traits, half)], axis=1)
        base[...] = all_rows

        @pl.when(no(start_group))
        def _():
            base[...] += dot_stacked(enter_f[...].reshape(traits, half), enter_rows_w[...])

        base[:, top:] -= upper_in[...].reshape(traits, half)
        base[...] = dot3(halves(base[...]), (inv_hi[...], inv_lo[...]), NN)

    @pl.when(no(end_group))
    def _():
        slope = dot3(halves(map_b_in[...].reshape(half, half)),
                     (inv_hi[pl.ds(top, half), :], inv_lo[pl.ds(top, half), :]), NN)
        enter_base_w[...] = stacked(halves(slope))
        pre_base_out[0] = base[:, top:]
        pre_slope_out[0] = slope[:, top:]
        pre_base_out[1] = base[:, :half]
        pre_slope_out[1] = slope[:, :half]
        for copy in ahead(0):
            copy.start()

        @pl.when(no(head))
        def _():
            for copy in ahead(1):
                copy.start()

    @pl.when(g < count // 2)
    def _():
        make_mask()

    def drain_early():
        each(both(no(start_group), no(tail)), lambda c: map_f(c).wait_send())
        each(no(tail), lambda c: local_f(c).wait_send())
        each(both(tail, no(end_group)), lambda c: group_f(c).wait_send())
        each(both(tail, no(end_group)), lambda c: head_f(c).wait_send())
        each(both(jnp.logical_or(gives_left, gives_right), no(start_group)),
             lambda c: pass_f_left(c).wait_send())
        each(both(no(end_group), no(head)), lambda c: map_b(c).wait_send())
        each(both(no(head), no(end_group)), lambda c: local_b(c).wait_send())

    @pl.when(g < count // 2)
    def _():
        drain_early()

    @pl.when(both(no(end_group), head))
    def _():
        whole = stacked(halves(map_b_out[...].reshape(half, half)))

        def go(c, _):
            group_b(c).wait_recv()
            pass_on_b(c)

            @pl.when(no(start_group))
            def _():
                upper_out[c] = upper_out[c] + dot_stacked(enter_b[c], whole)
                group_b(c).start()
            return 0
        lax.fori_loop(0, chunks, go, 0)
        each(no(start_group), lambda c: half_b(c).start())

    def step(c):
        group_b(c).wait_recv()
        pass_on_b(c)
    each(both(no(end_group), no(head)), step)

    @pl.when(no(end_group))
    def _():
        base[...] -= dot_stacked(enter_b[...].reshape(traits, half), enter_base_w[...])

    weights = base[...].astype(BF16)
    left_out[...] = weights[:, top:]
    right_out[...] = weights[:, :half]

    late_right = both(end_group, no(last))
    late_left = both(no(first), jnp.logical_or(head, end_group))

    @pl.when(late_right)
    def _():
        to_right().start()

    @pl.when(late_left)
    def _():
        to_left().start()

    def edge(side, state):
        for copy in ahead(side):
            copy.wait_recv()
        return (pre_base_in[side] - dot_stacked(
            state.reshape(traits, half), stacked(halves(pre_slope_in[side])))).astype(BF16)

    @pl.when(both(no(end_group), no(head)))
    def _():
        left_in[...] = edge(0, enter_b[...])

    @pl.when(both(head, no(start_group)))
    def _():
        left_in[...] = edge(0, upper_out[...])

    @pl.when(both(no(end_group), no(tail)))
    def _():
        right_in[...] = edge(1, enter_b[...])

    out_ref[...] = product(weights, masked[:, half:half + typed], NT)

    @pl.when(both(no(last), jnp.logical_or(tail, end_group)))
    def _():
        to_left().wait_recv()

    out_ref[...] += product(right_in[...], masked[:, half + typed:], NT)

    @pl.when(both(end_group, no(head)))
    def _():
        to_right().wait_recv()

    out_ref[...] += product(left_in[...], masked[:, :half], NT)

    @pl.when(g >= count // 2)
    def _():
        drain_early()

    each(both(head, no(start_group)), lambda c: group_b(c).wait_send())
    each(both(head, no(start_group)), lambda c: half_b(c).wait_send())
    each(both(gives_b, no(end_group)), lambda c: pass_b(c).wait_send())

    @pl.when(both(end_group, no(head)))
    def _():
        to_left_gram().wait_send()
        to_left_add().wait_send()

    @pl.when(late_right)
    def _():
        to_right().wait_send()

    @pl.when(late_left)
    def _():
        to_left().wait_send()

    @pl.when(no(end_group))
    def _():
        for copy in ahead(0):
            copy.wait_send()

    @pl.when(both(no(end_group), no(head)))
    def _():
        for copy in ahead(1):
            copy.wait_send()


def per_device(n, z_typed, diag_inverse, coupling, impute_coef, anchor):
    traits, typed = z_typed.shape
    half = coupling.shape[2]
    units, span = impute_coef.shape
    top = typed - half
    chunks = next(k for k in (8, 4, 2, 1) if traits % (16 * k) == half % (8 * k) == 0 or k == 1)
    rows = traits // chunks
    group = 1
    while n % (2 * group) == 0 and 4 * group * group <= n:
        group *= 2
    state = pltpu.VMEM((chunks, rows, half), F32)
    whole_state = pltpu.VMEM((traits, half), F32)
    square = pltpu.VMEM((half, half), F32)
    edge = pltpu.VMEM((traits, half), BF16)
    chain_map = pltpu.VMEM((chunks, half // chunks, half), F32)
    return pl.pallas_call(
        functools.partial(kernel, n, group),
        out_shape=jax.ShapeDtypeStruct((traits, units), F32),
        in_specs=[pl.BlockSpec(memory_space=pltpu.HBM)] * 5,
        out_specs=pl.BlockSpec(memory_space=pltpu.VMEM),
        scratch_shapes=[
            pltpu.VMEM((traits, typed), F32), pltpu.VMEM((typed, typed), F32),
            pltpu.VMEM((typed, half), F32), pltpu.VMEM((units, span), BF16),
            pltpu.VMEM((1, units), jnp.int32), pltpu.SemaphoreType.DMA((5,)),
            state, state, state, state, state, state, state,
            chain_map, chain_map, chain_map, chain_map, edge, edge, edge, edge,
            pltpu.VMEM((chunks, rows, top), F32), pltpu.VMEM((traits, typed), F32),
            pltpu.VMEM((3 * half, typed), BF16), pltpu.VMEM((3 * half, half), BF16),
            pltpu.VMEM((3 * half, typed), BF16),
            pltpu.VMEM((3 * half, half), BF16), pltpu.VMEM((3 * half, half), BF16),
            pltpu.VMEM((typed, typed), BF16), pltpu.VMEM((typed, typed), BF16),
            pltpu.VMEM((typed, half), BF16), pltpu.VMEM((typed, half), BF16),
            pltpu.VMEM((units, span), BF16),
            pltpu.VMEM((2, traits, half), F32), pltpu.VMEM((2, traits, half), F32),
            pltpu.VMEM((2, half, half), F32), pltpu.VMEM((2, half, half), F32),
            pltpu.SemaphoreType.DMA((2, 2)), pltpu.SemaphoreType.DMA((2, 2)),
            whole_state, whole_state, whole_state, square, square,
            pltpu.SemaphoreType.DMA((2,)), pltpu.SemaphoreType.DMA((2,)),
            pltpu.SemaphoreType.DMA((10, chunks)), pltpu.SemaphoreType.DMA((6, chunks)),
            pltpu.SemaphoreType.DMA((2,)), pltpu.SemaphoreType.DMA((2,)),
        ],
        compiler_params=pltpu.CompilerParams(
            collective_id=0, has_side_effects=True, vmem_limit_bytes=int(53.25 * 1024 * 1024)),
    )(z_typed, diag_inverse[0], coupling[0], impute_coef, anchor.reshape(1, units))


def solution(mesh):
    shared = ("seg", "genome")
    in_specs = (P(None, shared), P(shared, None, None), P(shared, None, None),
                P(shared, None), P(shared))
    return jax.shard_map(
        functools.partial(per_device, mesh.shape["genome"]), mesh=mesh, in_specs=in_specs,
        out_specs=P(None, shared), check_vma=False)
```

```python
import functools

import jax
import jax.numpy as jnp
from jax import lax
from jax.experimental import pallas as pl
from jax.experimental.pallas import tpu as pltpu
from jax.sharding import PartitionSpec as P

F32 = jnp.float32
BF16 = jnp.bfloat16
NN = (((1,), (0,)), ((), ()))
NT = (((1,), (1,)), ((), ()))


def halves(x):
    high = x.astype(BF16)
    return high, (x - high.astype(F32)).astype(BF16)


def product(a, b, dims):
    return lax.dot_general(a, b, dims, preferred_element_type=F32)


def dot3(a, b, dims):
    return product(a[0], b[0], dims) + (product(a[0], b[1], dims) + product(a[1], b[0], dims))


def stacked(b):
    return jnp.concatenate([b[0], b[0], b[1]], axis=0)


def dot_stacked(x, weights):
    high, low = halves(x)
    return product(jnp.concatenate([high, low, high], axis=1), weights, NN)


def kernel(
    n, group, z_hbm, inverse_hbm, couple_hbm, coef_hbm, anchor_hbm, out_ref,
    z_ref, inverse_ref, couple_ref, coef_ref, anchor_ref, fetched,
    tail_in, tail_out, upper_in, upper_out, enter_f, enter_b, carry_f,
    map_f_in, map_f_out, map_b_in, map_b_out, left_in, right_in, left_out, right_out,
    top_rows, base, enter_rows_w, enter_add_w, enter_base_w, forward_w, backward_w, inv_hi, inv_lo, proj_hi, proj_lo, masked,
    pre_base_out, pre_base_in, pre_slope_out, pre_slope_in, ps, pr,
    own, add_in, add_out, gram_in, gram_out, rs, rr,
    sent, got, es, er,
):
    me = lax.axis_index("genome")
    count = n // group
    g, q = me // group, lax.rem(me, group)
    first, last = me == 0, me == n - 1
    head, tail = q == 0, q == group - 1
    start_group, end_group = g == 0, g == count - 1
    right, left = lax.rem(me + 1, n), lax.rem(me + n - 1, n)
    far_right, far_left = lax.rem(me + group, n), lax.rem(me + n - group, n)
    chunks, rows, half = tail_in.shape
    typed = inverse_ref.shape[0]
    top = typed - half
    traits = chunks * rows
    no = jnp.logical_not
    fetch = [
        pltpu.make_async_copy(src, dst, fetched.at[i])
        for i, (src, dst) in enumerate((
            (inverse_hbm, inverse_ref), (z_hbm, z_ref), (couple_hbm, couple_ref),
            (anchor_hbm, anchor_ref), (coef_hbm, coef_ref)))]
    for copy in fetch:
        copy.start()

    def both(*conditions):
        return functools.reduce(jnp.logical_and, conditions)

    barrier = pltpu.get_barrier_semaphore()
    middle = group // 2
    half_right, half_left = lax.rem(me + middle, n), lax.rem(me + n - middle, n)
    to_end = g == count - 2
    expected = 0
    for other, meets in (
            (left, no(first)), (right, no(last)), (half_left, both(head, no(start_group))),
            (half_right, both(q == middle, no(end_group))),
            (far_left, no(start_group)), (far_right, no(end_group))):
        expected += jnp.where(meets, 1, 0)

        @pl.when(meets)
        def _():
            pl.semaphore_signal(barrier, inc=1, device_id={"genome": other},
                                device_id_type=pl.DeviceIdType.MESH)

    def remote(src, dst, send, recv, other):
        return pltpu.make_async_remote_copy(
            src_ref=src, dst_ref=dst, send_sem=send, recv_sem=recv,
            device_id={"genome": other}, device_id_type=pl.DeviceIdType.MESH)

    def channel(index, src, dst, landing, other):
        return lambda c: remote(src.at[c], dst.at[c], sent.at[index, c], got.at[landing, c], other)

    map_f = channel(0, map_f_out, map_f_in, 0, right)
    local_f = channel(1, tail_out, tail_in, 1, right)
    group_f = channel(2, carry_f, enter_f, 2, far_right)
    head_f = channel(8, carry_f, enter_f, 2, right)
    pass_f_left = channel(3, enter_f, enter_f, 2, left)
    pass_f_right = channel(3, enter_f, enter_f, 2, right)
    map_b = channel(4, map_b_out, map_b_in, 3, left)
    local_b = channel(5, upper_out, upper_in, 4, left)
    group_b = channel(6, upper_out, enter_b, 5, far_left)
    half_b = channel(9, upper_out, enter_b, 5, half_left)
    pass_b = channel(7, enter_b, enter_b, 5, right)
    gives_left, gives_right = q > middle, q + 1 < middle
    gives_b = lax.rem(q + 1, middle) != 0

    def pass_on_f(c):
        @pl.when(gives_left)
        def _():
            pass_f_left(c).start()

        @pl.when(gives_right)
        def _():
            pass_f_right(c).start()

    def pass_on_b(c):
        @pl.when(gives_b)
        def _():
            pass_b(c).start()

    def carry_first(c):
        @pl.when(to_end)
        def _():
            head_f(c).start()

        @pl.when(no(to_end))
        def _():
            group_f(c).start()

    def carry_second(c):
        @pl.when(to_end)
        def _():
            group_f(c).start()

        @pl.when(no(to_end))
        def _():
            head_f(c).start()

    def to_left_gram():
        return remote(gram_out, gram_in, rs.at[0], rr.at[0], left)

    def to_left_add():
        return remote(add_out, add_in, rs.at[1], rr.at[1], left)

    def to_right():
        return remote(left_out, left_in, es.at[0], er.at[0], right)

    def to_left():
        return remote(right_out, right_in, es.at[1], er.at[1], left)

    def ahead(side):
        other = (right, left)[side]
        return (remote(pre_base_out.at[side], pre_base_in.at[side], ps.at[side, 0], pr.at[side, 0], other),
                remote(pre_slope_out.at[side], pre_slope_in.at[side], ps.at[side, 1], pr.at[side, 1], other))

    def each(condition, step):
        @pl.when(condition)
        def _():
            def go(c, _):
                step(c)
                return 0
            lax.fori_loop(0, chunks, go, 0)

    def clear(condition, ref):
        @pl.when(condition)
        def _():
            ref[...] = jnp.zeros_like(ref)

    def unit(condition, ref):
        @pl.when(condition)
        def _():
            row = lax.broadcasted_iota(jnp.int32, (half, half), 0)
            col = lax.broadcasted_iota(jnp.int32, (half, half), 1)
            ref[...] = (row == col).astype(F32).reshape(ref.shape)

    fetch[0].wait()
    hi, lo = halves(inverse_ref[...])
    inv_hi[...] = hi
    inv_lo[...] = lo
    fetch[1].wait()
    z_halves = halves(z_ref[...])
    solved = dot3(z_halves, (inv_hi[pl.ds(top, half), :], inv_lo[pl.ds(top, half), :]), NT)
    tail_out[...] = solved.reshape(chunks, rows, half)
    pl.semaphore_wait(barrier, expected)

    each(both(head, start_group, no(tail)), lambda c: local_f(c).start())

    fetch[2].wait()
    projected = dot3((inv_hi[...], inv_lo[...]), halves(couple_ref[...]), NN)
    hi, lo = halves(projected)
    proj_hi[...] = hi
    proj_lo[...] = lo
    chain = -projected[top:, :]
    chain_t = chain.T
    map_f_out[...] = chain_t.reshape(map_f_out.shape)
    map_b_out[...] = chain.reshape(map_b_out.shape)
    forward_w[...] = stacked(halves(chain_t))
    backward_w[...] = stacked(halves(chain))

    def start_head(c):
        map_f(c).start()
        local_f(c).start()
    each(both(head, no(start_group), no(tail)), start_head)
    each(both(tail, no(end_group), no(head)), lambda c: map_b(c).start())

    clear(head, tail_in)
    clear(both(tail, start_group), upper_in)
    clear(start_group, enter_f)
    clear(both(tail, no(start_group)), gram_in)
    clear(both(tail, no(start_group)), add_in)
    clear(end_group, enter_b)
    clear(first, left_in)
    clear(last, right_in)
    unit(jnp.logical_or(head, start_group), map_f_in)
    unit(jnp.logical_or(tail, end_group), map_b_in)

    def solve_top():
        solved_top = dot3(z_halves, (inv_hi[pl.ds(0, top), :], inv_lo[pl.ds(0, top), :]), NT)
        top_rows[...] = solved_top.reshape(chunks, rows, top)

    @pl.when(no(start_group))
    def _():
        proj = (proj_hi[...], proj_lo[...])
        projected_t = jnp.concatenate([projected[:top, :].T, -chain_t], axis=1)
        gram_out[...] = dot3(halves(projected_t), proj, NN)

        @pl.when(tail)
        def _():
            to_left_gram().start()

        solve_top()
        own[...] = tail_out[...].reshape(traits, half)
        rows_now = jnp.concatenate([top_rows[...].reshape(traits, top), own[...]], axis=1)
        add_out[...] = dot3(halves(rows_now), proj, NN)

        @pl.when(tail)
        def _():
            to_left_add().start()

    def fold():
        to_left_gram().wait_recv()
        gram = halves(gram_in[...])
        step_map = (forward_w[pl.ds(0, half), :], forward_w[pl.ds(2 * half, half), :])
        gram_out[...] += dot_stacked(dot3(step_map, gram, NN), backward_w[...])

        @pl.when(no(head))
        def _():
            to_left_gram().start()

        to_left_add().wait_recv()
        add_out[...] += dot_stacked(add_in[...] - dot3(halves(own[...]), gram, NN), backward_w[...])

        @pl.when(no(head))
        def _():
            to_left_add().start()

    @pl.when(both(no(start_group), no(tail), q >= middle))
    def _():
        fold()

    def step(c):
        map_f(c).wait_recv()
        local_f(c).wait_recv()
        moved = dot_stacked(jnp.concatenate([map_f_in[c], tail_in[c]], axis=0), forward_w[...])
        map_f_out[c] = moved[:half // chunks]
        tail_out[c] = tail_out[c] + moved[half // chunks:]

        @pl.when(no(tail))
        def _():
            map_f(c).start()
            local_f(c).start()
    each(both(no(start_group), no(head)), step)

    def step(c):
        local_f(c).wait_recv()
        tail_out[c] = tail_out[c] + dot_stacked(tail_in[c], forward_w[...])

        @pl.when(no(tail))
        def _():
            local_f(c).start()

        @pl.when(both(tail, start_group, no(end_group)))
        def _():
            carry_f[c] = tail_out[c]
            carry_first(c)
    each(both(start_group, no(head)), step)
    each(both(tail, start_group, no(end_group)), carry_second)
    @pl.when(both(no(start_group), q < middle))
    def _():
        fold()

    @pl.when(start_group)
    def _():
        solve_top()

    def step(c):
        map_b(c).wait_recv()
        map_b_out[c] = dot_stacked(map_b_in[c], backward_w[...])

        @pl.when(no(head))
        def _():
            map_b(c).start()
    each(both(no(end_group), no(tail)), step)

    fetch[3].wait()
    fetch[4].wait()

    def make_mask():
        spread = 128
        units = anchor_ref.shape[1]
        nearest = jnp.broadcast_to(anchor_ref[...], (spread, units)).T
        start = me * typed - half
        lanes = lax.broadcasted_iota(jnp.int32, (units, spread), 1)
        for j in range(0, typed + 2 * half, spread):
            within = jnp.abs(lanes + (start + j) - nearest) <= half
            coef = coef_ref[:, j:j + spread].astype(F32)
            masked[:, j:j + spread] = jnp.where(within, coef, 0.0).astype(BF16)

    @pl.when(g >= count // 2)
    def _():
        make_mask()

    def prepare():
        proj = (proj_hi[...], proj_lo[...])
        proj_top = (proj_hi[pl.ds(0, top), :], proj_lo[pl.ds(0, top), :])
        above = top_rows[...].reshape(traits, top) - dot3(
            halves(tail_in[...].reshape(traits, half)), proj_top, NT)
        top_rows[...] = above.reshape(chunks, rows, top)
        all_rows = jnp.concatenate([above, tail_out[...].reshape(traits, half)], axis=1)
        upper_out[...] = dot3(halves(all_rows), proj, NN).reshape(chunks, rows, half)

    def prepare_end():
        proj_top = (proj_hi[pl.ds(0, top), :], proj_lo[pl.ds(0, top), :])
        inverse = (inv_hi[...], inv_lo[...])
        gram = halves(gram_in[...])
        low = tail_out[...].reshape(traits, half)
        above = top_rows[...].reshape(traits, top) - dot3(
            halves(tail_in[...].reshape(traits, half)), proj_top, NT)
        below = low - add_in[...] + dot3(halves(low), gram, NN)
        base[...] = dot3(halves(jnp.concatenate([above, below], axis=1)), inverse, NN)
        low = map_f_out[...].reshape(half, half)
        above = -dot3(halves(map_f_in[...].reshape(half, half)), proj_top, NT)
        below = low + dot3(halves(low), gram, NN)
        enter_rows_w[...] = stacked(halves(
            dot3(halves(jnp.concatenate([above, below], axis=1)), inverse, NN)))
        enter_add_w[...] = stacked(halves(gram_out[...]))

    relay = both(no(start_group), no(end_group), tail)

    @pl.when(start_group)
    def _():
        prepare()

    @pl.when(both(no(relay), no(start_group)))
    def _():
        prepare_end()

    @pl.when(relay)
    def _():
        whole = stacked(halves(map_f_out[...].reshape(half, half)))

        def go(c, _):
            group_f(c).wait_recv()
            pass_on_f(c)
            carry_f[c] = tail_out[c] + dot_stacked(enter_f[c], whole)
            carry_first(c)
            return 0
        lax.fori_loop(0, chunks, go, 0)
        each(True, carry_second)
        prepare_end()

    each(both(tail, no(head), start_group), lambda c: local_b(c).start())

    def step(c):
        local_b(c).wait_recv()
        upper_out[c] = upper_out[c] + dot_stacked(upper_in[c], backward_w[...])

        @pl.when(no(head))
        def _():
            local_b(c).start()
    each(both(no(tail), start_group), step)

    def step(c):
        group_f(c).wait_recv()
        pass_on_f(c)

        @pl.when(head)
        def _():
            upper_out[c] = add_out[pl.ds(pl.multiple_of(c * rows, rows), rows), :] - dot_stacked(
                enter_f[c], enter_add_w[...])

        @pl.when(both(head, end_group))
        def _():
            group_b(c).start()
    each(both(no(start_group), no(relay)), step)
    each(both(end_group, head), lambda c: half_b(c).start())

    @pl.when(no(start_group))
    def _():
        base[...] += dot_stacked(enter_f[...].reshape(traits, half), enter_rows_w[...])

    @pl.when(start_group)
    def _():
        base[:, :top] = top_rows[...].reshape(traits, top)
        base[:, top:] = (tail_out[...] - upper_in[...]).reshape(traits, half)
        base[...] = dot3(halves(base[...]), (inv_hi[...], inv_lo[...]), NN)

    @pl.when(no(end_group))
    def _():
        slope = dot3(halves(map_b_in[...].reshape(half, half)),
                     (inv_hi[pl.ds(top, half), :], inv_lo[pl.ds(top, half), :]), NN)
        enter_base_w[...] = stacked(halves(slope))
        pre_base_out[0] = base[:, top:]
        pre_slope_out[0] = slope[:, top:]
        pre_base_out[1] = base[:, :half]
        pre_slope_out[1] = slope[:, :half]
        for copy in ahead(0):
            copy.start()

        @pl.when(no(head))
        def _():
            for copy in ahead(1):
                copy.start()

    @pl.when(g < count // 2)
    def _():
        make_mask()

    def drain_early():
        each(both(no(start_group), no(tail)), lambda c: map_f(c).wait_send())
        each(no(tail), lambda c: local_f(c).wait_send())
        each(both(tail, no(end_group)), lambda c: group_f(c).wait_send())
        each(both(tail, no(end_group)), lambda c: head_f(c).wait_send())
        each(both(jnp.logical_or(gives_left, gives_right), no(start_group)),
             lambda c: pass_f_left(c).wait_send())
        each(both(no(end_group), no(head)), lambda c: map_b(c).wait_send())
        each(both(no(head), start_group), lambda c: local_b(c).wait_send())

    @pl.when(g < count // 2)
    def _():
        drain_early()

    @pl.when(both(no(end_group), head))
    def _():
        whole = stacked(halves(map_b_out[...].reshape(half, half)))

        def go(c, _):
            group_b(c).wait_recv()
            pass_on_b(c)

            @pl.when(no(start_group))
            def _():
                upper_out[c] = upper_out[c] + dot_stacked(enter_b[c], whole)
                group_b(c).start()
            return 0
        lax.fori_loop(0, chunks, go, 0)
        each(no(start_group), lambda c: half_b(c).start())

    def step(c):
        group_b(c).wait_recv()
        pass_on_b(c)
    each(both(no(end_group), no(head)), step)

    @pl.when(no(end_group))
    def _():
        base[...] -= dot_stacked(enter_b[...].reshape(traits, half), enter_base_w[...])

    weights = base[...].astype(BF16)
    left_out[...] = weights[:, top:]
    right_out[...] = weights[:, :half]

    late_right = both(end_group, no(last))
    late_left = both(no(first), jnp.logical_or(head, end_group))

    @pl.when(late_right)
    def _():
        to_right().start()

    @pl.when(late_left)
    def _():
        to_left().start()

    def edge(side, state):
        for copy in ahead(side):
            copy.wait_recv()
        return (pre_base_in[side] - dot_stacked(
            state.reshape(traits, half), stacked(halves(pre_slope_in[side])))).astype(BF16)

    @pl.when(both(no(end_group), no(head)))
    def _():
        left_in[...] = edge(0, enter_b[...])

    @pl.when(both(head, no(start_group)))
    def _():
        left_in[...] = edge(0, upper_out[...])

    @pl.when(both(no(end_group), no(tail)))
    def _():
        right_in[...] = edge(1, enter_b[...])

    out_ref[...] = product(weights, masked[:, half:half + typed], NT)

    @pl.when(both(no(last), jnp.logical_or(tail, end_group)))
    def _():
        to_left().wait_recv()

    out_ref[...] += product(right_in[...], masked[:, half + typed:], NT)

    @pl.when(both(end_group, no(head)))
    def _():
        to_right().wait_recv()

    out_ref[...] += product(left_in[...], masked[:, :half], NT)

    @pl.when(g >= count // 2)
    def _():
        drain_early()

    each(both(head, no(start_group)), lambda c: group_b(c).wait_send())
    each(both(head, no(start_group)), lambda c: half_b(c).wait_send())
    each(both(gives_b, no(end_group)), lambda c: pass_b(c).wait_send())

    @pl.when(both(no(start_group), no(head)))
    def _():
        to_left_gram().wait_send()
        to_left_add().wait_send()

    @pl.when(late_right)
    def _():
        to_right().wait_send()

    @pl.when(late_left)
    def _():
        to_left().wait_send()

    @pl.when(no(end_group))
    def _():
        for copy in ahead(0):
            copy.wait_send()

    @pl.when(both(no(end_group), no(head)))
    def _():
        for copy in ahead(1):
            copy.wait_send()


def per_device(n, z_typed, diag_inverse, coupling, impute_coef, anchor):
    traits, typed = z_typed.shape
    half = coupling.shape[2]
    units, span = impute_coef.shape
    top = typed - half
    chunks = next(k for k in (8, 4, 2, 1) if traits % (16 * k) == half % (8 * k) == 0 or k == 1)
    rows = traits // chunks
    group = 1
    while n % (2 * group) == 0 and 4 * group * group <= n:
        group *= 2
    state = pltpu.VMEM((chunks, rows, half), F32)
    whole_state = pltpu.VMEM((traits, half), F32)
    square = pltpu.VMEM((half, half), F32)
    edge = pltpu.VMEM((traits, half), BF16)
    chain_map = pltpu.VMEM((chunks, half // chunks, half), F32)
    return pl.pallas_call(
        functools.partial(kernel, n, group),
        out_shape=jax.ShapeDtypeStruct((traits, units), F32),
        in_specs=[pl.BlockSpec(memory_space=pltpu.HBM)] * 5,
        out_specs=pl.BlockSpec(memory_space=pltpu.VMEM),
        scratch_shapes=[
            pltpu.VMEM((traits, typed), F32), pltpu.VMEM((typed, typed), F32),
            pltpu.VMEM((typed, half), F32), pltpu.VMEM((units, span), BF16),
            pltpu.VMEM((1, units), jnp.int32), pltpu.SemaphoreType.DMA((5,)),
            state, state, state, state, state, state, state,
            chain_map, chain_map, chain_map, chain_map, edge, edge, edge, edge,
            pltpu.VMEM((chunks, rows, top), F32), pltpu.VMEM((traits, typed), F32),
            pltpu.VMEM((3 * half, typed), BF16), pltpu.VMEM((3 * half, half), BF16),
            pltpu.VMEM((3 * half, typed), BF16),
            pltpu.VMEM((3 * half, half), BF16), pltpu.VMEM((3 * half, half), BF16),
            pltpu.VMEM((typed, typed), BF16), pltpu.VMEM((typed, typed), BF16),
            pltpu.VMEM((typed, half), BF16), pltpu.VMEM((typed, half), BF16),
            pltpu.VMEM((units, span), BF16),
            pltpu.VMEM((2, traits, half), F32), pltpu.VMEM((2, traits, half), F32),
            pltpu.VMEM((2, half, half), F32), pltpu.VMEM((2, half, half), F32),
            pltpu.SemaphoreType.DMA((2, 2)), pltpu.SemaphoreType.DMA((2, 2)),
            whole_state, whole_state, whole_state, square, square,
            pltpu.SemaphoreType.DMA((2,)), pltpu.SemaphoreType.DMA((2,)),
            pltpu.SemaphoreType.DMA((10, chunks)), pltpu.SemaphoreType.DMA((6, chunks)),
            pltpu.SemaphoreType.DMA((2,)), pltpu.SemaphoreType.DMA((2,)),
        ],
        compiler_params=pltpu.CompilerParams(
            collective_id=0, has_side_effects=True, vmem_limit_bytes=int(53.25 * 1024 * 1024)),
    )(z_typed, diag_inverse[0], coupling[0], impute_coef, anchor.reshape(1, units))


def solution(mesh):
    shared = ("seg", "genome")
    in_specs = (P(None, shared), P(shared, None, None), P(shared, None, None),
                P(shared, None), P(shared))
    return jax.shard_map(
        functools.partial(per_device, mesh.shape["genome"]), mesh=mesh, in_specs=in_specs,
        out_specs=P(None, shared), check_vma=False)
```

```python
import functools

import jax
import jax.numpy as jnp
from jax import lax
from jax.experimental import pallas as pl
from jax.experimental.pallas import tpu as pltpu
from jax.sharding import PartitionSpec as P

F32 = jnp.float32
BF16 = jnp.bfloat16
NN = (((1,), (0,)), ((), ()))
NT = (((1,), (1,)), ((), ()))


def halves(x):
    high = x.astype(BF16)
    return high, (x - high.astype(F32)).astype(BF16)


def product(a, b, dims):
    return lax.dot_general(a, b, dims, preferred_element_type=F32)


def dot3(a, b, dims):
    return product(a[0], b[0], dims) + (product(a[0], b[1], dims) + product(a[1], b[0], dims))


def stacked(b):
    return jnp.concatenate([b[0], b[0], b[1]], axis=0)


def dot_stacked(x, weights):
    high, low = halves(x)
    return product(jnp.concatenate([high, low, high], axis=1), weights, NN)


def kernel(
    n, group, z_hbm, inverse_hbm, couple_hbm, coef_hbm, anchor_hbm, out_ref,
    z_ref, inverse_ref, couple_ref, coef_ref, anchor_ref, fetched,
    tail_in, tail_out, upper_in, upper_out, enter_f, enter_b, carry_f,
    map_f_in, map_f_out, map_b_in, map_b_out, left_in, right_in, left_out, right_out,
    top_rows, base, enter_rows_w, enter_add_w, enter_base_w, forward_w, backward_w, inv_hi, inv_lo, proj_hi, proj_lo, masked,
    pre_base_out, pre_base_in, pre_slope_out, pre_slope_in, ps, pr,
    own, add_in, add_out, gram_in, gram_out, rs, rr, credit,
    sent, got, es, er,
):
    me = lax.axis_index("genome")
    count = n // group
    g, q = me // group, lax.rem(me, group)
    first, last = me == 0, me == n - 1
    head, tail = q == 0, q == group - 1
    start_group, end_group = g == 0, g == count - 1
    right, left = lax.rem(me + 1, n), lax.rem(me + n - 1, n)
    far_right, far_left = lax.rem(me + group, n), lax.rem(me + n - group, n)
    chunks, rows, half = tail_in.shape
    typed = inverse_ref.shape[0]
    top = typed - half
    traits = chunks * rows
    no = jnp.logical_not
    fetch = [
        pltpu.make_async_copy(src, dst, fetched.at[i])
        for i, (src, dst) in enumerate((
            (inverse_hbm, inverse_ref), (z_hbm, z_ref), (couple_hbm, couple_ref),
            (anchor_hbm, anchor_ref), (coef_hbm, coef_ref)))]
    for copy in fetch:
        copy.start()

    def both(*conditions):
        return functools.reduce(jnp.logical_and, conditions)

    barrier = pltpu.get_barrier_semaphore()
    middle = group // 2
    half_right, half_left = lax.rem(me + middle, n), lax.rem(me + n - middle, n)
    to_end = g == count - 2
    expected = 0
    for other, meets in (
            (left, no(first)), (right, no(last)), (half_left, both(head, no(start_group))),
            (half_right, both(q == middle, no(end_group))),
            (far_left, no(start_group)), (far_right, no(end_group))):
        expected += jnp.where(meets, 1, 0)

        @pl.when(meets)
        def _():
            pl.semaphore_signal(barrier, inc=1, device_id={"genome": other},
                                device_id_type=pl.DeviceIdType.MESH)

    def remote(src, dst, send, recv, other):
        return pltpu.make_async_remote_copy(
            src_ref=src, dst_ref=dst, send_sem=send, recv_sem=recv,
            device_id={"genome": other}, device_id_type=pl.DeviceIdType.MESH)

    def channel(index, src, dst, landing, other):
        return lambda c: remote(src.at[c], dst.at[c], sent.at[index, c], got.at[landing, c], other)

    map_f = channel(0, map_f_out, map_f_in, 0, right)
    local_f = channel(1, tail_out, tail_in, 1, right)
    group_f = channel(2, carry_f, enter_f, 2, far_right)
    head_f = channel(8, carry_f, enter_f, 2, right)
    pass_f_left = channel(3, enter_f, enter_f, 2, left)
    pass_f_right = channel(3, enter_f, enter_f, 2, right)
    map_b = channel(4, map_b_out, map_b_in, 3, left)
    local_b = channel(5, upper_out, upper_in, 4, left)
    group_b = channel(6, upper_out, enter_b, 5, far_left)
    half_b = channel(9, upper_out, enter_b, 5, half_left)
    pass_b = channel(7, enter_b, enter_b, 5, right)
    gives_left, gives_right = q > middle, q + 1 < middle
    gives_b = lax.rem(q + 1, middle) != 0

    def pass_on_f(c):
        @pl.when(gives_left)
        def _():
            pass_f_left(c).start()

        @pl.when(gives_right)
        def _():
            pass_f_right(c).start()

    def pass_on_b(c):
        @pl.when(gives_b)
        def _():
            pass_b(c).start()

    def carry_first(c):
        @pl.when(to_end)
        def _():
            head_f(c).start()

        @pl.when(no(to_end))
        def _():
            group_f(c).start()

    def carry_second(c):
        @pl.when(to_end)
        def _():
            group_f(c).start()

        @pl.when(no(to_end))
        def _():
            head_f(c).start()

    def to_left_gram():
        return remote(gram_out, gram_in, rs.at[0], rr.at[0], left)

    def to_left_add():
        return remote(add_out, add_in, rs.at[1], rr.at[1], left)

    def to_right():
        return remote(left_out, left_in, es.at[0], er.at[0], right)

    def to_left():
        return remote(right_out, right_in, es.at[1], er.at[1], left)

    def ahead(side):
        other = (right, left)[side]
        return (remote(pre_base_out.at[side], pre_base_in.at[side], ps.at[side, 0], pr.at[side, 0], other),
                remote(pre_slope_out.at[side], pre_slope_in.at[side], ps.at[side, 1], pr.at[side, 1], other))

    def each(condition, step):
        @pl.when(condition)
        def _():
            def go(c, _):
                step(c)
                return 0
            lax.fori_loop(0, chunks, go, 0)

    def clear(condition, ref):
        @pl.when(condition)
        def _():
            ref[...] = jnp.zeros_like(ref)

    def unit(condition, ref):
        @pl.when(condition)
        def _():
            row = lax.broadcasted_iota(jnp.int32, (half, half), 0)
            col = lax.broadcasted_iota(jnp.int32, (half, half), 1)
            ref[...] = (row == col).astype(F32).reshape(ref.shape)

    fetch[0].wait()
    hi, lo = halves(inverse_ref[...])
    inv_hi[...] = hi
    inv_lo[...] = lo
    fetch[1].wait()
    z_halves = halves(z_ref[...])
    solved = dot3(z_halves, (inv_hi[pl.ds(top, half), :], inv_lo[pl.ds(top, half), :]), NT)
    tail_out[...] = solved.reshape(chunks, rows, half)
    pl.semaphore_wait(barrier, expected)

    each(both(head, start_group, no(tail)), lambda c: local_f(c).start())

    fetch[2].wait()
    projected = dot3((inv_hi[...], inv_lo[...]), halves(couple_ref[...]), NN)
    hi, lo = halves(projected)
    proj_hi[...] = hi
    proj_lo[...] = lo
    chain = -projected[top:, :]
    chain_t = chain.T
    map_f_out[...] = chain_t.reshape(map_f_out.shape)
    map_b_out[...] = chain.reshape(map_b_out.shape)
    forward_w[...] = stacked(halves(chain_t))
    backward_w[...] = stacked(halves(chain))

    def start_head(c):
        map_f(c).start()
        local_f(c).start()
    each(both(head, no(start_group), no(tail)), start_head)
    each(both(tail, no(end_group), no(head)), lambda c: map_b(c).start())

    clear(head, tail_in)
    clear(both(tail, start_group), upper_in)
    clear(start_group, enter_f)
    clear(both(tail, no(start_group)), gram_in)
    clear(both(tail, no(start_group)), add_in)
    clear(end_group, enter_b)
    clear(first, left_in)
    clear(last, right_in)
    unit(jnp.logical_or(head, start_group), map_f_in)
    unit(jnp.logical_or(tail, end_group), map_b_in)

    def solve_top():
        solved_top = dot3(z_halves, (inv_hi[pl.ds(0, top), :], inv_lo[pl.ds(0, top), :]), NT)
        top_rows[...] = solved_top.reshape(chunks, rows, top)

    @pl.when(no(start_group))
    def _():
        proj = (proj_hi[...], proj_lo[...])
        projected_t = jnp.concatenate([projected[:top, :].T, -chain_t], axis=1)
        gram_out[...] = dot3(halves(projected_t), proj, NN)

        @pl.when(tail)
        def _():
            to_left_gram().start()

        solve_top()
        own[...] = tail_out[...].reshape(traits, half)
        rows_now = jnp.concatenate([top_rows[...].reshape(traits, top), own[...]], axis=1)
        add_out[...] = dot3(halves(rows_now), proj, NN)

        @pl.when(tail)
        def _():
            to_left_add().start()

    def fold():
        to_left_gram().wait_recv()
        gram = halves(gram_in[...])
        step_map = (forward_w[pl.ds(0, half), :], forward_w[pl.ds(2 * half, half), :])
        gram_out[...] += dot_stacked(dot3(step_map, gram, NN), backward_w[...])

        @pl.when(no(head))
        def _():
            to_left_gram().start()

        to_left_add().wait_recv()
        add_out[...] += dot_stacked(add_in[...] - dot3(halves(own[...]), gram, NN), backward_w[...])

        @pl.when(no(head))
        def _():
            to_left_add().start()

    @pl.when(both(no(start_group), no(tail), q >= middle))
    def _():
        fold()

    def step(c):
        map_f(c).wait_recv()
        local_f(c).wait_recv()
        moved = dot_stacked(jnp.concatenate([map_f_in[c], tail_in[c]], axis=0), forward_w[...])
        map_f_out[c] = moved[:half // chunks]
        tail_out[c] = tail_out[c] + moved[half // chunks:]

        @pl.when(no(tail))
        def _():
            map_f(c).start()
            local_f(c).start()
    each(both(no(start_group), no(head)), step)

    def step(c):
        local_f(c).wait_recv()
        tail_out[c] = tail_out[c] + dot_stacked(tail_in[c], forward_w[...])

        @pl.when(no(tail))
        def _():
            local_f(c).start()

        @pl.when(both(tail, start_group, no(end_group)))
        def _():
            carry_f[c] = tail_out[c]
            carry_first(c)
    each(both(start_group, no(head)), step)
    each(both(tail, start_group, no(end_group)), carry_second)
    @pl.when(both(no(start_group), q < middle))
    def _():
        fold()

    @pl.when(start_group)
    def _():
        solve_top()

    def step(c):
        map_b(c).wait_recv()
        map_b_out[c] = dot_stacked(map_b_in[c], backward_w[...])

        @pl.when(no(head))
        def _():
            map_b(c).start()
    each(both(no(end_group), no(tail)), step)

    fetch[3].wait()
    fetch[4].wait()

    def make_mask():
        spread = 128
        units = anchor_ref.shape[1]
        nearest = jnp.broadcast_to(anchor_ref[...], (spread, units)).T
        start = me * typed - half
        lanes = lax.broadcasted_iota(jnp.int32, (units, spread), 1)
        for j in range(0, typed + 2 * half, spread):
            within = jnp.abs(lanes + (start + j) - nearest) <= half
            coef = coef_ref[:, j:j + spread].astype(F32)
            masked[:, j:j + spread] = jnp.where(within, coef, 0.0).astype(BF16)

    @pl.when(g >= count // 2)
    def _():
        make_mask()

    def prepare():
        proj = (proj_hi[...], proj_lo[...])
        proj_top = (proj_hi[pl.ds(0, top), :], proj_lo[pl.ds(0, top), :])
        above = top_rows[...].reshape(traits, top) - dot3(
            halves(tail_in[...].reshape(traits, half)), proj_top, NT)
        top_rows[...] = above.reshape(chunks, rows, top)
        all_rows = jnp.concatenate([above, tail_out[...].reshape(traits, half)], axis=1)
        upper_out[...] = dot3(halves(all_rows), proj, NN).reshape(chunks, rows, half)

    def prepare_end():
        proj_top = (proj_hi[pl.ds(0, top), :], proj_lo[pl.ds(0, top), :])
        inverse = (inv_hi[...], inv_lo[...])
        gram = halves(gram_in[...])
        low = tail_out[...].reshape(traits, half)
        above = top_rows[...].reshape(traits, top) - dot3(
            halves(tail_in[...].reshape(traits, half)), proj_top, NT)
        below = low - add_in[...] + dot3(halves(low), gram, NN)
        base[...] = dot3(halves(jnp.concatenate([above, below], axis=1)), inverse, NN)
        low = map_f_out[...].reshape(half, half)
        above = -dot3(halves(map_f_in[...].reshape(half, half)), proj_top, NT)
        below = low + dot3(halves(low), gram, NN)
        enter_rows_w[...] = stacked(halves(
            dot3(halves(jnp.concatenate([above, below], axis=1)), inverse, NN)))
        enter_add_w[...] = stacked(halves(gram_out[...]))

    relay = both(no(start_group), no(end_group), tail)

    @pl.when(start_group)
    def _():
        prepare()

    @pl.when(both(no(relay), no(start_group)))
    def _():
        prepare_end()

    @pl.when(relay)
    def _():
        whole = stacked(halves(map_f_out[...].reshape(half, half)))

        def go(c, _):
            group_f(c).wait_recv()
            pass_on_f(c)
            carry_f[c] = tail_out[c] + dot_stacked(enter_f[c], whole)
            carry_first(c)
            return 0
        lax.fori_loop(0, chunks, go, 0)
        each(True, carry_second)
        prepare_end()

    each(both(tail, no(head), start_group), lambda c: local_b(c).start())

    def step(c):
        local_b(c).wait_recv()
        upper_out[c] = upper_out[c] + dot_stacked(upper_in[c], backward_w[...])

        @pl.when(no(head))
        def _():
            local_b(c).start()
    each(both(no(tail), start_group), step)

    def step(c):
        group_f(c).wait_recv()
        pass_on_f(c)

        @pl.when(head)
        def _():
            upper_out[c] = add_out[pl.ds(pl.multiple_of(c * rows, rows), rows), :] - dot_stacked(
                enter_f[c], enter_add_w[...])

        @pl.when(both(head, end_group))
        def _():
            group_b(c).start()
    each(both(no(start_group), no(relay)), step)
    each(both(end_group, head), lambda c: half_b(c).start())

    @pl.when(both(head, g == 1))
    def _():
        pl.semaphore_signal(credit, inc=1, device_id={"genome": left},
                            device_id_type=pl.DeviceIdType.MESH)

    @pl.when(no(start_group))
    def _():
        base[...] += dot_stacked(enter_f[...].reshape(traits, half), enter_rows_w[...])

    @pl.when(start_group)
    def _():
        base[:, :top] = top_rows[...].reshape(traits, top)
        base[:, top:] = (tail_out[...] - upper_in[...]).reshape(traits, half)
        base[...] = dot3(halves(base[...]), (inv_hi[...], inv_lo[...]), NN)

    @pl.when(no(end_group))
    def _():
        slope = dot3(halves(map_b_in[...].reshape(half, half)),
                     (inv_hi[pl.ds(top, half), :], inv_lo[pl.ds(top, half), :]), NN)
        enter_base_w[...] = stacked(halves(slope))
        pre_base_out[0] = base[:, top:]
        pre_slope_out[0] = slope[:, top:]
        pre_base_out[1] = base[:, :half]
        pre_slope_out[1] = slope[:, :half]
        each(tail, lambda c: group_f(c).wait_send())
        each(tail, lambda c: head_f(c).wait_send())
        @pl.when(no(head))
        def _():
            for copy in ahead(1):
                copy.start()

        @pl.when(both(tail, start_group))
        def _():
            pl.semaphore_wait(credit, 1)

        for copy in ahead(0):
            copy.start()

    @pl.when(g < count // 2)
    def _():
        make_mask()

    def drain_early():
        each(both(no(start_group), no(tail)), lambda c: map_f(c).wait_send())
        each(no(tail), lambda c: local_f(c).wait_send())
        each(both(jnp.logical_or(gives_left, gives_right), no(start_group)),
             lambda c: pass_f_left(c).wait_send())
        each(both(no(end_group), no(head)), lambda c: map_b(c).wait_send())
        each(both(no(head), start_group), lambda c: local_b(c).wait_send())

    @pl.when(g < count // 2)
    def _():
        drain_early()

    @pl.when(both(no(end_group), head))
    def _():
        whole = stacked(halves(map_b_out[...].reshape(half, half)))

        def go(c, _):
            group_b(c).wait_recv()
            pass_on_b(c)

            @pl.when(no(start_group))
            def _():
                upper_out[c] = upper_out[c] + dot_stacked(enter_b[c], whole)
                group_b(c).start()
            return 0
        lax.fori_loop(0, chunks, go, 0)
        each(no(start_group), lambda c: half_b(c).start())

    def step(c):
        group_b(c).wait_recv()
        pass_on_b(c)
    each(both(no(end_group), no(head)), step)

    @pl.when(no(end_group))
    def _():
        base[...] -= dot_stacked(enter_b[...].reshape(traits, half), enter_base_w[...])

    weights = base[...].astype(BF16)
    left_out[...] = weights[:, top:]
    right_out[...] = weights[:, :half]

    late_right = both(end_group, no(last))
    late_left = both(no(first), jnp.logical_or(head, end_group))

    @pl.when(late_right)
    def _():
        to_right().start()

    @pl.when(late_left)
    def _():
        to_left().start()

    def edge(side, state):
        for copy in ahead(side):
            copy.wait_recv()
        return (pre_base_in[side] - dot_stacked(
            state.reshape(traits, half), stacked(halves(pre_slope_in[side])))).astype(BF16)

    @pl.when(both(no(end_group), no(head)))
    def _():
        left_in[...] = edge(0, enter_b[...])

    @pl.when(both(head, no(start_group)))
    def _():
        left_in[...] = edge(0, upper_out[...])

    @pl.when(both(no(end_group), no(tail)))
    def _():
        right_in[...] = edge(1, enter_b[...])

    out_ref[...] = product(weights, masked[:, half:half + typed], NT)

    @pl.when(both(no(last), jnp.logical_or(tail, end_group)))
    def _():
        to_left().wait_recv()

    out_ref[...] += product(right_in[...], masked[:, half + typed:], NT)

    @pl.when(both(end_group, no(head)))
    def _():
        to_right().wait_recv()

    out_ref[...] += product(left_in[...], masked[:, :half], NT)

    @pl.when(g >= count // 2)
    def _():
        drain_early()

    each(both(head, no(start_group)), lambda c: group_b(c).wait_send())
    each(both(head, no(start_group)), lambda c: half_b(c).wait_send())
    each(both(gives_b, no(end_group)), lambda c: pass_b(c).wait_send())

    @pl.when(both(no(start_group), no(head)))
    def _():
        to_left_gram().wait_send()
        to_left_add().wait_send()

    @pl.when(late_right)
    def _():
        to_right().wait_send()

    @pl.when(late_left)
    def _():
        to_left().wait_send()

    @pl.when(no(end_group))
    def _():
        for copy in ahead(0):
            copy.wait_send()

    @pl.when(both(no(end_group), no(head)))
    def _():
        for copy in ahead(1):
            copy.wait_send()


def per_device(n, z_typed, diag_inverse, coupling, impute_coef, anchor):
    traits, typed = z_typed.shape
    half = coupling.shape[2]
    units, span = impute_coef.shape
    top = typed - half
    chunks = next(k for k in (8, 4, 2, 1) if traits % (16 * k) == half % (8 * k) == 0 or k == 1)
    rows = traits // chunks
    group = 1
    while n % (2 * group) == 0 and 4 * group * group <= n:
        group *= 2
    state = pltpu.VMEM((chunks, rows, half), F32)
    whole_state = pltpu.VMEM((traits, half), F32)
    square = pltpu.VMEM((half, half), F32)
    edge = pltpu.VMEM((traits, half), BF16)
    chain_map = pltpu.VMEM((chunks, half // chunks, half), F32)
    return pl.pallas_call(
        functools.partial(kernel, n, group),
        out_shape=jax.ShapeDtypeStruct((traits, units), F32),
        in_specs=[pl.BlockSpec(memory_space=pltpu.HBM)] * 5,
        out_specs=pl.BlockSpec(memory_space=pltpu.VMEM),
        scratch_shapes=[
            pltpu.VMEM((traits, typed), F32), pltpu.VMEM((typed, typed), F32),
            pltpu.VMEM((typed, half), F32), pltpu.VMEM((units, span), BF16),
            pltpu.VMEM((1, units), jnp.int32), pltpu.SemaphoreType.DMA((5,)),
            state, state, state, state, state, state, state,
            chain_map, chain_map, chain_map, chain_map, edge, edge, edge, edge,
            pltpu.VMEM((chunks, rows, top), F32), pltpu.VMEM((traits, typed), F32),
            pltpu.VMEM((3 * half, typed), BF16), pltpu.VMEM((3 * half, half), BF16),
            pltpu.VMEM((3 * half, typed), BF16),
            pltpu.VMEM((3 * half, half), BF16), pltpu.VMEM((3 * half, half), BF16),
            pltpu.VMEM((typed, typed), BF16), pltpu.VMEM((typed, typed), BF16),
            pltpu.VMEM((typed, half), BF16), pltpu.VMEM((typed, half), BF16),
            pltpu.VMEM((units, span), BF16),
            pltpu.VMEM((2, traits, half), F32), pltpu.VMEM((2, traits, half), F32),
            pltpu.VMEM((2, half, half), F32), pltpu.VMEM((2, half, half), F32),
            pltpu.SemaphoreType.DMA((2, 2)), pltpu.SemaphoreType.DMA((2, 2)),
            whole_state, whole_state, whole_state, square, square,
            pltpu.SemaphoreType.DMA((2,)), pltpu.SemaphoreType.DMA((2,)), pltpu.SemaphoreType.REGULAR,
            pltpu.SemaphoreType.DMA((10, chunks)), pltpu.SemaphoreType.DMA((6, chunks)),
            pltpu.SemaphoreType.DMA((2,)), pltpu.SemaphoreType.DMA((2,)),
        ],
        compiler_params=pltpu.CompilerParams(
            collective_id=0, has_side_effects=True, vmem_limit_bytes=int(53.25 * 1024 * 1024)),
    )(z_typed, diag_inverse[0], coupling[0], impute_coef, anchor.reshape(1, units))


def solution(mesh):
    shared = ("seg", "genome")
    in_specs = (P(None, shared), P(shared, None, None), P(shared, None, None),
                P(shared, None), P(shared))
    return jax.shard_map(
        functools.partial(per_device, mesh.shape["genome"]), mesh=mesh, in_specs=in_specs,
        out_specs=P(None, shared), check_vma=False)
```

```python
import functools

import jax
import jax.numpy as jnp
from jax import lax
from jax.experimental import pallas as pl
from jax.experimental.pallas import tpu as pltpu
from jax.sharding import PartitionSpec as P

F32 = jnp.float32
BF16 = jnp.bfloat16
NN = (((1,), (0,)), ((), ()))
NT = (((1,), (1,)), ((), ()))


def halves(x):
    high = x.astype(BF16)
    return high, (x - high.astype(F32)).astype(BF16)


def product(a, b, dims):
    return lax.dot_general(a, b, dims, preferred_element_type=F32)


def dot3(a, b, dims):
    return product(a[0], b[0], dims) + (product(a[0], b[1], dims) + product(a[1], b[0], dims))


def stacked(b):
    return jnp.concatenate([b[0], b[0], b[1]], axis=0)


def dot_stacked(x, weights):
    high, low = halves(x)
    return product(jnp.concatenate([high, low, high], axis=1), weights, NN)


def kernel(
    n, group, z_hbm, inverse_hbm, couple_hbm, coef_hbm, anchor_hbm, out_ref,
    z_ref, inverse_ref, couple_ref, coef_ref, anchor_ref, fetched,
    tail_in, tail_out, upper_in, upper_out, enter_f, enter_b, carry_f,
    map_f_in, map_f_out, map_b_in, map_b_out, left_in, right_in, left_out, right_out,
    top_rows, base, enter_rows_w, enter_add_w, enter_base_w, forward_w, backward_w, inv_hi, inv_lo, proj_hi, proj_lo, masked,
    pre_base_out, pre_base_in, pre_slope_out, pre_slope_in, ps, pr,
    own, add_in, add_out, gram_in, gram_out, rs, rr, credit,
    sent, got, es, er,
):
    me = lax.axis_index("genome")
    count = n // group
    g, q = me // group, lax.rem(me, group)
    first, last = me == 0, me == n - 1
    head, tail = q == 0, q == group - 1
    start_group, end_group = g == 0, g == count - 1
    right, left = lax.rem(me + 1, n), lax.rem(me + n - 1, n)
    far_right, far_left = lax.rem(me + group, n), lax.rem(me + n - group, n)
    chunks, rows, half = tail_in.shape
    typed = inverse_ref.shape[0]
    top = typed - half
    traits = chunks * rows
    no = jnp.logical_not
    fetch = [
        pltpu.make_async_copy(src, dst, fetched.at[i])
        for i, (src, dst) in enumerate((
            (inverse_hbm, inverse_ref), (z_hbm, z_ref), (couple_hbm, couple_ref),
            (anchor_hbm, anchor_ref), (coef_hbm, coef_ref)))]
    for copy in fetch:
        copy.start()

    def both(*conditions):
        return functools.reduce(jnp.logical_and, conditions)

    barrier = pltpu.get_barrier_semaphore()
    middle = group // 2
    half_right, half_left = lax.rem(me + middle, n), lax.rem(me + n - middle, n)
    to_end = g == count - 2
    expected = 0
    for other, meets in (
            (left, no(first)), (right, no(last)), (half_left, both(head, no(start_group))),
            (half_right, both(q == middle, no(end_group))),
            (far_left, no(start_group)), (far_right, no(end_group))):
        expected += jnp.where(meets, 1, 0)

        @pl.when(meets)
        def _():
            pl.semaphore_signal(barrier, inc=1, device_id={"genome": other},
                                device_id_type=pl.DeviceIdType.MESH)

    def remote(src, dst, send, recv, other):
        return pltpu.make_async_remote_copy(
            src_ref=src, dst_ref=dst, send_sem=send, recv_sem=recv,
            device_id={"genome": other}, device_id_type=pl.DeviceIdType.MESH)

    def channel(index, src, dst, landing, other):
        return lambda c: remote(src.at[c], dst.at[c], sent.at[index, c], got.at[landing, c], other)

    map_f = channel(0, map_f_out, map_f_in, 0, right)
    local_f = channel(1, tail_out, tail_in, 1, right)
    group_f = channel(2, carry_f, enter_f, 2, far_right)
    head_f = channel(8, carry_f, enter_f, 2, right)
    pass_f_left = channel(3, enter_f, enter_f, 2, left)
    pass_f_right = channel(3, enter_f, enter_f, 2, right)
    map_b = channel(4, map_b_out, map_b_in, 3, left)
    local_b = channel(5, upper_out, upper_in, 4, left)
    group_b = channel(6, upper_out, enter_b, 5, far_left)
    half_b = channel(9, upper_out, enter_b, 5, half_left)
    pass_b = channel(7, enter_b, enter_b, 5, right)
    gives_left, gives_right = q > middle, q + 1 < middle
    gives_b = lax.rem(q + 1, middle) != 0

    def pass_on_f(c):
        @pl.when(gives_left)
        def _():
            pass_f_left(c).start()

        @pl.when(gives_right)
        def _():
            pass_f_right(c).start()

    def pass_on_b(c):
        @pl.when(gives_b)
        def _():
            pass_b(c).start()

    def carry_first(c):
        @pl.when(to_end)
        def _():
            head_f(c).start()

        @pl.when(no(to_end))
        def _():
            group_f(c).start()

    def carry_second(c):
        @pl.when(to_end)
        def _():
            group_f(c).start()

        @pl.when(no(to_end))
        def _():
            head_f(c).start()

    def to_left_gram():
        return remote(gram_out, gram_in, rs.at[0], rr.at[0], left)

    def to_left_add():
        return remote(add_out, add_in, rs.at[1], rr.at[1], left)

    def to_right():
        return remote(left_out, left_in, es.at[0], er.at[0], right)

    def to_left():
        return remote(right_out, right_in, es.at[1], er.at[1], left)

    def ahead_base(side):
        return remote(pre_base_out.at[side], pre_base_in.at[side], ps.at[side, 0], pr.at[side, 0],
                      (right, left)[side])

    def ahead_slope(side):
        return remote(pre_slope_out.at[side], pre_slope_in.at[side], ps.at[side, 1], pr.at[side, 1],
                      (right, left)[side])

    def ahead(side):
        return ahead_base(side), ahead_slope(side)

    def each(condition, step):
        @pl.when(condition)
        def _():
            def go(c, _):
                step(c)
                return 0
            lax.fori_loop(0, chunks, go, 0)

    def clear(condition, ref):
        @pl.when(condition)
        def _():
            ref[...] = jnp.zeros_like(ref)

    def unit(condition, ref):
        @pl.when(condition)
        def _():
            row = lax.broadcasted_iota(jnp.int32, (half, half), 0)
            col = lax.broadcasted_iota(jnp.int32, (half, half), 1)
            ref[...] = (row == col).astype(F32).reshape(ref.shape)

    fetch[0].wait()
    hi, lo = halves(inverse_ref[...])
    inv_hi[...] = hi
    inv_lo[...] = lo
    fetch[1].wait()
    z_halves = halves(z_ref[...])
    solved = dot3(z_halves, (inv_hi[pl.ds(top, half), :], inv_lo[pl.ds(top, half), :]), NT)
    tail_out[...] = solved.reshape(chunks, rows, half)
    pl.semaphore_wait(barrier, expected)

    each(both(head, start_group, no(tail)), lambda c: local_f(c).start())

    fetch[2].wait()
    projected = dot3((inv_hi[...], inv_lo[...]), halves(couple_ref[...]), NN)
    hi, lo = halves(projected)
    proj_hi[...] = hi
    proj_lo[...] = lo
    chain = -projected[top:, :]
    chain_t = chain.T
    map_f_out[...] = chain_t.reshape(map_f_out.shape)
    map_b_out[...] = chain.reshape(map_b_out.shape)
    forward_w[...] = stacked(halves(chain_t))
    backward_w[...] = stacked(halves(chain))

    def start_head(c):
        map_f(c).start()
        local_f(c).start()
    each(both(head, no(start_group), no(tail)), start_head)
    each(both(tail, no(end_group), no(head)), lambda c: map_b(c).start())

    clear(head, tail_in)
    clear(both(tail, start_group), upper_in)
    clear(start_group, enter_f)
    clear(both(tail, no(start_group)), gram_in)
    clear(both(tail, no(start_group)), add_in)
    clear(end_group, enter_b)
    clear(first, left_in)
    clear(last, right_in)
    unit(jnp.logical_or(head, start_group), map_f_in)
    unit(jnp.logical_or(tail, end_group), map_b_in)

    def solve_top():
        solved_top = dot3(z_halves, (inv_hi[pl.ds(0, top), :], inv_lo[pl.ds(0, top), :]), NT)
        top_rows[...] = solved_top.reshape(chunks, rows, top)

    @pl.when(no(start_group))
    def _():
        proj = (proj_hi[...], proj_lo[...])
        projected_t = jnp.concatenate([projected[:top, :].T, -chain_t], axis=1)
        gram_out[...] = dot3(halves(projected_t), proj, NN)

        @pl.when(tail)
        def _():
            to_left_gram().start()

        solve_top()
        own[...] = tail_out[...].reshape(traits, half)
        rows_now = jnp.concatenate([top_rows[...].reshape(traits, top), own[...]], axis=1)
        add_out[...] = dot3(halves(rows_now), proj, NN)

        @pl.when(tail)
        def _():
            to_left_add().start()

    def fold():
        to_left_gram().wait_recv()
        gram = halves(gram_in[...])
        step_map = (forward_w[pl.ds(0, half), :], forward_w[pl.ds(2 * half, half), :])
        gram_out[...] += dot_stacked(dot3(step_map, gram, NN), backward_w[...])

        @pl.when(no(head))
        def _():
            to_left_gram().start()

        to_left_add().wait_recv()
        add_out[...] += dot_stacked(add_in[...] - dot3(halves(own[...]), gram, NN), backward_w[...])

        @pl.when(no(head))
        def _():
            to_left_add().start()

    @pl.when(both(no(start_group), no(tail), q >= middle))
    def _():
        fold()

    def step(c):
        map_f(c).wait_recv()
        local_f(c).wait_recv()
        moved = dot_stacked(jnp.concatenate([map_f_in[c], tail_in[c]], axis=0), forward_w[...])
        map_f_out[c] = moved[:half // chunks]
        tail_out[c] = tail_out[c] + moved[half // chunks:]

        @pl.when(no(tail))
        def _():
            map_f(c).start()
            local_f(c).start()
    each(both(no(start_group), no(head)), step)

    def step(c):
        local_f(c).wait_recv()
        tail_out[c] = tail_out[c] + dot_stacked(tail_in[c], forward_w[...])

        @pl.when(no(tail))
        def _():
            local_f(c).start()

        @pl.when(both(tail, start_group, no(end_group)))
        def _():
            carry_f[c] = tail_out[c]
            carry_first(c)
    each(both(start_group, no(head)), step)
    each(both(tail, start_group, no(end_group)), carry_second)
    @pl.when(both(no(start_group), q < middle))
    def _():
        fold()

    @pl.when(start_group)
    def _():
        solve_top()

    def map_step(c):
        map_b(c).wait_recv()
        map_b_out[c] = dot_stacked(map_b_in[c], backward_w[...])
        map_b(c).start()
    early = both(head, no(start_group), to_end)
    late_map = both(head, no(start_group), no(end_group), no(early))
    each(both(no(end_group), no(tail), no(head)), map_step)

    def map_last():
        def go(c, _):
            map_b(c).wait_recv()
            return 0
        lax.fori_loop(0, chunks, go, 0)
        map_b_out[...] = dot_stacked(
            map_b_in[...].reshape(half, half), backward_w[...]).reshape(map_b_out.shape)

    @pl.when(both(no(end_group), head, no(late_map)))
    def _():
        map_last()

    fetch[3].wait()
    fetch[4].wait()

    def make_mask():
        spread = 128
        units = anchor_ref.shape[1]
        nearest = jnp.broadcast_to(anchor_ref[...], (spread, units)).T
        start = me * typed - half
        lanes = lax.broadcasted_iota(jnp.int32, (units, spread), 1)
        for j in range(0, typed + 2 * half, spread):
            within = jnp.abs(lanes + (start + j) - nearest) <= half
            coef = coef_ref[:, j:j + spread].astype(F32)
            masked[:, j:j + spread] = jnp.where(within, coef, 0.0).astype(BF16)

    @pl.when(g >= count // 2)
    def _():
        make_mask()

    def prepare():
        proj = (proj_hi[...], proj_lo[...])
        proj_top = (proj_hi[pl.ds(0, top), :], proj_lo[pl.ds(0, top), :])
        above = top_rows[...].reshape(traits, top) - dot3(
            halves(tail_in[...].reshape(traits, half)), proj_top, NT)
        top_rows[...] = above.reshape(chunks, rows, top)
        all_rows = jnp.concatenate([above, tail_out[...].reshape(traits, half)], axis=1)
        upper_out[...] = dot3(halves(all_rows), proj, NN).reshape(chunks, rows, half)

    def prepare_end():
        proj_top = (proj_hi[pl.ds(0, top), :], proj_lo[pl.ds(0, top), :])
        inverse = (inv_hi[...], inv_lo[...])
        gram = halves(gram_in[...])
        low = tail_out[...].reshape(traits, half)
        above = top_rows[...].reshape(traits, top) - dot3(
            halves(tail_in[...].reshape(traits, half)), proj_top, NT)
        below = low - add_in[...] + dot3(halves(low), gram, NN)
        base[...] = dot3(halves(jnp.concatenate([above, below], axis=1)), inverse, NN)
        low = map_f_out[...].reshape(half, half)
        above = -dot3(halves(map_f_in[...].reshape(half, half)), proj_top, NT)
        below = low + dot3(halves(low), gram, NN)
        enter_rows_w[...] = stacked(halves(
            dot3(halves(jnp.concatenate([above, below], axis=1)), inverse, NN)))

    relay = both(no(start_group), no(end_group), tail)

    @pl.when(start_group)
    def _():
        prepare()

    @pl.when(both(no(relay), no(start_group), no(late_map), no(early)))
    def _():
        prepare_end()

    def make_slope():
        slope = dot3(halves(map_b_in[...].reshape(half, half)),
                     (inv_hi[pl.ds(top, half), :], inv_lo[pl.ds(top, half), :]), NN)
        enter_base_w[...] = stacked(halves(slope))
        pre_slope_out[0] = slope[:, top:]
        pre_slope_out[1] = slope[:, :half]

    inner = both(no(head), no(tail))

    @pl.when(both(no(end_group), inner))
    def _():
        make_slope()
        ahead_slope(0).start()
        ahead_slope(1).start()

    @pl.when(both(head, no(start_group)))
    def _():
        enter_add_w[...] = stacked(halves(gram_out[...]))

    @pl.when(relay)
    def _():
        whole = stacked(halves(map_f_out[...].reshape(half, half)))

        def go(c, _):
            group_f(c).wait_recv()
            pass_on_f(c)
            carry_f[c] = tail_out[c] + dot_stacked(enter_f[c], whole)
            carry_first(c)
            return 0
        lax.fori_loop(0, chunks, go, 0)
        each(True, carry_second)
        prepare_end()

    each(both(tail, no(head), start_group), lambda c: local_b(c).start())

    def step(c):
        local_b(c).wait_recv()
        upper_out[c] = upper_out[c] + dot_stacked(upper_in[c], backward_w[...])

        @pl.when(no(head))
        def _():
            local_b(c).start()
    each(both(no(tail), start_group), step)

    def step(c):
        group_f(c).wait_recv()
        pass_on_f(c)

        @pl.when(head)
        def _():
            upper_out[c] = add_out[pl.ds(pl.multiple_of(c * rows, rows), rows), :] - dot_stacked(
                enter_f[c], enter_add_w[...])

        @pl.when(both(head, end_group))
        def _():
            group_b(c).start()
    each(both(no(start_group), no(relay)), step)
    each(both(end_group, head), lambda c: half_b(c).start())

    def relay_back():
        whole = stacked(halves(map_b_out[...].reshape(half, half)))

        def go(c, _):
            group_b(c).wait_recv()
            pass_on_b(c)

            @pl.when(no(start_group))
            def _():
                upper_out[c] = upper_out[c] + dot_stacked(enter_b[c], whole)
                group_b(c).start()
            return 0
        lax.fori_loop(0, chunks, go, 0)
        each(no(start_group), lambda c: half_b(c).start())

    @pl.when(late_map)
    def _():
        map_last()

    @pl.when(early)
    def _():
        relay_back()

    @pl.when(jnp.logical_or(late_map, early))
    def _():
        prepare_end()

    @pl.when(both(head, g == 1))
    def _():
        pl.semaphore_signal(credit, inc=1, device_id={"genome": left},
                            device_id_type=pl.DeviceIdType.MESH)

    @pl.when(no(start_group))
    def _():
        base[...] += dot_stacked(enter_f[...].reshape(traits, half), enter_rows_w[...])

    @pl.when(start_group)
    def _():
        base[:, :top] = top_rows[...].reshape(traits, top)
        base[:, top:] = (tail_out[...] - upper_in[...]).reshape(traits, half)
        base[...] = dot3(halves(base[...]), (inv_hi[...], inv_lo[...]), NN)

    @pl.when(both(no(end_group), no(inner)))
    def _():
        make_slope()

    @pl.when(no(end_group))
    def _():
        pre_base_out[0] = base[:, top:]
        pre_base_out[1] = base[:, :half]
        each(tail, lambda c: group_f(c).wait_send())
        each(tail, lambda c: head_f(c).wait_send())

        @pl.when(no(head))
        def _():
            ahead_base(1).start()

        @pl.when(tail)
        def _():
            ahead_slope(1).start()

        @pl.when(both(tail, start_group))
        def _():
            pl.semaphore_wait(credit, 1)

        ahead_base(0).start()

        @pl.when(no(inner))
        def _():
            ahead_slope(0).start()

    @pl.when(g < count // 2)
    def _():
        make_mask()

    def drain_early():
        each(both(no(start_group), no(tail)), lambda c: map_f(c).wait_send())
        each(no(tail), lambda c: local_f(c).wait_send())
        each(both(jnp.logical_or(gives_left, gives_right), no(start_group)),
             lambda c: pass_f_left(c).wait_send())
        each(both(no(end_group), no(head)), lambda c: map_b(c).wait_send())
        each(both(no(head), start_group), lambda c: local_b(c).wait_send())

    @pl.when(g < count // 2)
    def _():
        drain_early()

    @pl.when(both(no(end_group), head, no(early)))
    def _():
        relay_back()

    def step(c):
        group_b(c).wait_recv()
        pass_on_b(c)
    each(both(no(end_group), no(head)), step)

    @pl.when(no(end_group))
    def _():
        base[...] -= dot_stacked(enter_b[...].reshape(traits, half), enter_base_w[...])

    weights = base[...].astype(BF16)
    left_out[...] = weights[:, top:]
    right_out[...] = weights[:, :half]

    late_right = both(end_group, no(last))
    late_left = both(no(first), jnp.logical_or(head, end_group))

    @pl.when(late_right)
    def _():
        to_right().start()

    @pl.when(late_left)
    def _():
        to_left().start()

    def edge(side, state):
        for copy in ahead(side):
            copy.wait_recv()
        return (pre_base_in[side] - dot_stacked(
            state.reshape(traits, half), stacked(halves(pre_slope_in[side])))).astype(BF16)

    @pl.when(both(no(end_group), no(head)))
    def _():
        left_in[...] = edge(0, enter_b[...])

    @pl.when(both(head, no(start_group)))
    def _():
        left_in[...] = edge(0, upper_out[...])

    @pl.when(both(no(end_group), no(tail)))
    def _():
        right_in[...] = edge(1, enter_b[...])

    out_ref[...] = product(weights, masked[:, half:half + typed], NT)

    @pl.when(both(no(last), jnp.logical_or(tail, end_group)))
    def _():
        to_left().wait_recv()

    out_ref[...] += product(right_in[...], masked[:, half + typed:], NT)

    @pl.when(both(end_group, no(head)))
    def _():
        to_right().wait_recv()

    out_ref[...] += product(left_in[...], masked[:, :half], NT)

    @pl.when(g >= count // 2)
    def _():
        drain_early()

    each(both(head, no(start_group)), lambda c: group_b(c).wait_send())
    each(both(head, no(start_group)), lambda c: half_b(c).wait_send())
    each(both(gives_b, no(end_group)), lambda c: pass_b(c).wait_send())

    @pl.when(both(no(start_group), no(head)))
    def _():
        to_left_gram().wait_send()
        to_left_add().wait_send()

    @pl.when(late_right)
    def _():
        to_right().wait_send()

    @pl.when(late_left)
    def _():
        to_left().wait_send()

    @pl.when(no(end_group))
    def _():
        for copy in ahead(0):
            copy.wait_send()

    @pl.when(both(no(end_group), no(head)))
    def _():
        for copy in ahead(1):
            copy.wait_send()


def per_device(n, z_typed, diag_inverse, coupling, impute_coef, anchor):
    traits, typed = z_typed.shape
    half = coupling.shape[2]
    units, span = impute_coef.shape
    top = typed - half
    chunks = next(k for k in (8, 4, 2, 1) if traits % (16 * k) == half % (8 * k) == 0 or k == 1)
    rows = traits // chunks
    group = 1
    while n % (2 * group) == 0 and 4 * group * group <= n:
        group *= 2
    state = pltpu.VMEM((chunks, rows, half), F32)
    whole_state = pltpu.VMEM((traits, half), F32)
    square = pltpu.VMEM((half, half), F32)
    edge = pltpu.VMEM((traits, half), BF16)
    chain_map = pltpu.VMEM((chunks, half // chunks, half), F32)
    return pl.pallas_call(
        functools.partial(kernel, n, group),
        out_shape=jax.ShapeDtypeStruct((traits, units), F32),
        in_specs=[pl.BlockSpec(memory_space=pltpu.HBM)] * 5,
        out_specs=pl.BlockSpec(memory_space=pltpu.VMEM),
        scratch_shapes=[
            pltpu.VMEM((traits, typed), F32), pltpu.VMEM((typed, typed), F32),
            pltpu.VMEM((typed, half), F32), pltpu.VMEM((units, span), BF16),
            pltpu.VMEM((1, units), jnp.int32), pltpu.SemaphoreType.DMA((5,)),
            state, state, state, state, state, state, state,
            chain_map, chain_map, chain_map, chain_map, edge, edge, edge, edge,
            pltpu.VMEM((chunks, rows, top), F32), pltpu.VMEM((traits, typed), F32),
            pltpu.VMEM((3 * half, typed), BF16), pltpu.VMEM((3 * half, half), BF16),
            pltpu.VMEM((3 * half, typed), BF16),
            pltpu.VMEM((3 * half, half), BF16), pltpu.VMEM((3 * half, half), BF16),
            pltpu.VMEM((typed, typed), BF16), pltpu.VMEM((typed, typed), BF16),
            pltpu.VMEM((typed, half), BF16), pltpu.VMEM((typed, half), BF16),
            pltpu.VMEM((units, span), BF16),
            pltpu.VMEM((2, traits, half), F32), pltpu.VMEM((2, traits, half), F32),
            pltpu.VMEM((2, half, half), F32), pltpu.VMEM((2, half, half), F32),
            pltpu.SemaphoreType.DMA((2, 2)), pltpu.SemaphoreType.DMA((2, 2)),
            whole_state, whole_state, whole_state, square, square,
            pltpu.SemaphoreType.DMA((2,)), pltpu.SemaphoreType.DMA((2,)), pltpu.SemaphoreType.REGULAR,
            pltpu.SemaphoreType.DMA((10, chunks)), pltpu.SemaphoreType.DMA((6, chunks)),
            pltpu.SemaphoreType.DMA((2,)), pltpu.SemaphoreType.DMA((2,)),
        ],
        compiler_params=pltpu.CompilerParams(
            collective_id=0, has_side_effects=True, vmem_limit_bytes=int(53.25 * 1024 * 1024)),
    )(z_typed, diag_inverse[0], coupling[0], impute_coef, anchor.reshape(1, units))


def solution(mesh):
    shared = ("seg", "genome")
    in_specs = (P(None, shared), P(shared, None, None), P(shared, None, None),
                P(shared, None), P(shared))
    return jax.shard_map(
        functools.partial(per_device, mesh.shape["genome"]), mesh=mesh, in_specs=in_specs,
        out_specs=P(None, shared), check_vma=False)
```

```python
import functools

import jax
import jax.numpy as jnp
from jax import lax
from jax.experimental import pallas as pl
from jax.experimental.pallas import tpu as pltpu
from jax.sharding import PartitionSpec as P

F32 = jnp.float32
BF16 = jnp.bfloat16
NN = (((1,), (0,)), ((), ()))
NT = (((1,), (1,)), ((), ()))


def halves(x):
    high = x.astype(BF16)
    return high, (x - high.astype(F32)).astype(BF16)


def product(a, b, dims):
    return lax.dot_general(a, b, dims, preferred_element_type=F32)


def dot3(a, b, dims):
    return product(a[0], b[0], dims) + (product(a[0], b[1], dims) + product(a[1], b[0], dims))


def stacked(b):
    return jnp.concatenate([b[0], b[0], b[1]], axis=0)


def dot_stacked(x, weights):
    high, low = halves(x)
    return product(jnp.concatenate([high, low, high], axis=1), weights, NN)


class Both:
    def __init__(self, *copies):
        self.copies = copies

    def start(self):
        for copy in self.copies:
            copy.start()

    def wait_recv(self):
        for copy in self.copies:
            copy.wait_recv()

    def wait_send(self):
        for copy in self.copies:
            copy.wait_send()


def kernel(
    n, group, z_hbm, inverse_hbm, couple_hbm, coef_hbm, anchor_hbm, out_ref,
    z_ref, inverse_ref, couple_ref, coef_ref, anchor_ref, fetched,
    tail_in, tail_out, upper_in, upper_out, enter_f, enter_b, carry_f,
    map_f_in, map_f_out, map_b_in, map_b_out, left_in, right_in, left_out, right_out,
    top_rows, base, enter_rows_w, enter_add_w, enter_base_w, forward_w, backward_w, inv_hi, inv_lo, proj_hi, proj_lo, masked,
    pre_base_out, pre_base_in, pre_slope_out, pre_slope_in, ps, pr,
    own, add_in, add_out, gram_in, gram_out, rs, rr, credit,
    upper_q, upper_s, enter_q, enter_s,
    sent, got, es, er,
):
    me = lax.axis_index("genome")
    count = n // group
    g, q = me // group, lax.rem(me, group)
    first, last = me == 0, me == n - 1
    head, tail = q == 0, q == group - 1
    start_group, end_group = g == 0, g == count - 1
    right, left = lax.rem(me + 1, n), lax.rem(me + n - 1, n)
    far_right, far_left = lax.rem(me + group, n), lax.rem(me + n - group, n)
    chunks, rows, half = tail_in.shape
    typed = inverse_ref.shape[0]
    top = typed - half
    traits = chunks * rows
    no = jnp.logical_not
    fetch = [
        pltpu.make_async_copy(src, dst, fetched.at[i])
        for i, (src, dst) in enumerate((
            (inverse_hbm, inverse_ref), (z_hbm, z_ref), (couple_hbm, couple_ref),
            (anchor_hbm, anchor_ref), (coef_hbm, coef_ref)))]
    for copy in fetch:
        copy.start()

    def both(*conditions):
        return functools.reduce(jnp.logical_and, conditions)

    barrier = pltpu.get_barrier_semaphore()
    middle = group // 2
    half_right, half_left = lax.rem(me + middle, n), lax.rem(me + n - middle, n)
    to_end = g == count - 2
    expected = 0
    for other, meets in (
            (left, no(first)), (right, no(last)), (half_left, both(head, no(start_group))),
            (half_right, both(q == middle, no(end_group))),
            (far_left, no(start_group)), (far_right, no(end_group))):
        expected += jnp.where(meets, 1, 0)

        @pl.when(meets)
        def _():
            pl.semaphore_signal(barrier, inc=1, device_id={"genome": other},
                                device_id_type=pl.DeviceIdType.MESH)

    def remote(src, dst, send, recv, other):
        return pltpu.make_async_remote_copy(
            src_ref=src, dst_ref=dst, send_sem=send, recv_sem=recv,
            device_id={"genome": other}, device_id_type=pl.DeviceIdType.MESH)

    def channel(index, src, dst, landing, other):
        return lambda c: remote(src.at[c], dst.at[c], sent.at[index, c], got.at[landing, c], other)

    map_f = channel(0, map_f_out, map_f_in, 0, right)
    local_f = channel(1, tail_out, tail_in, 1, right)
    group_f = channel(2, carry_f, enter_f, 2, far_right)
    head_f = channel(8, carry_f, enter_f, 2, right)
    pass_f_left = channel(3, enter_f, enter_f, 2, left)
    pass_f_right = channel(3, enter_f, enter_f, 2, right)
    map_b = channel(4, map_b_out, map_b_in, 3, left)
    local_b = channel(5, upper_out, upper_in, 4, left)

    def coded_channel(i, j, coded, scale, other):
        values, factors = channel(i, coded, enter_q, 5, other), channel(j, scale, enter_s, 6, other)
        return lambda c: Both(values(c), factors(c))

    group_b = coded_channel(6, 10, upper_q, upper_s, far_left)
    half_b = coded_channel(9, 11, upper_q, upper_s, half_left)
    pass_b = coded_channel(7, 12, enter_q, enter_s, right)

    def encode(c):
        values = upper_out[c]
        peak = jnp.maximum(jnp.max(jnp.abs(values), axis=0, keepdims=True), 1e-30)
        upper_s[c] = peak * (1.0 / 32000.0)
        upper_q[c] = jnp.round(values * (32000.0 / peak)).astype(jnp.int32).astype(jnp.int16)

    def decode(c):
        enter_b[c] = enter_q[c].astype(jnp.int32).astype(F32) * enter_s[c]

    gives_left, gives_right = q > middle, q + 1 < middle
    gives_b = lax.rem(q + 1, middle) != 0

    def pass_on_f(c):
        @pl.when(gives_left)
        def _():
            pass_f_left(c).start()

        @pl.when(gives_right)
        def _():
            pass_f_right(c).start()

    def pass_on_b(c):
        @pl.when(gives_b)
        def _():
            pass_b(c).start()

    def carry_first(c):
        @pl.when(to_end)
        def _():
            head_f(c).start()

        @pl.when(no(to_end))
        def _():
            group_f(c).start()

    def carry_second(c):
        @pl.when(to_end)
        def _():
            group_f(c).start()

        @pl.when(no(to_end))
        def _():
            head_f(c).start()

    def to_left_gram():
        return remote(gram_out, gram_in, rs.at[0], rr.at[0], left)

    def to_left_add():
        return remote(add_out, add_in, rs.at[1], rr.at[1], left)

    def to_right():
        return remote(left_out, left_in, es.at[0], er.at[0], right)

    def to_left():
        return remote(right_out, right_in, es.at[1], er.at[1], left)

    def ahead_base(side):
        return remote(pre_base_out.at[side], pre_base_in.at[side], ps.at[side, 0], pr.at[side, 0],
                      (right, left)[side])

    def ahead_slope(side):
        return remote(pre_slope_out.at[side], pre_slope_in.at[side], ps.at[side, 1], pr.at[side, 1],
                      (right, left)[side])

    def ahead(side):
        return ahead_base(side), ahead_slope(side)

    def each(condition, step):
        @pl.when(condition)
        def _():
            def go(c, _):
                step(c)
                return 0
            lax.fori_loop(0, chunks, go, 0)

    def clear(condition, ref):
        @pl.when(condition)
        def _():
            ref[...] = jnp.zeros_like(ref)

    def unit(condition, ref):
        @pl.when(condition)
        def _():
            row = lax.broadcasted_iota(jnp.int32, (half, half), 0)
            col = lax.broadcasted_iota(jnp.int32, (half, half), 1)
            ref[...] = (row == col).astype(F32).reshape(ref.shape)

    fetch[0].wait()
    hi, lo = halves(inverse_ref[...])
    inv_hi[...] = hi
    inv_lo[...] = lo
    fetch[1].wait()
    z_halves = halves(z_ref[...])
    solved = dot3(z_halves, (inv_hi[pl.ds(top, half), :], inv_lo[pl.ds(top, half), :]), NT)
    tail_out[...] = solved.reshape(chunks, rows, half)
    pl.semaphore_wait(barrier, expected)

    each(both(head, start_group, no(tail)), lambda c: local_f(c).start())

    fetch[2].wait()
    projected = dot3((inv_hi[...], inv_lo[...]), halves(couple_ref[...]), NN)
    hi, lo = halves(projected)
    proj_hi[...] = hi
    proj_lo[...] = lo
    chain = -projected[top:, :]
    chain_t = chain.T
    map_f_out[...] = chain_t.reshape(map_f_out.shape)
    map_b_out[...] = chain.reshape(map_b_out.shape)
    forward_w[...] = stacked(halves(chain_t))
    backward_w[...] = stacked(halves(chain))

    each(both(head, no(start_group), no(tail)), lambda c: map_f(c).start())
    each(both(head, no(start_group), no(tail)), lambda c: local_f(c).start())
    each(both(tail, no(end_group), no(head)), lambda c: map_b(c).start())

    clear(head, tail_in)
    clear(both(tail, start_group), upper_in)
    clear(start_group, enter_f)
    clear(both(tail, no(start_group)), gram_in)
    clear(both(tail, no(start_group)), add_in)
    clear(end_group, enter_b)
    clear(first, left_in)
    clear(last, right_in)
    unit(jnp.logical_or(head, start_group), map_f_in)
    unit(jnp.logical_or(tail, end_group), map_b_in)

    def solve_top():
        solved_top = dot3(z_halves, (inv_hi[pl.ds(0, top), :], inv_lo[pl.ds(0, top), :]), NT)
        top_rows[...] = solved_top.reshape(chunks, rows, top)

    @pl.when(no(start_group))
    def _():
        proj = (proj_hi[...], proj_lo[...])
        projected_t = jnp.concatenate([projected[:top, :].T, -chain_t], axis=1)
        gram_out[...] = dot3(halves(projected_t), proj, NN)

        @pl.when(tail)
        def _():
            to_left_gram().start()

        solve_top()
        own[...] = tail_out[...].reshape(traits, half)
        rows_now = jnp.concatenate([top_rows[...].reshape(traits, top), own[...]], axis=1)
        add_out[...] = dot3(halves(rows_now), proj, NN)

        @pl.when(tail)
        def _():
            to_left_add().start()

    def fold():
        to_left_gram().wait_recv()
        gram = halves(gram_in[...])
        step_map = (forward_w[pl.ds(0, half), :], forward_w[pl.ds(2 * half, half), :])
        gram_out[...] += dot_stacked(dot3(step_map, gram, NN), backward_w[...])

        @pl.when(no(head))
        def _():
            to_left_gram().start()

        to_left_add().wait_recv()
        add_out[...] += dot_stacked(add_in[...] - dot3(halves(own[...]), gram, NN), backward_w[...])

        @pl.when(no(head))
        def _():
            to_left_add().start()

    def map_step(c):
        map_b(c).wait_recv()
        map_b_out[c] = dot_stacked(map_b_in[c], backward_w[...])
        map_b(c).start()
    soon_map = both(no(start_group), no(end_group), no(tail), no(head), q >= middle)

    @pl.when(both(no(start_group), no(tail), q >= middle))
    def _():
        fold()

    each(soon_map, map_step)

    relay = both(no(start_group), no(end_group), tail)

    def step(c):
        map_f(c).wait_recv()
        map_f_out[c] = dot_stacked(map_f_in[c], forward_w[...])

        @pl.when(no(tail))
        def _():
            map_f(c).start()
    each(both(no(start_group), no(head)), step)

    def add_local(c):
        local_f(c).wait_recv()
        tail_out[c] = tail_out[c] + dot_stacked(tail_in[c], forward_w[...])

    def step(c):
        add_local(c)

        @pl.when(no(tail))
        def _():
            local_f(c).start()
    each(both(no(start_group), no(head), no(relay)), step)

    def step(c):
        local_f(c).wait_recv()
        tail_out[c] = tail_out[c] + dot_stacked(tail_in[c], forward_w[...])

        @pl.when(no(tail))
        def _():
            local_f(c).start()

        @pl.when(both(tail, start_group, no(end_group)))
        def _():
            carry_f[c] = tail_out[c]
            carry_first(c)
    each(both(start_group, no(head)), step)
    each(both(tail, start_group, no(end_group)), carry_second)
    @pl.when(both(no(start_group), q < middle))
    def _():
        fold()

    @pl.when(start_group)
    def _():
        solve_top()

    last_head = both(end_group, head)
    early = both(head, no(start_group), to_end)
    late_map = both(head, no(start_group), no(end_group), no(early))
    each(both(no(end_group), no(tail), no(head), no(soon_map)), map_step)

    def map_last():
        def go(c, _):
            map_b(c).wait_recv()
            return 0
        lax.fori_loop(0, chunks, go, 0)
        map_b_out[...] = dot_stacked(
            map_b_in[...].reshape(half, half), backward_w[...]).reshape(map_b_out.shape)

    @pl.when(both(no(end_group), head, no(late_map)))
    def _():
        map_last()

    fetch[3].wait()
    fetch[4].wait()

    def make_mask():
        spread = 128
        units = anchor_ref.shape[1]
        nearest = jnp.broadcast_to(anchor_ref[...], (spread, units)).T
        start = me * typed - half
        lanes = lax.broadcasted_iota(jnp.int32, (units, spread), 1)
        for j in range(0, typed + 2 * half, spread):
            within = jnp.abs(lanes + (start + j) - nearest) <= half
            coef = coef_ref[:, j:j + spread].astype(F32)
            masked[:, j:j + spread] = jnp.where(within, coef, 0.0).astype(BF16)

    @pl.when(g >= count // 2)
    def _():
        make_mask()

    def prepare():
        proj = (proj_hi[...], proj_lo[...])
        proj_top = (proj_hi[pl.ds(0, top), :], proj_lo[pl.ds(0, top), :])
        above = top_rows[...].reshape(traits, top) - dot3(
            halves(tail_in[...].reshape(traits, half)), proj_top, NT)
        top_rows[...] = above.reshape(chunks, rows, top)
        all_rows = jnp.concatenate([above, tail_out[...].reshape(traits, half)], axis=1)
        upper_out[...] = dot3(halves(all_rows), proj, NN).reshape(chunks, rows, half)

    def prepare_end():
        proj_top = (proj_hi[pl.ds(0, top), :], proj_lo[pl.ds(0, top), :])
        inverse = (inv_hi[...], inv_lo[...])
        gram = halves(gram_in[...])
        low = tail_out[...].reshape(traits, half)
        above = top_rows[...].reshape(traits, top) - dot3(
            halves(tail_in[...].reshape(traits, half)), proj_top, NT)
        below = low - add_in[...] + dot3(halves(low), gram, NN)
        base[...] = dot3(halves(jnp.concatenate([above, below], axis=1)), inverse, NN)
        low = map_f_out[...].reshape(half, half)
        above = -dot3(halves(map_f_in[...].reshape(half, half)), proj_top, NT)
        below = low + dot3(halves(low), gram, NN)
        enter_rows_w[...] = stacked(halves(
            dot3(halves(jnp.concatenate([above, below], axis=1)), inverse, NN)))

    @pl.when(start_group)
    def _():
        prepare()

    @pl.when(both(no(relay), no(start_group), no(late_map), no(early)))
    def _():
        prepare_end()

    def make_slope():
        slope = dot3(halves(map_b_in[...].reshape(half, half)),
                     (inv_hi[pl.ds(top, half), :], inv_lo[pl.ds(top, half), :]), NN)
        enter_base_w[...] = stacked(halves(slope))
        pre_slope_out[0] = slope[:, top:]
        pre_slope_out[1] = slope[:, :half]

    inner = both(no(head), no(tail))

    @pl.when(both(no(end_group), inner))
    def _():
        make_slope()
        ahead_slope(0).start()
        ahead_slope(1).start()

    @pl.when(both(head, no(start_group)))
    def _():
        enter_add_w[...] = stacked(halves(gram_out[...]))

    @pl.when(relay)
    def _():
        whole = stacked(halves(map_f_out[...].reshape(half, half)))

        def go(c, _):
            add_local(c)
            group_f(c).wait_recv()
            pass_on_f(c)
            carry_f[c] = tail_out[c] + dot_stacked(enter_f[c], whole)
            carry_first(c)
            return 0
        lax.fori_loop(0, chunks, go, 0)
        each(True, carry_second)
        prepare_end()

    each(both(tail, no(head), start_group), lambda c: local_b(c).start())

    def step(c):
        local_b(c).wait_recv()
        upper_out[c] = upper_out[c] + dot_stacked(upper_in[c], backward_w[...])

        @pl.when(no(head))
        def _():
            local_b(c).start()
    each(both(no(tail), start_group), step)

    def step(c):
        group_f(c).wait_recv()
        pass_on_f(c)

        @pl.when(last_head)
        def _():
            upper_out[c] = add_out[pl.ds(pl.multiple_of(c * rows, rows), rows), :] - dot_stacked(
                enter_f[c], enter_add_w[...])
            encode(c)
            group_b(c).start()
    each(both(no(start_group), no(relay)), step)

    @pl.when(both(head, no(start_group), no(end_group)))
    def _():
        upper_out[...] = (add_out[...] - dot_stacked(
            enter_f[...].reshape(traits, half), enter_add_w[...])).reshape(chunks, rows, half)
    each(both(end_group, head), lambda c: half_b(c).start())

    def relay_back():
        whole = stacked(halves(map_b_out[...].reshape(half, half)))

        def go(c, _):
            group_b(c).wait_recv()
            decode(c)

            @pl.when(no(start_group))
            def _():
                upper_out[c] = upper_out[c] + dot_stacked(enter_b[c], whole)
                encode(c)
                group_b(c).start()
            pass_on_b(c)
            return 0
        lax.fori_loop(0, chunks, go, 0)
        each(no(start_group), lambda c: half_b(c).start())

    @pl.when(late_map)
    def _():
        map_last()

    @pl.when(both(head, no(start_group), no(end_group)))
    def _():
        pl.semaphore_signal(credit, inc=1, device_id={"genome": left},
                            device_id_type=pl.DeviceIdType.MESH)

    @pl.when(early)
    def _():
        relay_back()

    @pl.when(jnp.logical_or(late_map, early))
    def _():
        prepare_end()

    @pl.when(no(start_group))
    def _():
        base[...] += dot_stacked(enter_f[...].reshape(traits, half), enter_rows_w[...])

    @pl.when(start_group)
    def _():
        base[:, :top] = top_rows[...].reshape(traits, top)
        base[:, top:] = (tail_out[...] - upper_in[...]).reshape(traits, half)
        base[...] = dot3(halves(base[...]), (inv_hi[...], inv_lo[...]), NN)

    @pl.when(both(no(end_group), no(inner)))
    def _():
        make_slope()

    @pl.when(no(end_group))
    def _():
        pre_base_out[0] = base[:, top:]
        pre_base_out[1] = base[:, :half]
        each(tail, lambda c: group_f(c).wait_send())
        each(tail, lambda c: head_f(c).wait_send())

        @pl.when(no(head))
        def _():
            ahead_base(1).start()

        @pl.when(tail)
        def _():
            ahead_slope(1).start()

        @pl.when(both(tail, g + 2 < count))
        def _():
            pl.semaphore_wait(credit, 1)

        ahead_base(0).start()

        @pl.when(no(inner))
        def _():
            ahead_slope(0).start()

    @pl.when(g < count // 2)
    def _():
        make_mask()

    def drain_early():
        each(both(no(start_group), no(tail)), lambda c: map_f(c).wait_send())
        each(no(tail), lambda c: local_f(c).wait_send())
        each(both(jnp.logical_or(gives_left, gives_right), no(start_group)),
             lambda c: pass_f_left(c).wait_send())
        each(both(no(end_group), no(head)), lambda c: map_b(c).wait_send())
        each(both(no(head), start_group), lambda c: local_b(c).wait_send())

    @pl.when(g < count // 2)
    def _():
        drain_early()

    @pl.when(both(no(end_group), head, no(early)))
    def _():
        relay_back()

    def step(c):
        group_b(c).wait_recv()
        pass_on_b(c)
        decode(c)
    each(both(no(end_group), no(head)), step)

    @pl.when(no(end_group))
    def _():
        base[...] -= dot_stacked(enter_b[...].reshape(traits, half), enter_base_w[...])

    weights = base[...].astype(BF16)
    left_out[...] = weights[:, top:]
    right_out[...] = weights[:, :half]

    late_right = both(end_group, no(last))
    late_left = both(no(first), jnp.logical_or(head, end_group))

    @pl.when(late_right)
    def _():
        to_right().start()

    @pl.when(late_left)
    def _():
        to_left().start()

    def edge(side, state):
        for copy in ahead(side):
            copy.wait_recv()
        return (pre_base_in[side] - dot_stacked(
            state.reshape(traits, half), stacked(halves(pre_slope_in[side])))).astype(BF16)

    @pl.when(both(no(end_group), no(head)))
    def _():
        left_in[...] = edge(0, enter_b[...])

    @pl.when(both(head, no(start_group)))
    def _():
        left_in[...] = edge(0, upper_out[...])

    @pl.when(both(no(end_group), no(tail)))
    def _():
        right_in[...] = edge(1, enter_b[...])

    out_ref[...] = product(weights, masked[:, half:half + typed], NT)

    @pl.when(both(no(last), jnp.logical_or(tail, end_group)))
    def _():
        to_left().wait_recv()

    out_ref[...] += product(right_in[...], masked[:, half + typed:], NT)

    @pl.when(both(end_group, no(head)))
    def _():
        to_right().wait_recv()

    out_ref[...] += product(left_in[...], masked[:, :half], NT)

    @pl.when(g >= count // 2)
    def _():
        drain_early()

    each(both(head, no(start_group)), lambda c: group_b(c).wait_send())
    each(both(head, no(start_group)), lambda c: half_b(c).wait_send())
    each(both(gives_b, no(end_group)), lambda c: pass_b(c).wait_send())

    @pl.when(both(no(start_group), no(head)))
    def _():
        to_left_gram().wait_send()
        to_left_add().wait_send()

    @pl.when(late_right)
    def _():
        to_right().wait_send()

    @pl.when(late_left)
    def _():
        to_left().wait_send()

    @pl.when(no(end_group))
    def _():
        for copy in ahead(0):
            copy.wait_send()

    @pl.when(both(no(end_group), no(head)))
    def _():
        for copy in ahead(1):
            copy.wait_send()


def per_device(n, z_typed, diag_inverse, coupling, impute_coef, anchor):
    traits, typed = z_typed.shape
    half = coupling.shape[2]
    units, span = impute_coef.shape
    top = typed - half
    chunks = next(k for k in (4, 2, 1) if traits % (16 * k) == half % (8 * k) == 0 or k == 1)
    rows = traits // chunks
    group = 1
    while n % (2 * group) == 0 and 4 * group * group <= n:
        group *= 2
    state = pltpu.VMEM((chunks, rows, half), F32)
    whole_state = pltpu.VMEM((traits, half), F32)
    square = pltpu.VMEM((half, half), F32)
    edge = pltpu.VMEM((traits, half), BF16)
    coded = pltpu.VMEM((chunks, rows, half), jnp.int16)
    scales = pltpu.VMEM((chunks, 1, half), F32)
    chain_map = pltpu.VMEM((chunks, half // chunks, half), F32)
    return pl.pallas_call(
        functools.partial(kernel, n, group),
        out_shape=jax.ShapeDtypeStruct((traits, units), F32),
        in_specs=[pl.BlockSpec(memory_space=pltpu.HBM)] * 5,
        out_specs=pl.BlockSpec(memory_space=pltpu.VMEM),
        scratch_shapes=[
            pltpu.VMEM((traits, typed), F32), pltpu.VMEM((typed, typed), F32),
            pltpu.VMEM((typed, half), F32), pltpu.VMEM((units, span), BF16),
            pltpu.VMEM((1, units), jnp.int32), pltpu.SemaphoreType.DMA((5,)),
            state, state, state, state, state, state, state,
            chain_map, chain_map, chain_map, chain_map, edge, edge, edge, edge,
            pltpu.VMEM((chunks, rows, top), F32), pltpu.VMEM((traits, typed), F32),
            pltpu.VMEM((3 * half, typed), BF16), pltpu.VMEM((3 * half, half), BF16),
            pltpu.VMEM((3 * half, typed), BF16),
            pltpu.VMEM((3 * half, half), BF16), pltpu.VMEM((3 * half, half), BF16),
            pltpu.VMEM((typed, typed), BF16), pltpu.VMEM((typed, typed), BF16),
            pltpu.VMEM((typed, half), BF16), pltpu.VMEM((typed, half), BF16),
            pltpu.VMEM((units, span), BF16),
            pltpu.VMEM((2, traits, half), F32), pltpu.VMEM((2, traits, half), F32),
            pltpu.VMEM((2, half, half), F32), pltpu.VMEM((2, half, half), F32),
            pltpu.SemaphoreType.DMA((2, 2)), pltpu.SemaphoreType.DMA((2, 2)),
            whole_state, whole_state, whole_state, square, square,
            pltpu.SemaphoreType.DMA((2,)), pltpu.SemaphoreType.DMA((2,)), pltpu.SemaphoreType.REGULAR,
            coded, scales, coded, scales,
            pltpu.SemaphoreType.DMA((13, chunks)), pltpu.SemaphoreType.DMA((7, chunks)),
            pltpu.SemaphoreType.DMA((2,)), pltpu.SemaphoreType.DMA((2,)),
        ],
        compiler_params=pltpu.CompilerParams(
            collective_id=0, has_side_effects=True, vmem_limit_bytes=int(53.25 * 1024 * 1024)),
    )(z_typed, diag_inverse[0], coupling[0], impute_coef, anchor.reshape(1, units))


def solution(mesh):
    shared = ("seg", "genome")
    in_specs = (P(None, shared), P(shared, None, None), P(shared, None, None),
                P(shared, None), P(shared))
    return jax.shard_map(
        functools.partial(per_device, mesh.shape["genome"]), mesh=mesh, in_specs=in_specs,
        out_specs=P(None, shared), check_vma=False)
```

```python
import functools

import jax
import jax.numpy as jnp
from jax import lax
from jax.experimental import pallas as pl
from jax.experimental.pallas import tpu as pltpu
from jax.sharding import PartitionSpec as P

F32 = jnp.float32
BF16 = jnp.bfloat16
NN = (((1,), (0,)), ((), ()))
NT = (((1,), (1,)), ((), ()))


def halves(x):
    high = x.astype(BF16)
    return high, (x - high.astype(F32)).astype(BF16)


def product(a, b, dims):
    return lax.dot_general(a, b, dims, preferred_element_type=F32)


def dot3(a, b, dims):
    return product(a[0], b[0], dims) + (product(a[0], b[1], dims) + product(a[1], b[0], dims))


def stacked(b):
    return jnp.concatenate([b[0], b[0], b[1]], axis=0)


def dot_stacked(x, weights):
    high, low = halves(x)
    return product(jnp.concatenate([high, low, high], axis=1), weights, NN)


class Both:
    def __init__(self, *copies):
        self.copies = copies

    def start(self):
        for copy in self.copies:
            copy.start()

    def wait_recv(self):
        for copy in self.copies:
            copy.wait_recv()

    def wait_send(self):
        for copy in self.copies:
            copy.wait_send()


def kernel(
    n, group, z_hbm, inverse_hbm, couple_hbm, coef_hbm, anchor_hbm, out_ref,
    z_ref, inverse_ref, couple_ref, coef_ref, anchor_ref, fetched,
    tail_in, tail_out, upper_in, upper_out, enter_f, enter_b, carry_f,
    map_f_in, map_f_out, map_b_in, map_b_out, left_in, right_in, left_out, right_out,
    top_rows, base, enter_rows_w, enter_add_w, enter_base_w, forward_w, backward_w, inv_hi, inv_lo, proj_hi, proj_lo, masked,
    pre_base_out, pre_base_in, pre_slope_out, pre_slope_in, ps, pr,
    own, add_in, add_out, gram_in, gram_out, rs, rr, credit,
    upper_q, upper_s, enter_q, enter_s, carry_q, carry_s, state_q, state_s,
    tail_out_q, tail_out_s, tail_in_q, tail_in_s, map_f_out_q, map_f_out_s, map_f_in_q, map_f_in_s,
    map_b_out_q, map_b_out_s, map_b_in_q, map_b_in_s, gram_q, gram_s, add_q, add_s,
    sent, got, es, er,
):
    me = lax.axis_index("genome")
    count = n // group
    g, q = me // group, lax.rem(me, group)
    first, last = me == 0, me == n - 1
    head, tail = q == 0, q == group - 1
    start_group, end_group = g == 0, g == count - 1
    right, left = lax.rem(me + 1, n), lax.rem(me + n - 1, n)
    far_right, far_left = lax.rem(me + group, n), lax.rem(me + n - group, n)
    chunks, rows, half = tail_in.shape
    typed = inverse_ref.shape[0]
    top = typed - half
    traits = chunks * rows
    no = jnp.logical_not
    fetch = [
        pltpu.make_async_copy(src, dst, fetched.at[i])
        for i, (src, dst) in enumerate((
            (inverse_hbm, inverse_ref), (z_hbm, z_ref), (couple_hbm, couple_ref),
            (anchor_hbm, anchor_ref), (coef_hbm, coef_ref)))]
    for copy in fetch:
        copy.start()

    def both(*conditions):
        return functools.reduce(jnp.logical_and, conditions)

    barrier = pltpu.get_barrier_semaphore()
    middle = group // 2
    half_right, half_left = lax.rem(me + middle, n), lax.rem(me + n - middle, n)
    to_end = g == count - 2
    expected = 0
    for other, meets in (
            (left, no(first)), (right, no(last)), (half_left, both(head, no(start_group))),
            (half_right, both(q == middle, no(end_group))),
            (far_left, no(start_group)), (far_right, no(end_group))):
        expected += jnp.where(meets, 1, 0)

        @pl.when(meets)
        def _():
            pl.semaphore_signal(barrier, inc=1, device_id={"genome": other},
                                device_id_type=pl.DeviceIdType.MESH)

    def remote(src, dst, send, recv, other):
        return pltpu.make_async_remote_copy(
            src_ref=src, dst_ref=dst, send_sem=send, recv_sem=recv,
            device_id={"genome": other}, device_id_type=pl.DeviceIdType.MESH)

    def channel(index, src, dst, landing, other):
        return lambda c: remote(src.at[c], dst.at[c], sent.at[index, c], got.at[landing, c], other)

    def coded_channel(i, j, src, dst, k, l, other):
        values, factors = channel(i, src[0], dst[0], k, other), channel(j, src[1], dst[1], l, other)
        return lambda c: Both(values(c), factors(c))

    def encode(ref, code, c):
        values = ref[c]
        peak = jnp.maximum(jnp.max(jnp.abs(values), axis=0, keepdims=True), 1e-30)
        code[1][c] = peak * (1.0 / 32000.0)
        code[0][c] = jnp.round(values * (32000.0 / peak)).astype(jnp.int32).astype(jnp.int16)

    def decode(code, ref, c):
        ref[c] = code[0][c].astype(jnp.int32).astype(F32) * code[1][c]

    def encode_whole(ref, code, scale):
        values = ref[...]
        peak = jnp.maximum(jnp.max(jnp.abs(values), axis=0, keepdims=True), 1e-30)
        scale[0] = peak * (1.0 / 32000.0)
        code[0] = jnp.round(values * (32000.0 / peak)).astype(jnp.int32).astype(jnp.int16)

    def send_gram():
        encode_whole(gram_out, gram_q, gram_s)
        to_left_gram().start()

    def send_add():
        encode_whole(add_out, add_q, add_s)
        to_left_add().start()

    upper_code, enter_code = (upper_q, upper_s), (enter_q, enter_s)
    carry_code, state_code = (carry_q, carry_s), (state_q, state_s)
    tail_out_code, tail_in_code = (tail_out_q, tail_out_s), (tail_in_q, tail_in_s)
    map_f_out_code, map_f_in_code = (map_f_out_q, map_f_out_s), (map_f_in_q, map_f_in_s)
    map_b_out_code, map_b_in_code = (map_b_out_q, map_b_out_s), (map_b_in_q, map_b_in_s)
    map_f = coded_channel(0, 13, map_f_out_code, map_f_in_code, 0, 7, right)
    local_f = coded_channel(1, 14, tail_out_code, tail_in_code, 1, 8, right)
    group_f = coded_channel(2, 15, carry_code, state_code, 2, 9, far_right)
    head_f = coded_channel(8, 17, carry_code, state_code, 2, 9, right)
    pass_f_left = coded_channel(3, 16, state_code, state_code, 2, 9, left)
    pass_f_right = coded_channel(3, 16, state_code, state_code, 2, 9, right)
    map_b = coded_channel(4, 18, map_b_out_code, map_b_in_code, 3, 10, left)
    local_b = channel(5, upper_out, upper_in, 4, left)

    group_b = coded_channel(6, 10, upper_code, enter_code, 5, 6, far_left)
    half_b = coded_channel(9, 11, upper_code, enter_code, 5, 6, half_left)
    pass_b = coded_channel(7, 12, enter_code, enter_code, 5, 6, right)

    gives_left, gives_right = q > middle, q + 1 < middle
    gives_b = lax.rem(q + 1, middle) != 0

    def pass_on_f(c):
        @pl.when(gives_left)
        def _():
            pass_f_left(c).start()

        @pl.when(gives_right)
        def _():
            pass_f_right(c).start()

    def pass_on_b(c):
        @pl.when(gives_b)
        def _():
            pass_b(c).start()

    def carry_first(c):
        @pl.when(to_end)
        def _():
            head_f(c).start()

        @pl.when(no(to_end))
        def _():
            group_f(c).start()

    def carry_second(c):
        @pl.when(to_end)
        def _():
            group_f(c).start()

        @pl.when(no(to_end))
        def _():
            head_f(c).start()

    def to_left_gram():
        return Both(remote(gram_q.at[0], gram_q.at[1], rs.at[0], rr.at[0], left),
                    remote(gram_s.at[0], gram_s.at[1], rs.at[2], rr.at[2], left))

    def to_left_add():
        return Both(remote(add_q.at[0], add_q.at[1], rs.at[1], rr.at[1], left),
                    remote(add_s.at[0], add_s.at[1], rs.at[3], rr.at[3], left))

    def to_right():
        return remote(left_out, left_in, es.at[0], er.at[0], right)

    def to_left():
        return remote(right_out, right_in, es.at[1], er.at[1], left)

    def ahead_base(side):
        return remote(pre_base_out.at[side], pre_base_in.at[side], ps.at[side, 0], pr.at[side, 0],
                      (right, left)[side])

    def ahead_slope(side):
        return remote(pre_slope_out.at[side], pre_slope_in.at[side], ps.at[side, 1], pr.at[side, 1],
                      (right, left)[side])

    def ahead(side):
        return ahead_base(side), ahead_slope(side)

    def each(condition, step):
        @pl.when(condition)
        def _():
            def go(c, _):
                step(c)
                return 0
            lax.fori_loop(0, chunks, go, 0)

    def clear(condition, ref):
        @pl.when(condition)
        def _():
            ref[...] = jnp.zeros_like(ref)

    def unit(condition, ref):
        @pl.when(condition)
        def _():
            row = lax.broadcasted_iota(jnp.int32, (half, half), 0)
            col = lax.broadcasted_iota(jnp.int32, (half, half), 1)
            ref[...] = (row == col).astype(F32).reshape(ref.shape)

    fetch[0].wait()
    hi, lo = halves(inverse_ref[...])
    inv_hi[...] = hi
    inv_lo[...] = lo
    fetch[1].wait()
    z_halves = halves(z_ref[...])
    solved = dot3(z_halves, (inv_hi[pl.ds(top, half), :], inv_lo[pl.ds(top, half), :]), NT)
    tail_out[...] = solved.reshape(chunks, rows, half)
    pl.semaphore_wait(barrier, expected)

    def send_local(c):
        encode(tail_out, tail_out_code, c)
        local_f(c).start()

    def send_map_f(c):
        encode(map_f_out, map_f_out_code, c)
        map_f(c).start()

    def send_map_b(c):
        encode(map_b_out, map_b_out_code, c)
        map_b(c).start()

    each(both(head, start_group, no(tail)), send_local)

    fetch[2].wait()
    projected = dot3((inv_hi[...], inv_lo[...]), halves(couple_ref[...]), NN)
    hi, lo = halves(projected)
    proj_hi[...] = hi
    proj_lo[...] = lo
    chain = -projected[top:, :]
    chain_t = chain.T
    map_f_out[...] = chain_t.reshape(map_f_out.shape)
    map_b_out[...] = chain.reshape(map_b_out.shape)
    forward_w[...] = stacked(halves(chain_t))
    backward_w[...] = stacked(halves(chain))

    each(both(head, no(start_group), no(tail)), send_map_f)
    each(both(head, no(start_group), no(tail)), send_local)
    each(both(tail, no(end_group), no(head)), send_map_b)

    clear(head, tail_in)
    clear(both(tail, start_group), upper_in)
    clear(start_group, enter_f)
    clear(both(tail, no(start_group)), gram_in)
    clear(both(tail, no(start_group)), add_in)
    clear(end_group, enter_b)
    clear(first, left_in)
    clear(last, right_in)
    unit(jnp.logical_or(head, start_group), map_f_in)
    unit(jnp.logical_or(tail, end_group), map_b_in)

    def solve_top():
        solved_top = dot3(z_halves, (inv_hi[pl.ds(0, top), :], inv_lo[pl.ds(0, top), :]), NT)
        top_rows[...] = solved_top.reshape(chunks, rows, top)

    @pl.when(no(start_group))
    def _():
        proj = (proj_hi[...], proj_lo[...])
        projected_t = jnp.concatenate([projected[:top, :].T, -chain_t], axis=1)
        gram_out[...] = dot3(halves(projected_t), proj, NN)

        @pl.when(tail)
        def _():
            send_gram()

        solve_top()
        own[...] = tail_out[...].reshape(traits, half)
        rows_now = jnp.concatenate([top_rows[...].reshape(traits, top), own[...]], axis=1)
        add_out[...] = dot3(halves(rows_now), proj, NN)

        @pl.when(tail)
        def _():
            send_add()

    def fold():
        to_left_gram().wait_recv()
        gram_in[...] = gram_q[1].astype(jnp.int32).astype(F32) * gram_s[1]
        gram = halves(gram_in[...])
        step_map = (forward_w[pl.ds(0, half), :], forward_w[pl.ds(2 * half, half), :])
        gram_out[...] += dot_stacked(dot3(step_map, gram, NN), backward_w[...])

        @pl.when(no(head))
        def _():
            send_gram()

        to_left_add().wait_recv()
        add_in[...] = add_q[1].astype(jnp.int32).astype(F32) * add_s[1]
        add_out[...] += dot_stacked(add_in[...] - dot3(halves(own[...]), gram, NN), backward_w[...])

        @pl.when(no(head))
        def _():
            send_add()

    def map_step(c):
        map_b(c).wait_recv()
        decode(map_b_in_code, map_b_in, c)
        map_b_out[c] = dot_stacked(map_b_in[c], backward_w[...])
        send_map_b(c)
    soon_map = both(no(start_group), no(end_group), no(tail), no(head), q >= middle)

    @pl.when(both(no(start_group), no(tail), q >= middle))
    def _():
        fold()

    each(soon_map, map_step)

    relay = both(no(start_group), no(end_group), tail)

    def step(c):
        map_f(c).wait_recv()
        decode(map_f_in_code, map_f_in, c)
        map_f_out[c] = dot_stacked(map_f_in[c], forward_w[...])

        @pl.when(no(tail))
        def _():
            send_map_f(c)
    each(both(no(start_group), no(head)), step)

    def add_local(c):
        local_f(c).wait_recv()
        decode(tail_in_code, tail_in, c)
        tail_out[c] = tail_out[c] + dot_stacked(tail_in[c], forward_w[...])

    def step(c):
        add_local(c)

        @pl.when(no(tail))
        def _():
            send_local(c)
    each(both(no(start_group), no(head), no(relay)), step)

    def step(c):
        local_f(c).wait_recv()
        decode(tail_in_code, tail_in, c)
        tail_out[c] = tail_out[c] + dot_stacked(tail_in[c], forward_w[...])

        @pl.when(no(tail))
        def _():
            send_local(c)

        @pl.when(both(tail, start_group, no(end_group)))
        def _():
            carry_f[c] = tail_out[c]
            encode(carry_f, carry_code, c)
            carry_first(c)
    each(both(start_group, no(head)), step)
    each(both(tail, start_group, no(end_group)), carry_second)
    @pl.when(both(no(start_group), q < middle))
    def _():
        fold()

    @pl.when(start_group)
    def _():
        solve_top()

    last_head = both(end_group, head)
    early = both(head, no(start_group), to_end)
    late_map = both(head, no(start_group), no(end_group), no(early))
    each(both(no(end_group), no(tail), no(head), no(soon_map)), map_step)

    def map_last():
        def go(c, _):
            map_b(c).wait_recv()
            decode(map_b_in_code, map_b_in, c)
            return 0
        lax.fori_loop(0, chunks, go, 0)
        map_b_out[...] = dot_stacked(
            map_b_in[...].reshape(half, half), backward_w[...]).reshape(map_b_out.shape)

    @pl.when(both(no(end_group), head, no(late_map)))
    def _():
        map_last()

    fetch[3].wait()
    fetch[4].wait()

    def make_mask():
        spread = 128
        units = anchor_ref.shape[1]
        nearest = jnp.broadcast_to(anchor_ref[...], (spread, units)).T
        start = me * typed - half
        lanes = lax.broadcasted_iota(jnp.int32, (units, spread), 1)
        for j in range(0, typed + 2 * half, spread):
            within = jnp.abs(lanes + (start + j) - nearest) <= half
            coef = coef_ref[:, j:j + spread].astype(F32)
            masked[:, j:j + spread] = jnp.where(within, coef, 0.0).astype(BF16)

    @pl.when(g >= count // 2)
    def _():
        make_mask()

    def prepare():
        proj = (proj_hi[...], proj_lo[...])
        proj_top = (proj_hi[pl.ds(0, top), :], proj_lo[pl.ds(0, top), :])
        above = top_rows[...].reshape(traits, top) - dot3(
            halves(tail_in[...].reshape(traits, half)), proj_top, NT)
        top_rows[...] = above.reshape(chunks, rows, top)
        all_rows = jnp.concatenate([above, tail_out[...].reshape(traits, half)], axis=1)
        upper_out[...] = dot3(halves(all_rows), proj, NN).reshape(chunks, rows, half)

    def prepare_end():
        proj_top = (proj_hi[pl.ds(0, top), :], proj_lo[pl.ds(0, top), :])
        inverse = (inv_hi[...], inv_lo[...])
        gram = halves(gram_in[...])
        low = tail_out[...].reshape(traits, half)
        above = top_rows[...].reshape(traits, top) - dot3(
            halves(tail_in[...].reshape(traits, half)), proj_top, NT)
        below = low - add_in[...] + dot3(halves(low), gram, NN)
        base[...] = dot3(halves(jnp.concatenate([above, below], axis=1)), inverse, NN)
        low = map_f_out[...].reshape(half, half)
        above = -dot3(halves(map_f_in[...].reshape(half, half)), proj_top, NT)
        below = low + dot3(halves(low), gram, NN)
        enter_rows_w[...] = stacked(halves(
            dot3(halves(jnp.concatenate([above, below], axis=1)), inverse, NN)))

    @pl.when(start_group)
    def _():
        prepare()

    @pl.when(both(no(relay), no(start_group), no(late_map), no(early)))
    def _():
        prepare_end()

    def make_slope():
        slope = dot3(halves(map_b_in[...].reshape(half, half)),
                     (inv_hi[pl.ds(top, half), :], inv_lo[pl.ds(top, half), :]), NN)
        enter_base_w[...] = stacked(halves(slope))
        pre_slope_out[0] = slope[:, top:]
        pre_slope_out[1] = slope[:, :half]

    inner = both(no(head), no(tail))

    @pl.when(both(no(end_group), inner))
    def _():
        make_slope()
        ahead_slope(0).start()
        ahead_slope(1).start()

    @pl.when(both(head, no(start_group)))
    def _():
        enter_add_w[...] = stacked(halves(gram_out[...]))

    @pl.when(relay)
    def _():
        whole = stacked(halves(map_f_out[...].reshape(half, half)))

        def go(c, _):
            add_local(c)
            group_f(c).wait_recv()
            pass_on_f(c)
            decode(state_code, enter_f, c)
            carry_f[c] = tail_out[c] + dot_stacked(enter_f[c], whole)
            encode(carry_f, carry_code, c)
            carry_first(c)
            return 0
        lax.fori_loop(0, chunks, go, 0)
        each(True, carry_second)
        prepare_end()

    each(both(tail, no(head), start_group), lambda c: local_b(c).start())

    def step(c):
        local_b(c).wait_recv()
        upper_out[c] = upper_out[c] + dot_stacked(upper_in[c], backward_w[...])

        @pl.when(no(head))
        def _():
            local_b(c).start()
    each(both(no(tail), start_group), step)

    def step(c):
        group_f(c).wait_recv()
        pass_on_f(c)
        decode(state_code, enter_f, c)

        @pl.when(last_head)
        def _():
            upper_out[c] = add_out[pl.ds(pl.multiple_of(c * rows, rows), rows), :] - dot_stacked(
                enter_f[c], enter_add_w[...])
            encode(upper_out, upper_code, c)
            group_b(c).start()
    each(both(no(start_group), no(relay)), step)

    @pl.when(both(head, no(start_group), no(end_group)))
    def _():
        upper_out[...] = (add_out[...] - dot_stacked(
            enter_f[...].reshape(traits, half), enter_add_w[...])).reshape(chunks, rows, half)
    each(both(end_group, head), lambda c: half_b(c).start())

    def relay_back():
        whole = stacked(halves(map_b_out[...].reshape(half, half)))

        def go(c, _):
            group_b(c).wait_recv()
            decode(enter_code, enter_b, c)

            @pl.when(no(start_group))
            def _():
                upper_out[c] = upper_out[c] + dot_stacked(enter_b[c], whole)
                encode(upper_out, upper_code, c)
                group_b(c).start()
            pass_on_b(c)
            return 0
        lax.fori_loop(0, chunks, go, 0)
        each(no(start_group), lambda c: half_b(c).start())

    @pl.when(late_map)
    def _():
        map_last()

    @pl.when(both(head, no(start_group), no(end_group)))
    def _():
        pl.semaphore_signal(credit, inc=1, device_id={"genome": left},
                            device_id_type=pl.DeviceIdType.MESH)

    @pl.when(early)
    def _():
        relay_back()

    @pl.when(jnp.logical_or(late_map, early))
    def _():
        prepare_end()

    @pl.when(no(start_group))
    def _():
        base[...] += dot_stacked(enter_f[...].reshape(traits, half), enter_rows_w[...])

    @pl.when(start_group)
    def _():
        base[:, :top] = top_rows[...].reshape(traits, top)
        base[:, top:] = (tail_out[...] - upper_in[...]).reshape(traits, half)
        base[...] = dot3(halves(base[...]), (inv_hi[...], inv_lo[...]), NN)

    @pl.when(both(no(end_group), no(inner)))
    def _():
        make_slope()

    @pl.when(no(end_group))
    def _():
        pre_base_out[0] = base[:, top:]
        pre_base_out[1] = base[:, :half]
        each(tail, lambda c: group_f(c).wait_send())
        each(tail, lambda c: head_f(c).wait_send())

        @pl.when(no(head))
        def _():
            ahead_base(1).start()

        @pl.when(tail)
        def _():
            ahead_slope(1).start()

        @pl.when(both(tail, g + 2 < count))
        def _():
            pl.semaphore_wait(credit, 1)

        ahead_base(0).start()

        @pl.when(no(inner))
        def _():
            ahead_slope(0).start()

    @pl.when(g < count // 2)
    def _():
        make_mask()

    def drain_early():
        each(both(no(start_group), no(tail)), lambda c: map_f(c).wait_send())
        each(no(tail), lambda c: local_f(c).wait_send())
        each(both(jnp.logical_or(gives_left, gives_right), no(start_group)),
             lambda c: pass_f_left(c).wait_send())
        each(both(no(end_group), no(head)), lambda c: map_b(c).wait_send())
        each(both(no(head), start_group), lambda c: local_b(c).wait_send())

    @pl.when(g < count // 2)
    def _():
        drain_early()

    @pl.when(both(no(end_group), head, no(early)))
    def _():
        relay_back()

    def step(c):
        group_b(c).wait_recv()
        pass_on_b(c)
        decode(enter_code, enter_b, c)
    each(both(no(end_group), no(head)), step)

    @pl.when(no(end_group))
    def _():
        base[...] -= dot_stacked(enter_b[...].reshape(traits, half), enter_base_w[...])

    weights = base[...].astype(BF16)
    left_out[...] = weights[:, top:]
    right_out[...] = weights[:, :half]

    late_right = both(end_group, no(last))
    late_left = both(no(first), jnp.logical_or(head, end_group))

    @pl.when(late_right)
    def _():
        to_right().start()

    @pl.when(late_left)
    def _():
        to_left().start()

    def edge(side, state):
        for copy in ahead(side):
            copy.wait_recv()
        return (pre_base_in[side] - dot_stacked(
            state.reshape(traits, half), stacked(halves(pre_slope_in[side])))).astype(BF16)

    @pl.when(both(no(end_group), no(head)))
    def _():
        left_in[...] = edge(0, enter_b[...])

    @pl.when(both(head, no(start_group)))
    def _():
        left_in[...] = edge(0, upper_out[...])

    @pl.when(both(no(end_group), no(tail)))
    def _():
        right_in[...] = edge(1, enter_b[...])

    out_ref[...] = product(weights, masked[:, half:half + typed], NT)

    @pl.when(both(no(last), jnp.logical_or(tail, end_group)))
    def _():
        to_left().wait_recv()

    out_ref[...] += product(right_in[...], masked[:, half + typed:], NT)

    @pl.when(both(end_group, no(head)))
    def _():
        to_right().wait_recv()

    out_ref[...] += product(left_in[...], masked[:, :half], NT)

    @pl.when(g >= count // 2)
    def _():
        drain_early()

    each(both(head, no(start_group)), lambda c: group_b(c).wait_send())
    each(both(head, no(start_group)), lambda c: half_b(c).wait_send())
    each(both(gives_b, no(end_group)), lambda c: pass_b(c).wait_send())

    @pl.when(both(no(start_group), no(head)))
    def _():
        to_left_gram().wait_send()
        to_left_add().wait_send()

    @pl.when(late_right)
    def _():
        to_right().wait_send()

    @pl.when(late_left)
    def _():
        to_left().wait_send()

    @pl.when(no(end_group))
    def _():
        for copy in ahead(0):
            copy.wait_send()

    @pl.when(both(no(end_group), no(head)))
    def _():
        for copy in ahead(1):
            copy.wait_send()


def per_device(n, z_typed, diag_inverse, coupling, impute_coef, anchor):
    traits, typed = z_typed.shape
    half = coupling.shape[2]
    units, span = impute_coef.shape
    top = typed - half
    chunks = next(k for k in (4, 2, 1) if traits % (16 * k) == half % (8 * k) == 0 or k == 1)
    rows = traits // chunks
    group = 1
    while n % (2 * group) == 0 and 4 * group * group <= n:
        group *= 2
    state = pltpu.VMEM((chunks, rows, half), F32)
    whole_state = pltpu.VMEM((traits, half), F32)
    square = pltpu.VMEM((half, half), F32)
    edge = pltpu.VMEM((traits, half), BF16)
    coded = pltpu.VMEM((chunks, rows, half), jnp.int16)
    scales = pltpu.VMEM((chunks, 1, half), F32)
    coded_map = pltpu.VMEM((chunks, half // chunks, half), jnp.int16)
    chain_map = pltpu.VMEM((chunks, half // chunks, half), F32)
    return pl.pallas_call(
        functools.partial(kernel, n, group),
        out_shape=jax.ShapeDtypeStruct((traits, units), F32),
        in_specs=[pl.BlockSpec(memory_space=pltpu.HBM)] * 5,
        out_specs=pl.BlockSpec(memory_space=pltpu.VMEM),
        scratch_shapes=[
            pltpu.VMEM((traits, typed), F32), pltpu.VMEM((typed, typed), F32),
            pltpu.VMEM((typed, half), F32), pltpu.VMEM((units, span), BF16),
            pltpu.VMEM((1, units), jnp.int32), pltpu.SemaphoreType.DMA((5,)),
            state, state, state, state, state, state, state,
            chain_map, chain_map, chain_map, chain_map, edge, edge, edge, edge,
            pltpu.VMEM((chunks, rows, top), F32), pltpu.VMEM((traits, typed), F32),
            pltpu.VMEM((3 * half, typed), BF16), pltpu.VMEM((3 * half, half), BF16),
            pltpu.VMEM((3 * half, typed), BF16),
            pltpu.VMEM((3 * half, half), BF16), pltpu.VMEM((3 * half, half), BF16),
            pltpu.VMEM((typed, typed), BF16), pltpu.VMEM((typed, typed), BF16),
            pltpu.VMEM((typed, half), BF16), pltpu.VMEM((typed, half), BF16),
            pltpu.VMEM((units, span), BF16),
            pltpu.VMEM((2, traits, half), F32), pltpu.VMEM((2, traits, half), F32),
            pltpu.VMEM((2, half, half), F32), pltpu.VMEM((2, half, half), F32),
            pltpu.SemaphoreType.DMA((2, 2)), pltpu.SemaphoreType.DMA((2, 2)),
            whole_state, whole_state, whole_state, square, square,
            pltpu.SemaphoreType.DMA((4,)), pltpu.SemaphoreType.DMA((4,)), pltpu.SemaphoreType.REGULAR,
            coded, scales, coded, scales, coded, scales, coded, scales,
            coded, scales, coded, scales, coded_map, scales, coded_map, scales,
            coded_map, scales, coded_map, scales,
            pltpu.VMEM((2, half, half), jnp.int16), pltpu.VMEM((2, 1, half), F32),
            pltpu.VMEM((2, traits, half), jnp.int16), pltpu.VMEM((2, 1, half), F32),
            pltpu.SemaphoreType.DMA((19, chunks)), pltpu.SemaphoreType.DMA((11, chunks)),
            pltpu.SemaphoreType.DMA((2,)), pltpu.SemaphoreType.DMA((2,)),
        ],
        compiler_params=pltpu.CompilerParams(
            collective_id=0, has_side_effects=True, vmem_limit_bytes=int(53.25 * 1024 * 1024)),
    )(z_typed, diag_inverse[0], coupling[0], impute_coef, anchor.reshape(1, units))


def solution(mesh):
    shared = ("seg", "genome")
    in_specs = (P(None, shared), P(shared, None, None), P(shared, None, None),
                P(shared, None), P(shared))
    return jax.shard_map(
        functools.partial(per_device, mesh.shape["genome"]), mesh=mesh, in_specs=in_specs,
        out_specs=P(None, shared), check_vma=False)
```

```python
import functools

import jax
import jax.numpy as jnp
from jax import lax
from jax.experimental import pallas as pl
from jax.experimental.pallas import tpu as pltpu
from jax.sharding import PartitionSpec as P

F32 = jnp.float32
BF16 = jnp.bfloat16
NN = (((1,), (0,)), ((), ()))
NT = (((1,), (1,)), ((), ()))


def halves(x):
    high = x.astype(BF16)
    return high, (x - high.astype(F32)).astype(BF16)


def product(a, b, dims):
    return lax.dot_general(a, b, dims, preferred_element_type=F32)


def dot3(a, b, dims):
    return product(a[0], b[0], dims) + (product(a[0], b[1], dims) + product(a[1], b[0], dims))


def stacked(b):
    return jnp.concatenate([b[0], b[0], b[1]], axis=0)


def dot_stacked(x, weights):
    high, low = halves(x)
    return product(jnp.concatenate([high, low, high], axis=1), weights, NN)


class Both:
    def __init__(self, *copies):
        self.copies = copies

    def start(self):
        for copy in self.copies:
            copy.start()

    def wait_recv(self):
        for copy in self.copies:
            copy.wait_recv()

    def wait_send(self):
        for copy in self.copies:
            copy.wait_send()


def kernel(
    n, group, z_hbm, inverse_hbm, couple_hbm, coef_hbm, anchor_hbm, out_ref,
    z_ref, inverse_ref, couple_ref, coef_ref, anchor_ref, fetched,
    tail_in, tail_out, upper_in, upper_out, enter_f, enter_b, carry_f,
    map_f_in, map_f_out, map_b_in, map_b_out, left_in, right_in, left_out, right_out,
    top_rows, base, enter_rows_w, enter_add_w, enter_base_w, forward_w, backward_w, inv_hi, inv_lo, proj_hi, proj_lo, masked,
    pre_base_out, pre_base_in, pre_slope_out, pre_slope_in, ps, pr,
    own, add_in, add_out, gram_in, gram_out, rs, rr, credit,
    upper_q, upper_s, enter_q, enter_s, carry_q, carry_s, state_q, state_s,
    tail_out_q, tail_out_s, tail_in_q, tail_in_s, map_f_out_q, map_f_out_s, map_f_in_q, map_f_in_s,
    map_b_out_q, map_b_out_s, map_b_in_q, map_b_in_s, gram_q, gram_s, add_q, add_s,
    leap_in, leap_q, leap_s, mid_q, mid_s, far_map, far_q, far_s, far_w, ready,
    sent, got, es, er,
):
    me = lax.axis_index("genome")
    count = n // group
    g, q = me // group, lax.rem(me, group)
    first, last = me == 0, me == n - 1
    head, tail = q == 0, q == group - 1
    start_group, end_group = g == 0, g == count - 1
    right, left = lax.rem(me + 1, n), lax.rem(me + n - 1, n)
    far_right, far_left = lax.rem(me + group, n), lax.rem(me + n - group, n)
    chunks, rows, half = tail_in.shape
    typed = inverse_ref.shape[0]
    top = typed - half
    traits = chunks * rows
    no = jnp.logical_not
    fetch = [
        pltpu.make_async_copy(src, dst, fetched.at[i])
        for i, (src, dst) in enumerate((
            (inverse_hbm, inverse_ref), (z_hbm, z_ref), (couple_hbm, couple_ref),
            (anchor_hbm, anchor_ref), (coef_hbm, coef_ref)))]
    for copy in fetch:
        copy.start()

    def both(*conditions):
        return functools.reduce(jnp.logical_and, conditions)

    barrier = pltpu.get_barrier_semaphore()
    middle = group // 2
    half_right, half_left = lax.rem(me + middle, n), lax.rem(me + n - middle, n)
    to_end = g == count - 2
    near = g == (count - 2 if count > 2 else n)
    leap = g == (count - 3 if count > 2 else n)
    leap_left = lax.rem(me + 2 * n - 2 * group, n)
    expected = 0
    for other, meets in (
            (left, no(first)), (right, no(last)), (half_left, both(head, no(start_group))),
            (half_right, both(q == middle, no(end_group))),
            (half_left, both(q == middle, leap)), (half_right, both(head, leap)),
            (far_left, no(start_group)), (far_right, no(end_group))):
        expected += jnp.where(meets, 1, 0)

        @pl.when(meets)
        def _():
            pl.semaphore_signal(barrier, inc=1, device_id={"genome": other},
                                device_id_type=pl.DeviceIdType.MESH)

    def remote(src, dst, send, recv, other):
        return pltpu.make_async_remote_copy(
            src_ref=src, dst_ref=dst, send_sem=send, recv_sem=recv,
            device_id={"genome": other}, device_id_type=pl.DeviceIdType.MESH)

    def channel(index, src, dst, landing, other):
        return lambda c: remote(src.at[c], dst.at[c], sent.at[index, c], got.at[landing, c], other)

    def coded_channel(i, j, src, dst, k, l, other):
        values, factors = channel(i, src[0], dst[0], k, other), channel(j, src[1], dst[1], l, other)
        return lambda c: Both(values(c), factors(c))

    def encode(ref, code, c):
        values = ref[c]
        peak = jnp.maximum(jnp.max(jnp.abs(values), axis=0, keepdims=True), 1e-30)
        code[1][c] = peak * (1.0 / 32000.0)
        code[0][c] = jnp.round(values * (32000.0 / peak)).astype(jnp.int32).astype(jnp.int16)

    def decode(code, ref, c):
        ref[c] = code[0][c].astype(jnp.int32).astype(F32) * code[1][c]

    def encode_whole(ref, code, scale):
        values = ref[...]
        peak = jnp.maximum(jnp.max(jnp.abs(values), axis=0, keepdims=True), 1e-30)
        scale[0] = peak * (1.0 / 32000.0)
        code[0] = jnp.round(values * (32000.0 / peak)).astype(jnp.int32).astype(jnp.int16)

    def send_gram():
        encode_whole(gram_out, gram_q, gram_s)
        to_left_gram().start()

    def send_add():
        encode_whole(add_out, add_q, add_s)
        to_left_add().start()

    upper_code, enter_code = (upper_q, upper_s), (enter_q, enter_s)
    carry_code, state_code = (carry_q, carry_s), (state_q, state_s)
    tail_out_code, tail_in_code = (tail_out_q, tail_out_s), (tail_in_q, tail_in_s)
    map_f_out_code, map_f_in_code = (map_f_out_q, map_f_out_s), (map_f_in_q, map_f_in_s)
    map_b_out_code, map_b_in_code = (map_b_out_q, map_b_out_s), (map_b_in_q, map_b_in_s)
    map_f = coded_channel(0, 13, map_f_out_code, map_f_in_code, 0, 7, right)
    local_f = coded_channel(1, 14, tail_out_code, tail_in_code, 1, 8, right)
    group_f = coded_channel(2, 15, carry_code, state_code, 2, 9, far_right)
    head_f = coded_channel(8, 17, carry_code, state_code, 2, 9, right)
    pass_f_left = coded_channel(3, 16, state_code, state_code, 2, 9, left)
    pass_f_right = coded_channel(3, 16, state_code, state_code, 2, 9, right)
    map_b = coded_channel(4, 18, map_b_out_code, map_b_in_code, 3, 10, left)
    local_b = channel(5, upper_out, upper_in, 4, left)

    group_b = coded_channel(6, 10, upper_code, enter_code, 5, 6, far_left)
    half_b = coded_channel(9, 11, upper_code, enter_code, 5, 6, half_left)
    pass_b = coded_channel(7, 12, enter_code, enter_code, 5, 6, right)
    leap_code, mid_code, far_code = (leap_q, leap_s), (mid_q, mid_s), (far_q, far_s)
    leap_b = coded_channel(19, 20, upper_code, leap_code, 11, 12, leap_left)
    far_b = coded_channel(21, 22, map_b_out_code, far_code, 13, 14, far_left)
    mid_b = coded_channel(23, 24, mid_code, enter_code, 5, 6, half_right)
    pass_mid = coded_channel(7, 12, mid_code, enter_code, 5, 6, right)

    gives_left, gives_right = q > middle, q + 1 < middle
    gives_b = lax.rem(q + 1, middle) != 0

    def pass_on_f(c):
        @pl.when(gives_left)
        def _():
            pass_f_left(c).start()

        @pl.when(gives_right)
        def _():
            pass_f_right(c).start()

    def pass_on_b(c):
        @pl.when(gives_b)
        def _():
            pass_b(c).start()

    def carry_first(c):
        @pl.when(to_end)
        def _():
            head_f(c).start()

        @pl.when(no(to_end))
        def _():
            group_f(c).start()

    def carry_second(c):
        @pl.when(to_end)
        def _():
            group_f(c).start()

        @pl.when(no(to_end))
        def _():
            head_f(c).start()

    def to_left_gram():
        return Both(remote(gram_q.at[0], gram_q.at[1], rs.at[0], rr.at[0], left),
                    remote(gram_s.at[0], gram_s.at[1], rs.at[2], rr.at[2], left))

    def to_left_add():
        return Both(remote(add_q.at[0], add_q.at[1], rs.at[1], rr.at[1], left),
                    remote(add_s.at[0], add_s.at[1], rs.at[3], rr.at[3], left))

    def to_right():
        return remote(left_out, left_in, es.at[0], er.at[0], right)

    def to_left():
        return remote(right_out, right_in, es.at[1], er.at[1], left)

    def ahead_base(side):
        return remote(pre_base_out.at[side], pre_base_in.at[side], ps.at[side, 0], pr.at[side, 0],
                      (right, left)[side])

    def ahead_slope(side):
        return remote(pre_slope_out.at[side], pre_slope_in.at[side], ps.at[side, 1], pr.at[side, 1],
                      (right, left)[side])

    def ahead(side):
        return ahead_base(side), ahead_slope(side)

    def each(condition, step):
        @pl.when(condition)
        def _():
            def go(c, _):
                step(c)
                return 0
            lax.fori_loop(0, chunks, go, 0)

    def clear(condition, ref):
        @pl.when(condition)
        def _():
            ref[...] = jnp.zeros_like(ref)

    def unit(condition, ref):
        @pl.when(condition)
        def _():
            row = lax.broadcasted_iota(jnp.int32, (half, half), 0)
            col = lax.broadcasted_iota(jnp.int32, (half, half), 1)
            ref[...] = (row == col).astype(F32).reshape(ref.shape)

    fetch[0].wait()
    hi, lo = halves(inverse_ref[...])
    inv_hi[...] = hi
    inv_lo[...] = lo
    fetch[1].wait()
    z_halves = halves(z_ref[...])
    solved = dot3(z_halves, (inv_hi[pl.ds(top, half), :], inv_lo[pl.ds(top, half), :]), NT)
    tail_out[...] = solved.reshape(chunks, rows, half)
    pl.semaphore_wait(barrier, expected)

    @pl.when(both(near, head))
    def _():
        pl.semaphore_signal(ready, inc=1, device_id={"genome": far_right},
                            device_id_type=pl.DeviceIdType.MESH)

    def send_local(c):
        encode(tail_out, tail_out_code, c)
        local_f(c).start()

    def send_map_f(c):
        encode(map_f_out, map_f_out_code, c)
        map_f(c).start()

    def send_map_b(c):
        encode(map_b_out, map_b_out_code, c)
        map_b(c).start()

    each(both(head, start_group, no(tail)), send_local)

    fetch[2].wait()
    projected = dot3((inv_hi[...], inv_lo[...]), halves(couple_ref[...]), NN)
    hi, lo = halves(projected)
    proj_hi[...] = hi
    proj_lo[...] = lo
    chain = -projected[top:, :]
    chain_t = chain.T
    map_f_out[...] = chain_t.reshape(map_f_out.shape)
    map_b_out[...] = chain.reshape(map_b_out.shape)
    forward_w[...] = stacked(halves(chain_t))
    backward_w[...] = stacked(halves(chain))

    each(both(head, no(start_group), no(tail)), send_map_f)
    each(both(head, no(start_group), no(tail)), send_local)
    each(both(tail, no(end_group), no(head)), send_map_b)

    clear(head, tail_in)
    clear(both(tail, start_group), upper_in)
    clear(start_group, enter_f)
    clear(both(tail, no(start_group)), gram_in)
    clear(both(tail, no(start_group)), add_in)
    clear(end_group, enter_b)
    clear(first, left_in)
    clear(last, right_in)
    unit(jnp.logical_or(head, start_group), map_f_in)
    unit(jnp.logical_or(tail, end_group), map_b_in)

    def solve_top():
        solved_top = dot3(z_halves, (inv_hi[pl.ds(0, top), :], inv_lo[pl.ds(0, top), :]), NT)
        top_rows[...] = solved_top.reshape(chunks, rows, top)

    @pl.when(no(start_group))
    def _():
        proj = (proj_hi[...], proj_lo[...])
        projected_t = jnp.concatenate([projected[:top, :].T, -chain_t], axis=1)
        gram_out[...] = dot3(halves(projected_t), proj, NN)

        @pl.when(tail)
        def _():
            send_gram()

        solve_top()
        own[...] = tail_out[...].reshape(traits, half)
        rows_now = jnp.concatenate([top_rows[...].reshape(traits, top), own[...]], axis=1)
        add_out[...] = dot3(halves(rows_now), proj, NN)

        @pl.when(tail)
        def _():
            send_add()

    def fold():
        to_left_gram().wait_recv()
        gram_in[...] = gram_q[1].astype(jnp.int32).astype(F32) * gram_s[1]
        gram = halves(gram_in[...])
        step_map = (forward_w[pl.ds(0, half), :], forward_w[pl.ds(2 * half, half), :])
        gram_out[...] += dot_stacked(dot3(step_map, gram, NN), backward_w[...])

        @pl.when(no(head))
        def _():
            send_gram()

        to_left_add().wait_recv()
        add_in[...] = add_q[1].astype(jnp.int32).astype(F32) * add_s[1]
        add_out[...] += dot_stacked(add_in[...] - dot3(halves(own[...]), gram, NN), backward_w[...])

        @pl.when(no(head))
        def _():
            send_add()

    def map_step(c):
        map_b(c).wait_recv()
        decode(map_b_in_code, map_b_in, c)
        map_b_out[c] = dot_stacked(map_b_in[c], backward_w[...])
        send_map_b(c)
    soon_map = both(no(start_group), no(end_group), no(tail), no(head), q >= middle)

    @pl.when(both(no(start_group), no(tail), q >= middle))
    def _():
        fold()

    each(soon_map, map_step)

    relay = both(no(start_group), no(end_group), tail)

    def step(c):
        map_f(c).wait_recv()
        decode(map_f_in_code, map_f_in, c)
        map_f_out[c] = dot_stacked(map_f_in[c], forward_w[...])

        @pl.when(no(tail))
        def _():
            send_map_f(c)
    each(both(no(start_group), no(head)), step)

    def add_local(c):
        local_f(c).wait_recv()
        decode(tail_in_code, tail_in, c)
        tail_out[c] = tail_out[c] + dot_stacked(tail_in[c], forward_w[...])

    def step(c):
        add_local(c)

        @pl.when(no(tail))
        def _():
            send_local(c)
    each(both(no(start_group), no(head), no(relay)), step)

    def step(c):
        local_f(c).wait_recv()
        decode(tail_in_code, tail_in, c)
        tail_out[c] = tail_out[c] + dot_stacked(tail_in[c], forward_w[...])

        @pl.when(no(tail))
        def _():
            send_local(c)

        @pl.when(both(tail, start_group, no(end_group)))
        def _():
            carry_f[c] = tail_out[c]
            encode(carry_f, carry_code, c)
            carry_first(c)
    each(both(start_group, no(head)), step)
    each(both(tail, start_group, no(end_group)), carry_second)
    @pl.when(both(no(start_group), q < middle))
    def _():
        fold()

    @pl.when(start_group)
    def _():
        solve_top()

    last_head = both(end_group, head)
    early = both(head, no(start_group), to_end)
    late_map = both(head, no(start_group), no(end_group), no(early))
    each(both(no(end_group), no(tail), no(head), no(soon_map)), map_step)

    def map_last():
        def go(c, _):
            map_b(c).wait_recv()
            decode(map_b_in_code, map_b_in, c)
            return 0
        lax.fori_loop(0, chunks, go, 0)
        map_b_out[...] = dot_stacked(
            map_b_in[...].reshape(half, half), backward_w[...]).reshape(map_b_out.shape)

    @pl.when(both(no(end_group), head, no(late_map)))
    def _():
        map_last()

    def send_far(c):
        encode(map_b_out, map_b_out_code, c)
        far_b(c).start()
    each(both(near, head), send_far)

    fetch[3].wait()
    fetch[4].wait()

    def make_mask():
        spread = 128
        units = anchor_ref.shape[1]
        nearest = jnp.broadcast_to(anchor_ref[...], (spread, units)).T
        start = me * typed - half
        lanes = lax.broadcasted_iota(jnp.int32, (units, spread), 1)
        for j in range(0, typed + 2 * half, spread):
            within = jnp.abs(lanes + (start + j) - nearest) <= half
            coef = coef_ref[:, j:j + spread].astype(F32)
            masked[:, j:j + spread] = jnp.where(within, coef, 0.0).astype(BF16)

    @pl.when(g >= count // 2)
    def _():
        make_mask()

    def prepare():
        proj = (proj_hi[...], proj_lo[...])
        proj_top = (proj_hi[pl.ds(0, top), :], proj_lo[pl.ds(0, top), :])
        above = top_rows[...].reshape(traits, top) - dot3(
            halves(tail_in[...].reshape(traits, half)), proj_top, NT)
        top_rows[...] = above.reshape(chunks, rows, top)
        all_rows = jnp.concatenate([above, tail_out[...].reshape(traits, half)], axis=1)
        upper_out[...] = dot3(halves(all_rows), proj, NN).reshape(chunks, rows, half)

    def prepare_end():
        proj_top = (proj_hi[pl.ds(0, top), :], proj_lo[pl.ds(0, top), :])
        inverse = (inv_hi[...], inv_lo[...])
        gram = halves(gram_in[...])
        low = tail_out[...].reshape(traits, half)
        above = top_rows[...].reshape(traits, top) - dot3(
            halves(tail_in[...].reshape(traits, half)), proj_top, NT)
        below = low - add_in[...] + dot3(halves(low), gram, NN)
        base[...] = dot3(halves(jnp.concatenate([above, below], axis=1)), inverse, NN)
        low = map_f_out[...].reshape(half, half)
        above = -dot3(halves(map_f_in[...].reshape(half, half)), proj_top, NT)
        below = low + dot3(halves(low), gram, NN)
        enter_rows_w[...] = stacked(halves(
            dot3(halves(jnp.concatenate([above, below], axis=1)), inverse, NN)))

    @pl.when(start_group)
    def _():
        prepare()

    @pl.when(both(no(relay), no(start_group), no(late_map), no(early), no(last_head)))
    def _():
        prepare_end()

    def make_slope():
        slope = dot3(halves(map_b_in[...].reshape(half, half)),
                     (inv_hi[pl.ds(top, half), :], inv_lo[pl.ds(top, half), :]), NN)
        enter_base_w[...] = stacked(halves(slope))
        pre_slope_out[0] = slope[:, top:]
        pre_slope_out[1] = slope[:, :half]

    inner = both(no(head), no(tail))

    @pl.when(both(no(end_group), inner))
    def _():
        make_slope()
        ahead_slope(0).start()
        ahead_slope(1).start()

    @pl.when(both(head, no(start_group)))
    def _():
        enter_add_w[...] = stacked(halves(gram_out[...]))

    @pl.when(relay)
    def _():
        whole = stacked(halves(map_f_out[...].reshape(half, half)))

        def go(c, _):
            add_local(c)
            group_f(c).wait_recv()
            pass_on_f(c)
            decode(state_code, enter_f, c)
            carry_f[c] = tail_out[c] + dot_stacked(enter_f[c], whole)
            encode(carry_f, carry_code, c)
            carry_first(c)
            return 0
        lax.fori_loop(0, chunks, go, 0)
        each(True, carry_second)
        prepare_end()

    each(both(tail, no(head), start_group), lambda c: local_b(c).start())

    def step(c):
        local_b(c).wait_recv()
        upper_out[c] = upper_out[c] + dot_stacked(upper_in[c], backward_w[...])

        @pl.when(no(head))
        def _():
            local_b(c).start()
    each(both(no(tail), start_group), step)

    def step(c):
        group_f(c).wait_recv()
        pass_on_f(c)
        decode(state_code, enter_f, c)

        @pl.when(last_head)
        def _():
            upper_out[c] = add_out[pl.ds(pl.multiple_of(c * rows, rows), rows), :] - dot_stacked(
                enter_f[c], enter_add_w[...])
            encode(upper_out, upper_code, c)
            if count > 2:
                leap_b(c).start()
            else:
                group_b(c).start()
    if count > 2:
        @pl.when(last_head)
        def _():
            pl.semaphore_wait(ready, 1)
    each(both(no(start_group), no(relay)), step)
    if count > 2:
        each(last_head, lambda c: group_b(c).start())

    @pl.when(both(head, no(start_group), no(end_group)))
    def _():
        upper_out[...] = (add_out[...] - dot_stacked(
            enter_f[...].reshape(traits, half), enter_add_w[...])).reshape(chunks, rows, half)
    each(both(end_group, head), lambda c: half_b(c).start())

    def relay_back():
        whole = stacked(halves(map_b_out[...].reshape(half, half)))

        @pl.when(leap)
        def _():
            def take(c, _):
                far_b(c).wait_recv()
                decode(far_code, far_map, c)
                return 0
            lax.fori_loop(0, chunks, take, 0)
            far_w[...] = stacked(halves(far_map[...].reshape(half, half)))

        def go(c, _):
            group_b(c).wait_recv()
            decode(enter_code, enter_b, c)

            @pl.when(leap)
            def _():
                leap_b(c).wait_recv()
                decode(leap_code, leap_in, c)
                enter_b[c] = enter_b[c] + dot_stacked(leap_in[c], far_w[...])

            @pl.when(no(start_group))
            def _():
                upper_out[c] = upper_out[c] + dot_stacked(enter_b[c], whole)

            @pl.when(both(no(start_group), no(near)))
            def _():
                encode(upper_out, upper_code, c)
                group_b(c).start()

            @pl.when(leap)
            def _():
                encode(enter_b, mid_code, c)
                mid_b(c).start()

            @pl.when(both(leap, gives_b))
            def _():
                pass_mid(c).start()

            @pl.when(no(leap))
            def _():
                pass_on_b(c)
            return 0
        lax.fori_loop(0, chunks, go, 0)
        each(both(no(start_group), no(near)), lambda c: half_b(c).start())

    def send_near(c):
        encode(upper_out, upper_code, c)
        group_b(c).start()
    each(both(near, head), send_near)

    @pl.when(late_map)
    def _():
        map_last()

    @pl.when(both(head, no(start_group), no(end_group)))
    def _():
        pl.semaphore_signal(credit, inc=1, device_id={"genome": left},
                            device_id_type=pl.DeviceIdType.MESH)

    @pl.when(early)
    def _():
        relay_back()

    @pl.when(both(head, no(start_group)))
    def _():
        prepare_end()

    @pl.when(no(start_group))
    def _():
        base[...] += dot_stacked(enter_f[...].reshape(traits, half), enter_rows_w[...])

    @pl.when(start_group)
    def _():
        base[:, :top] = top_rows[...].reshape(traits, top)
        base[:, top:] = (tail_out[...] - upper_in[...]).reshape(traits, half)
        base[...] = dot3(halves(base[...]), (inv_hi[...], inv_lo[...]), NN)

    @pl.when(both(no(end_group), no(inner)))
    def _():
        make_slope()

    @pl.when(no(end_group))
    def _():
        pre_base_out[0] = base[:, top:]
        pre_base_out[1] = base[:, :half]
        each(tail, lambda c: group_f(c).wait_send())
        each(tail, lambda c: head_f(c).wait_send())

        @pl.when(no(head))
        def _():
            ahead_base(1).start()

        @pl.when(tail)
        def _():
            ahead_slope(1).start()

        @pl.when(both(tail, g + 2 < count))
        def _():
            pl.semaphore_wait(credit, 1)

        ahead_base(0).start()

        @pl.when(no(inner))
        def _():
            ahead_slope(0).start()

    @pl.when(g < count // 2)
    def _():
        make_mask()

    def drain_early():
        each(both(no(start_group), no(tail)), lambda c: map_f(c).wait_send())
        each(no(tail), lambda c: local_f(c).wait_send())
        each(both(jnp.logical_or(gives_left, gives_right), no(start_group)),
             lambda c: pass_f_left(c).wait_send())
        each(both(no(end_group), no(head)), lambda c: map_b(c).wait_send())
        each(both(no(head), start_group), lambda c: local_b(c).wait_send())

    @pl.when(g < count // 2)
    def _():
        drain_early()

    @pl.when(both(no(end_group), head, no(early)))
    def _():
        relay_back()

    def step(c):
        group_b(c).wait_recv()
        pass_on_b(c)
        decode(enter_code, enter_b, c)
    each(both(no(end_group), no(head)), step)

    @pl.when(no(end_group))
    def _():
        base[...] -= dot_stacked(enter_b[...].reshape(traits, half), enter_base_w[...])

    weights = base[...].astype(BF16)
    left_out[...] = weights[:, top:]
    right_out[...] = weights[:, :half]

    late_right = both(end_group, no(last))
    late_left = both(no(first), jnp.logical_or(head, end_group))

    @pl.when(late_right)
    def _():
        to_right().start()

    @pl.when(late_left)
    def _():
        to_left().start()

    def edge(side, state):
        for copy in ahead(side):
            copy.wait_recv()
        return (pre_base_in[side] - dot_stacked(
            state.reshape(traits, half), stacked(halves(pre_slope_in[side])))).astype(BF16)

    @pl.when(both(no(end_group), no(head)))
    def _():
        left_in[...] = edge(0, enter_b[...])

    @pl.when(both(head, no(start_group)))
    def _():
        left_in[...] = edge(0, upper_out[...])

    @pl.when(both(no(end_group), no(tail)))
    def _():
        right_in[...] = edge(1, enter_b[...])

    out_ref[...] = product(weights, masked[:, half:half + typed], NT)

    @pl.when(both(no(last), jnp.logical_or(tail, end_group)))
    def _():
        to_left().wait_recv()

    out_ref[...] += product(right_in[...], masked[:, half + typed:], NT)

    @pl.when(both(end_group, no(head)))
    def _():
        to_right().wait_recv()

    out_ref[...] += product(left_in[...], masked[:, :half], NT)

    @pl.when(g >= count // 2)
    def _():
        drain_early()

    each(both(head, no(start_group)), lambda c: group_b(c).wait_send())
    each(both(head, no(start_group), no(near)), lambda c: half_b(c).wait_send())
    each(both(head, leap), lambda c: mid_b(c).wait_send())
    each(both(head, near), lambda c: far_b(c).wait_send())
    if count > 2:
        each(last_head, lambda c: leap_b(c).wait_send())
    each(both(gives_b, no(end_group)), lambda c: pass_b(c).wait_send())

    @pl.when(both(no(start_group), no(head)))
    def _():
        to_left_gram().wait_send()
        to_left_add().wait_send()

    @pl.when(late_right)
    def _():
        to_right().wait_send()

    @pl.when(late_left)
    def _():
        to_left().wait_send()

    @pl.when(no(end_group))
    def _():
        for copy in ahead(0):
            copy.wait_send()

    @pl.when(both(no(end_group), no(head)))
    def _():
        for copy in ahead(1):
            copy.wait_send()


def per_device(n, z_typed, diag_inverse, coupling, impute_coef, anchor):
    traits, typed = z_typed.shape
    half = coupling.shape[2]
    units, span = impute_coef.shape
    top = typed - half
    chunks = next(k for k in (4, 2, 1) if traits % (16 * k) == half % (8 * k) == 0 or k == 1)
    rows = traits // chunks
    group = 1
    while n % (2 * group) == 0 and 4 * group * group <= n:
        group *= 2
    state = pltpu.VMEM((chunks, rows, half), F32)
    whole_state = pltpu.VMEM((traits, half), F32)
    square = pltpu.VMEM((half, half), F32)
    edge = pltpu.VMEM((traits, half), BF16)
    coded = pltpu.VMEM((chunks, rows, half), jnp.int16)
    scales = pltpu.VMEM((chunks, 1, half), F32)
    coded_map = pltpu.VMEM((chunks, half // chunks, half), jnp.int16)
    chain_map = pltpu.VMEM((chunks, half // chunks, half), F32)
    return pl.pallas_call(
        functools.partial(kernel, n, group),
        out_shape=jax.ShapeDtypeStruct((traits, units), F32),
        in_specs=[pl.BlockSpec(memory_space=pltpu.HBM)] * 5,
        out_specs=pl.BlockSpec(memory_space=pltpu.VMEM),
        scratch_shapes=[
            pltpu.VMEM((traits, typed), F32), pltpu.VMEM((typed, typed), F32),
            pltpu.VMEM((typed, half), F32), pltpu.VMEM((units, span), BF16),
            pltpu.VMEM((1, units), jnp.int32), pltpu.SemaphoreType.DMA((5,)),
            state, state, state, state, state, state, state,
            chain_map, chain_map, chain_map, chain_map, edge, edge, edge, edge,
            pltpu.VMEM((chunks, rows, top), F32), pltpu.VMEM((traits, typed), F32),
            pltpu.VMEM((3 * half, typed), BF16), pltpu.VMEM((3 * half, half), BF16),
            pltpu.VMEM((3 * half, typed), BF16),
            pltpu.VMEM((3 * half, half), BF16), pltpu.VMEM((3 * half, half), BF16),
            pltpu.VMEM((typed, typed), BF16), pltpu.VMEM((typed, typed), BF16),
            pltpu.VMEM((typed, half), BF16), pltpu.VMEM((typed, half), BF16),
            pltpu.VMEM((units, span), BF16),
            pltpu.VMEM((2, traits, half), F32), pltpu.VMEM((2, traits, half), F32),
            pltpu.VMEM((2, half, half), F32), pltpu.VMEM((2, half, half), F32),
            pltpu.SemaphoreType.DMA((2, 2)), pltpu.SemaphoreType.DMA((2, 2)),
            whole_state, whole_state, whole_state, square, square,
            pltpu.SemaphoreType.DMA((4,)), pltpu.SemaphoreType.DMA((4,)), pltpu.SemaphoreType.REGULAR,
            coded, scales, coded, scales, coded, scales, coded, scales,
            coded, scales, coded, scales, coded_map, scales, coded_map, scales,
            coded_map, scales, coded_map, scales,
            pltpu.VMEM((2, half, half), jnp.int16), pltpu.VMEM((2, 1, half), F32),
            pltpu.VMEM((2, traits, half), jnp.int16), pltpu.VMEM((2, 1, half), F32),
            state, coded, scales, coded, scales, chain_map, coded_map, scales,
            pltpu.VMEM((3 * half, half), BF16), pltpu.SemaphoreType.REGULAR,
            pltpu.SemaphoreType.DMA((25, chunks)), pltpu.SemaphoreType.DMA((15, chunks)),
            pltpu.SemaphoreType.DMA((2,)), pltpu.SemaphoreType.DMA((2,)),
        ],
        compiler_params=pltpu.CompilerParams(
            collective_id=0, has_side_effects=True, vmem_limit_bytes=int(53.25 * 1024 * 1024)),
    )(z_typed, diag_inverse[0], coupling[0], impute_coef, anchor.reshape(1, units))


def solution(mesh):
    shared = ("seg", "genome")
    in_specs = (P(None, shared), P(shared, None, None), P(shared, None, None),
                P(shared, None), P(shared))
    return jax.shard_map(
        functools.partial(per_device, mesh.shape["genome"]), mesh=mesh, in_specs=in_specs,
        out_specs=P(None, shared), check_vma=False)
```

```python
import functools

import jax
import jax.numpy as jnp
from jax import lax
from jax.experimental import pallas as pl
from jax.experimental.pallas import tpu as pltpu
from jax.sharding import PartitionSpec as P

F32 = jnp.float32
BF16 = jnp.bfloat16
NN = (((1,), (0,)), ((), ()))
NT = (((1,), (1,)), ((), ()))


def halves(x):
    high = x.astype(BF16)
    return high, (x - high.astype(F32)).astype(BF16)


def product(a, b, dims):
    return lax.dot_general(a, b, dims, preferred_element_type=F32)


def dot3(a, b, dims):
    return product(a[0], b[0], dims) + (product(a[0], b[1], dims) + product(a[1], b[0], dims))


def stacked(b):
    return jnp.concatenate([b[0], b[0], b[1]], axis=0)


def dot_stacked(x, weights):
    high, low = halves(x)
    return product(jnp.concatenate([high, low, high], axis=1), weights, NN)


class Both:
    def __init__(self, *copies):
        self.copies = copies

    def start(self):
        for copy in self.copies:
            copy.start()

    def wait_recv(self):
        for copy in self.copies:
            copy.wait_recv()

    def wait_send(self):
        for copy in self.copies:
            copy.wait_send()


def kernel(
    n, group, z_hbm, inverse_hbm, couple_hbm, coef_hbm, anchor_hbm, out_ref,
    z_ref, inverse_ref, couple_ref, coef_ref, anchor_ref, fetched,
    tail_in, tail_out, upper_in, upper_out, enter_f, enter_b, carry_f,
    map_f_in, map_f_out, map_b_in, map_b_out, left_in, right_in, left_out, right_out,
    top_rows, base, enter_rows_w, enter_add_w, enter_base_w, forward_w, backward_w, inv_hi, inv_lo, proj_hi, proj_lo, masked,
    pre_base_out, pre_base_in, pre_slope_out, pre_slope_in, ps, pr,
    own, add_in, add_out, gram_in, gram_out, rs, rr, credit,
    upper_q, upper_s, enter_q, enter_s, carry_q, carry_s, state_q, state_s,
    tail_out_q, tail_out_s, tail_in_q, tail_in_s, map_f_out_q, map_f_out_s, map_f_in_q, map_f_in_s,
    map_b_out_q, map_b_out_s, map_b_in_q, map_b_in_s, gram_q, gram_s, add_q, add_s,
    leap_in, leap_q, leap_s, mid_q, mid_s, far_map, far_q, far_s, far_w, ready,
    sent, got, es, er,
):
    me = lax.axis_index("genome")
    count = n // group
    g, q = me // group, lax.rem(me, group)
    first, last = me == 0, me == n - 1
    head, tail = q == 0, q == group - 1
    start_group, end_group = g == 0, g == count - 1
    right, left = lax.rem(me + 1, n), lax.rem(me + n - 1, n)
    far_right, far_left = lax.rem(me + group, n), lax.rem(me + n - group, n)
    chunks, rows, half = tail_in.shape
    typed = inverse_ref.shape[0]
    top = typed - half
    traits = chunks * rows
    no = jnp.logical_not
    fetch = [
        pltpu.make_async_copy(src, dst, fetched.at[i])
        for i, (src, dst) in enumerate((
            (inverse_hbm, inverse_ref), (z_hbm, z_ref), (couple_hbm, couple_ref),
            (anchor_hbm, anchor_ref), (coef_hbm, coef_ref)))]
    for copy in fetch:
        copy.start()

    def both(*conditions):
        return functools.reduce(jnp.logical_and, conditions)

    barrier = pltpu.get_barrier_semaphore()
    middle = group // 2
    half_right, half_left = lax.rem(me + middle, n), lax.rem(me + n - middle, n)
    to_end = g == count - 2
    near = g == (count - 2 if count > 2 else n)
    leap = g == (count - 3 if count > 2 else n)
    leap_left = lax.rem(me + 2 * n - 2 * group, n)
    expected = 0
    for other, meets in (
            (left, no(first)), (right, no(last)), (half_left, both(head, no(start_group))),
            (half_right, both(q == middle, no(end_group))),
            (half_left, both(q == middle, leap)), (half_right, both(head, leap)),
            (far_left, no(start_group)), (far_right, no(end_group))):
        expected += jnp.where(meets, 1, 0)

        @pl.when(meets)
        def _():
            pl.semaphore_signal(barrier, inc=1, device_id={"genome": other},
                                device_id_type=pl.DeviceIdType.MESH)

    def remote(src, dst, send, recv, other):
        return pltpu.make_async_remote_copy(
            src_ref=src, dst_ref=dst, send_sem=send, recv_sem=recv,
            device_id={"genome": other}, device_id_type=pl.DeviceIdType.MESH)

    def channel(index, src, dst, landing, other):
        return lambda c: remote(src.at[c], dst.at[c], sent.at[index, c], got.at[landing, c], other)

    def coded_channel(i, j, src, dst, k, l, other):
        values, factors = channel(i, src[0], dst[0], k, other), channel(j, src[1], dst[1], l, other)
        return lambda c: Both(values(c), factors(c))

    def encode(ref, code, c):
        values = ref[c]
        peak = jnp.maximum(jnp.max(jnp.abs(values), axis=0, keepdims=True), 1e-30)
        code[1][c] = peak * (1.0 / 32000.0)
        code[0][c] = jnp.round(values * (32000.0 / peak)).astype(jnp.int32).astype(jnp.int16)

    def decode(code, ref, c):
        ref[c] = code[0][c].astype(jnp.int32).astype(F32) * code[1][c]

    def encode_whole(ref, code, scale):
        values = ref[...]
        peak = jnp.maximum(jnp.max(jnp.abs(values), axis=0, keepdims=True), 1e-30)
        scale[0] = peak * (1.0 / 32000.0)
        code[0] = jnp.round(values * (32000.0 / peak)).astype(jnp.int32).astype(jnp.int16)

    def send_gram():
        encode_whole(gram_out, gram_q, gram_s)
        to_left_gram().start()

    def send_add():
        encode_whole(add_out, add_q, add_s)
        to_left_add().start()

    upper_code, enter_code = (upper_q, upper_s), (enter_q, enter_s)
    carry_code, state_code = (carry_q, carry_s), (state_q, state_s)
    tail_out_code, tail_in_code = (tail_out_q, tail_out_s), (tail_in_q, tail_in_s)
    map_f_out_code, map_f_in_code = (map_f_out_q, map_f_out_s), (map_f_in_q, map_f_in_s)
    map_b_out_code, map_b_in_code = (map_b_out_q, map_b_out_s), (map_b_in_q, map_b_in_s)
    map_f = coded_channel(0, 13, map_f_out_code, map_f_in_code, 0, 7, right)
    local_f = coded_channel(1, 14, tail_out_code, tail_in_code, 1, 8, right)
    group_f = coded_channel(2, 15, carry_code, state_code, 2, 9, far_right)
    head_f = coded_channel(8, 17, carry_code, state_code, 2, 9, right)
    pass_f_left = coded_channel(3, 16, state_code, state_code, 2, 9, left)
    pass_f_right = coded_channel(3, 16, state_code, state_code, 2, 9, right)
    map_b = coded_channel(4, 18, map_b_out_code, map_b_in_code, 3, 10, left)
    local_b = channel(5, upper_out, upper_in, 4, left)

    group_b = coded_channel(6, 10, upper_code, enter_code, 5, 6, far_left)
    half_b = coded_channel(9, 11, upper_code, enter_code, 5, 6, half_left)
    pass_b = coded_channel(7, 12, enter_code, enter_code, 5, 6, right)
    leap_code, mid_code, far_code = (leap_q, leap_s), (mid_q, mid_s), (far_q, far_s)
    leap_b = coded_channel(19, 20, upper_code, leap_code, 11, 12, leap_left)
    far_b = coded_channel(21, 22, map_b_out_code, far_code, 13, 14, far_left)
    mid_b = coded_channel(23, 24, mid_code, enter_code, 5, 6, half_right)
    pass_mid = coded_channel(7, 12, mid_code, enter_code, 5, 6, right)

    gives_left, gives_right = q > middle, q + 1 < middle
    gives_b = lax.rem(q + 1, middle) != 0

    def pass_on_f(c):
        @pl.when(gives_left)
        def _():
            pass_f_left(c).start()

        @pl.when(gives_right)
        def _():
            pass_f_right(c).start()

    def pass_on_b(c):
        @pl.when(gives_b)
        def _():
            pass_b(c).start()

    def carry_first(c):
        @pl.when(to_end)
        def _():
            head_f(c).start()

        @pl.when(no(to_end))
        def _():
            group_f(c).start()

    def carry_second(c):
        @pl.when(to_end)
        def _():
            group_f(c).start()

        @pl.when(no(to_end))
        def _():
            head_f(c).start()

    def to_left_gram():
        return Both(remote(gram_q.at[0], gram_q.at[1], rs.at[0], rr.at[0], left),
                    remote(gram_s.at[0], gram_s.at[1], rs.at[2], rr.at[2], left))

    def to_left_add():
        return Both(remote(add_q.at[0], add_q.at[1], rs.at[1], rr.at[1], left),
                    remote(add_s.at[0], add_s.at[1], rs.at[3], rr.at[3], left))

    def to_right():
        return remote(left_out, left_in, es.at[0], er.at[0], right)

    def to_left():
        return remote(right_out, right_in, es.at[1], er.at[1], left)

    def ahead_base(side):
        return remote(pre_base_out.at[side], pre_base_in.at[side], ps.at[side, 0], pr.at[side, 0],
                      (right, left)[side])

    def ahead_slope(side):
        return remote(pre_slope_out.at[side], pre_slope_in.at[side], ps.at[side, 1], pr.at[side, 1],
                      (right, left)[side])

    def ahead(side):
        return ahead_base(side), ahead_slope(side)

    def each(condition, step):
        @pl.when(condition)
        def _():
            def go(c, _):
                step(c)
                return 0
            lax.fori_loop(0, chunks, go, 0)

    def clear(condition, ref):
        @pl.when(condition)
        def _():
            ref[...] = jnp.zeros_like(ref)

    def unit(condition, ref):
        @pl.when(condition)
        def _():
            row = lax.broadcasted_iota(jnp.int32, (half, half), 0)
            col = lax.broadcasted_iota(jnp.int32, (half, half), 1)
            ref[...] = (row == col).astype(F32).reshape(ref.shape)

    fetch[0].wait()
    hi, lo = halves(inverse_ref[...])
    inv_hi[...] = hi
    inv_lo[...] = lo
    fetch[1].wait()
    z_halves = halves(z_ref[...])
    solved = dot3(z_halves, (inv_hi[pl.ds(top, half), :], inv_lo[pl.ds(top, half), :]), NT)
    tail_out[...] = solved.reshape(chunks, rows, half)
    pl.semaphore_wait(barrier, expected)

    @pl.when(both(near, head))
    def _():
        pl.semaphore_signal(ready, inc=1, device_id={"genome": far_right},
                            device_id_type=pl.DeviceIdType.MESH)

    def send_local(c):
        encode(tail_out, tail_out_code, c)
        local_f(c).start()

    def send_map_f(c):
        encode(map_f_out, map_f_out_code, c)
        map_f(c).start()

    def send_map_b(c):
        encode(map_b_out, map_b_out_code, c)
        map_b(c).start()

    each(both(head, start_group, no(tail)), send_local)

    fetch[2].wait()
    projected = dot3((inv_hi[...], inv_lo[...]), halves(couple_ref[...]), NN)
    hi, lo = halves(projected)
    proj_hi[...] = hi
    proj_lo[...] = lo
    chain = -projected[top:, :]
    chain_t = chain.T
    map_f_out[...] = chain_t.reshape(map_f_out.shape)
    map_b_out[...] = chain.reshape(map_b_out.shape)
    forward_w[...] = stacked(halves(chain_t))
    backward_w[...] = stacked(halves(chain))

    each(both(head, no(start_group), no(tail)), send_map_f)
    each(both(head, no(start_group), no(tail)), send_local)
    each(both(tail, no(end_group), no(head)), send_map_b)

    clear(head, tail_in)
    clear(both(tail, start_group), upper_in)
    clear(start_group, enter_f)
    clear(both(tail, no(start_group)), gram_in)
    clear(both(tail, no(start_group)), add_in)
    clear(end_group, enter_b)
    clear(first, left_in)
    clear(last, right_in)
    unit(jnp.logical_or(head, start_group), map_f_in)
    unit(jnp.logical_or(tail, end_group), map_b_in)

    def solve_top():
        solved_top = dot3(z_halves, (inv_hi[pl.ds(0, top), :], inv_lo[pl.ds(0, top), :]), NT)
        top_rows[...] = solved_top.reshape(chunks, rows, top)

    @pl.when(no(start_group))
    def _():
        proj = (proj_hi[...], proj_lo[...])
        projected_t = jnp.concatenate([projected[:top, :].T, -chain_t], axis=1)
        gram_out[...] = dot3(halves(projected_t), proj, NN)

        @pl.when(tail)
        def _():
            send_gram()

        solve_top()
        own[...] = tail_out[...].reshape(traits, half)
        rows_now = jnp.concatenate([top_rows[...].reshape(traits, top), own[...]], axis=1)
        add_out[...] = dot3(halves(rows_now), proj, NN)

        @pl.when(tail)
        def _():
            send_add()

    def fold():
        to_left_gram().wait_recv()
        gram_in[...] = gram_q[1].astype(jnp.int32).astype(F32) * gram_s[1]
        gram = halves(gram_in[...])
        step_map = (forward_w[pl.ds(0, half), :], forward_w[pl.ds(2 * half, half), :])
        gram_out[...] += dot_stacked(dot3(step_map, gram, NN), backward_w[...])

        @pl.when(no(head))
        def _():
            send_gram()

        to_left_add().wait_recv()
        add_in[...] = add_q[1].astype(jnp.int32).astype(F32) * add_s[1]
        add_out[...] += dot_stacked(add_in[...] - dot3(halves(own[...]), gram, NN), backward_w[...])

        @pl.when(no(head))
        def _():
            send_add()

    def map_step(c):
        map_b(c).wait_recv()
        decode(map_b_in_code, map_b_in, c)
        map_b_out[c] = dot_stacked(map_b_in[c], backward_w[...])
        send_map_b(c)
    soon_map = both(no(start_group), no(end_group), no(tail), no(head), q >= middle)

    @pl.when(both(no(start_group), no(tail), q >= middle))
    def _():
        fold()

    each(soon_map, map_step)

    relay = both(no(start_group), no(end_group), tail)

    def step(c):
        map_f(c).wait_recv()
        decode(map_f_in_code, map_f_in, c)
        map_f_out[c] = dot_stacked(map_f_in[c], forward_w[...])

        @pl.when(no(tail))
        def _():
            send_map_f(c)
    each(both(no(start_group), no(head)), step)

    def add_local(c):
        local_f(c).wait_recv()
        decode(tail_in_code, tail_in, c)
        tail_out[c] = tail_out[c] + dot_stacked(tail_in[c], forward_w[...])

    def step(c):
        add_local(c)

        @pl.when(no(tail))
        def _():
            send_local(c)
    each(both(no(start_group), no(head), no(relay)), step)

    def step(c):
        local_f(c).wait_recv()
        decode(tail_in_code, tail_in, c)
        tail_out[c] = tail_out[c] + dot_stacked(tail_in[c], forward_w[...])

        @pl.when(no(tail))
        def _():
            send_local(c)

        @pl.when(both(tail, start_group, no(end_group)))
        def _():
            carry_f[c] = tail_out[c]
            encode(carry_f, carry_code, c)
            carry_first(c)
    each(both(start_group, no(head)), step)
    each(both(tail, start_group, no(end_group)), carry_second)
    @pl.when(both(no(start_group), q < middle))
    def _():
        fold()

    @pl.when(start_group)
    def _():
        solve_top()

    last_head = both(end_group, head)
    early = both(head, no(start_group), to_end)
    late_map = both(head, no(start_group), no(end_group), no(early))
    each(both(no(end_group), no(tail), no(head), no(soon_map)), map_step)

    def map_last():
        def go(c, _):
            map_b(c).wait_recv()
            decode(map_b_in_code, map_b_in, c)
            return 0
        lax.fori_loop(0, chunks, go, 0)
        map_b_out[...] = dot_stacked(
            map_b_in[...].reshape(half, half), backward_w[...]).reshape(map_b_out.shape)

    @pl.when(both(no(end_group), head, no(late_map)))
    def _():
        map_last()

    def send_far(c):
        encode(map_b_out, map_b_out_code, c)
        far_b(c).start()
    each(both(near, head), send_far)

    fetch[3].wait()
    fetch[4].wait()

    def make_mask():
        spread = 128
        units = anchor_ref.shape[1]
        nearest = jnp.broadcast_to(anchor_ref[...], (spread, units)).T
        start = me * typed - half
        lanes = lax.broadcasted_iota(jnp.int32, (units, spread), 1)
        for j in range(0, typed + 2 * half, spread):
            within = jnp.abs(lanes + (start + j) - nearest) <= half
            coef = coef_ref[:, j:j + spread].astype(F32)
            masked[:, j:j + spread] = jnp.where(within, coef, 0.0).astype(BF16)

    @pl.when(g >= count // 2)
    def _():
        make_mask()

    def prepare():
        proj = (proj_hi[...], proj_lo[...])
        proj_top = (proj_hi[pl.ds(0, top), :], proj_lo[pl.ds(0, top), :])
        above = top_rows[...].reshape(traits, top) - dot3(
            halves(tail_in[...].reshape(traits, half)), proj_top, NT)
        top_rows[...] = above.reshape(chunks, rows, top)
        all_rows = jnp.concatenate([above, tail_out[...].reshape(traits, half)], axis=1)
        upper_out[...] = dot3(halves(all_rows), proj, NN).reshape(chunks, rows, half)

    def prepare_end():
        proj_top = (proj_hi[pl.ds(0, top), :], proj_lo[pl.ds(0, top), :])
        inverse = (inv_hi[...], inv_lo[...])
        gram = halves(gram_in[...])
        low = tail_out[...].reshape(traits, half)
        above = top_rows[...].reshape(traits, top) - dot3(
            halves(tail_in[...].reshape(traits, half)), proj_top, NT)
        below = low - add_in[...] + dot3(halves(low), gram, NN)
        base[...] = dot3(halves(jnp.concatenate([above, below], axis=1)), inverse, NN)
        low = map_f_out[...].reshape(half, half)
        above = -dot3(halves(map_f_in[...].reshape(half, half)), proj_top, NT)
        below = low + dot3(halves(low), gram, NN)
        enter_rows_w[...] = stacked(halves(
            dot3(halves(jnp.concatenate([above, below], axis=1)), inverse, NN)))

    @pl.when(start_group)
    def _():
        prepare()

    @pl.when(both(no(relay), no(start_group), no(late_map), no(early), no(last_head)))
    def _():
        prepare_end()

    def make_slope():
        slope = dot3(halves(map_b_in[...].reshape(half, half)),
                     (inv_hi[pl.ds(top, half), :], inv_lo[pl.ds(top, half), :]), NN)
        enter_base_w[...] = stacked(halves(slope))
        pre_slope_out[0] = slope[:, top:]
        pre_slope_out[1] = slope[:, :half]

    inner = both(no(head), no(tail))

    @pl.when(both(no(end_group), inner))
    def _():
        make_slope()
        ahead_slope(0).start()
        ahead_slope(1).start()

    @pl.when(both(head, no(start_group)))
    def _():
        enter_add_w[...] = stacked(halves(gram_out[...]))

    @pl.when(relay)
    def _():
        whole = stacked(halves(map_f_out[...].reshape(half, half)))

        def go(c, _):
            add_local(c)
            group_f(c).wait_recv()
            pass_on_f(c)
            decode(state_code, enter_f, c)
            carry_f[c] = tail_out[c] + dot_stacked(enter_f[c], whole)
            encode(carry_f, carry_code, c)
            carry_first(c)
            return 0
        lax.fori_loop(0, chunks, go, 0)
        each(True, carry_second)
        prepare_end()

    each(both(tail, no(head), start_group), lambda c: local_b(c).start())

    def step(c):
        local_b(c).wait_recv()
        upper_out[c] = upper_out[c] + dot_stacked(upper_in[c], backward_w[...])

        @pl.when(no(head))
        def _():
            local_b(c).start()
    each(both(no(tail), start_group), step)

    def step(c):
        group_f(c).wait_recv()
        pass_on_f(c)
        decode(state_code, enter_f, c)

        @pl.when(last_head)
        def _():
            upper_out[c] = add_out[pl.ds(pl.multiple_of(c * rows, rows), rows), :] - dot_stacked(
                enter_f[c], enter_add_w[...])
            encode(upper_out, upper_code, c)
            if count > 2:
                leap_b(c).start()
            else:
                group_b(c).start()
    if count > 2:
        @pl.when(last_head)
        def _():
            pl.semaphore_wait(ready, 1)
    each(both(no(start_group), no(relay)), step)
    if count > 2:
        each(last_head, lambda c: group_b(c).start())

    @pl.when(both(head, no(start_group), no(end_group)))
    def _():
        upper_out[...] = (add_out[...] - dot_stacked(
            enter_f[...].reshape(traits, half), enter_add_w[...])).reshape(chunks, rows, half)
    each(both(end_group, head), lambda c: half_b(c).start())

    def relay_back():
        whole = stacked(halves(map_b_out[...].reshape(half, half)))

        @pl.when(leap)
        def _():
            def take(c, _):
                far_b(c).wait_recv()
                decode(far_code, far_map, c)
                return 0
            lax.fori_loop(0, chunks, take, 0)
            far_w[...] = stacked(halves(far_map[...].reshape(half, half)))

        def go(c, _):
            group_b(c).wait_recv()
            decode(enter_code, enter_b, c)

            @pl.when(leap)
            def _():
                leap_b(c).wait_recv()
                decode(leap_code, leap_in, c)
                enter_b[c] = enter_b[c] + dot_stacked(leap_in[c], far_w[...])

            @pl.when(no(start_group))
            def _():
                upper_out[c] = upper_out[c] + dot_stacked(enter_b[c], whole)

            @pl.when(both(no(start_group), no(near)))
            def _():
                encode(upper_out, upper_code, c)
                group_b(c).start()
                half_b(c).start()

            @pl.when(leap)
            def _():
                encode(enter_b, mid_code, c)
                mid_b(c).start()

            @pl.when(both(leap, gives_b))
            def _():
                pass_mid(c).start()

            @pl.when(no(leap))
            def _():
                pass_on_b(c)
            return 0
        lax.fori_loop(0, chunks, go, 0)

    def send_near(c):
        encode(upper_out, upper_code, c)
        group_b(c).start()
    each(both(near, head), send_near)

    @pl.when(late_map)
    def _():
        map_last()

    @pl.when(both(head, no(start_group), no(end_group)))
    def _():
        pl.semaphore_signal(credit, inc=1, device_id={"genome": left},
                            device_id_type=pl.DeviceIdType.MESH)

    @pl.when(early)
    def _():
        relay_back()

    @pl.when(both(head, no(start_group)))
    def _():
        prepare_end()

    @pl.when(no(start_group))
    def _():
        base[...] += dot_stacked(enter_f[...].reshape(traits, half), enter_rows_w[...])

    @pl.when(start_group)
    def _():
        base[:, :top] = top_rows[...].reshape(traits, top)
        base[:, top:] = (tail_out[...] - upper_in[...]).reshape(traits, half)
        base[...] = dot3(halves(base[...]), (inv_hi[...], inv_lo[...]), NN)

    @pl.when(both(no(end_group), no(inner)))
    def _():
        make_slope()

    @pl.when(no(end_group))
    def _():
        pre_base_out[0] = base[:, top:]
        pre_base_out[1] = base[:, :half]
        each(tail, lambda c: group_f(c).wait_send())
        each(tail, lambda c: head_f(c).wait_send())

        @pl.when(no(head))
        def _():
            ahead_base(1).start()

        @pl.when(tail)
        def _():
            ahead_slope(1).start()

        @pl.when(both(tail, g + 2 < count))
        def _():
            pl.semaphore_wait(credit, 1)

        ahead_base(0).start()

        @pl.when(no(inner))
        def _():
            ahead_slope(0).start()

    @pl.when(g < count // 2)
    def _():
        make_mask()

    def drain_early():
        each(both(no(start_group), no(tail)), lambda c: map_f(c).wait_send())
        each(no(tail), lambda c: local_f(c).wait_send())
        each(both(jnp.logical_or(gives_left, gives_right), no(start_group)),
             lambda c: pass_f_left(c).wait_send())
        each(both(no(end_group), no(head)), lambda c: map_b(c).wait_send())
        each(both(no(head), start_group), lambda c: local_b(c).wait_send())

    @pl.when(g < count // 2)
    def _():
        drain_early()

    @pl.when(both(no(end_group), head, no(early)))
    def _():
        relay_back()

    def step(c):
        group_b(c).wait_recv()
        pass_on_b(c)
        decode(enter_code, enter_b, c)
    each(both(no(end_group), no(head)), step)

    @pl.when(no(end_group))
    def _():
        base[...] -= dot_stacked(enter_b[...].reshape(traits, half), enter_base_w[...])

    weights = base[...].astype(BF16)
    left_out[...] = weights[:, top:]
    right_out[...] = weights[:, :half]

    late_right = both(end_group, no(last))
    late_left = both(no(first), jnp.logical_or(head, end_group))

    @pl.when(late_right)
    def _():
        to_right().start()

    @pl.when(late_left)
    def _():
        to_left().start()

    def edge(side, state):
        for copy in ahead(side):
            copy.wait_recv()
        return (pre_base_in[side] - dot_stacked(
            state.reshape(traits, half), stacked(halves(pre_slope_in[side])))).astype(BF16)

    @pl.when(both(no(end_group), no(head)))
    def _():
        left_in[...] = edge(0, enter_b[...])

    @pl.when(both(head, no(start_group)))
    def _():
        left_in[...] = edge(0, upper_out[...])

    @pl.when(both(no(end_group), no(tail)))
    def _():
        right_in[...] = edge(1, enter_b[...])

    out_ref[...] = product(weights, masked[:, half:half + typed], NT)

    @pl.when(both(no(last), jnp.logical_or(tail, end_group)))
    def _():
        to_left().wait_recv()

    out_ref[...] += product(right_in[...], masked[:, half + typed:], NT)

    @pl.when(both(end_group, no(head)))
    def _():
        to_right().wait_recv()

    out_ref[...] += product(left_in[...], masked[:, :half], NT)

    @pl.when(g >= count // 2)
    def _():
        drain_early()

    each(both(head, no(start_group)), lambda c: group_b(c).wait_send())
    each(both(head, no(start_group), no(near)), lambda c: half_b(c).wait_send())
    each(both(head, leap), lambda c: mid_b(c).wait_send())
    each(both(head, near), lambda c: far_b(c).wait_send())
    if count > 2:
        each(last_head, lambda c: leap_b(c).wait_send())
    each(both(gives_b, no(end_group)), lambda c: pass_b(c).wait_send())

    @pl.when(both(no(start_group), no(head)))
    def _():
        to_left_gram().wait_send()
        to_left_add().wait_send()

    @pl.when(late_right)
    def _():
        to_right().wait_send()

    @pl.when(late_left)
    def _():
        to_left().wait_send()

    @pl.when(no(end_group))
    def _():
        for copy in ahead(0):
            copy.wait_send()

    @pl.when(both(no(end_group), no(head)))
    def _():
        for copy in ahead(1):
            copy.wait_send()


def per_device(n, z_typed, diag_inverse, coupling, impute_coef, anchor):
    traits, typed = z_typed.shape
    half = coupling.shape[2]
    units, span = impute_coef.shape
    top = typed - half
    chunks = next(k for k in (2, 1) if traits % (16 * k) == half % (8 * k) == 0 or k == 1)
    rows = traits // chunks
    group = 1
    while n % (2 * group) == 0 and 4 * group * group <= n:
        group *= 2
    state = pltpu.VMEM((chunks, rows, half), F32)
    whole_state = pltpu.VMEM((traits, half), F32)
    square = pltpu.VMEM((half, half), F32)
    edge = pltpu.VMEM((traits, half), BF16)
    coded = pltpu.VMEM((chunks, rows, half), jnp.int16)
    scales = pltpu.VMEM((chunks, 1, half), F32)
    coded_map = pltpu.VMEM((chunks, half // chunks, half), jnp.int16)
    chain_map = pltpu.VMEM((chunks, half // chunks, half), F32)
    return pl.pallas_call(
        functools.partial(kernel, n, group),
        out_shape=jax.ShapeDtypeStruct((traits, units), F32),
        in_specs=[pl.BlockSpec(memory_space=pltpu.HBM)] * 5,
        out_specs=pl.BlockSpec(memory_space=pltpu.VMEM),
        scratch_shapes=[
            pltpu.VMEM((traits, typed), F32), pltpu.VMEM((typed, typed), F32),
            pltpu.VMEM((typed, half), F32), pltpu.VMEM((units, span), BF16),
            pltpu.VMEM((1, units), jnp.int32), pltpu.SemaphoreType.DMA((5,)),
            state, state, state, state, state, state, state,
            chain_map, chain_map, chain_map, chain_map, edge, edge, edge, edge,
            pltpu.VMEM((chunks, rows, top), F32), pltpu.VMEM((traits, typed), F32),
            pltpu.VMEM((3 * half, typed), BF16), pltpu.VMEM((3 * half, half), BF16),
            pltpu.VMEM((3 * half, typed), BF16),
            pltpu.VMEM((3 * half, half), BF16), pltpu.VMEM((3 * half, half), BF16),
            pltpu.VMEM((typed, typed), BF16), pltpu.VMEM((typed, typed), BF16),
            pltpu.VMEM((typed, half), BF16), pltpu.VMEM((typed, half), BF16),
            pltpu.VMEM((units, span), BF16),
            pltpu.VMEM((2, traits, half), F32), pltpu.VMEM((2, traits, half), F32),
            pltpu.VMEM((2, half, half), F32), pltpu.VMEM((2, half, half), F32),
            pltpu.SemaphoreType.DMA((2, 2)), pltpu.SemaphoreType.DMA((2, 2)),
            whole_state, whole_state, whole_state, square, square,
            pltpu.SemaphoreType.DMA((4,)), pltpu.SemaphoreType.DMA((4,)), pltpu.SemaphoreType.REGULAR,
            coded, scales, coded, scales, coded, scales, coded, scales,
            coded, scales, coded, scales, coded_map, scales, coded_map, scales,
            coded_map, scales, coded_map, scales,
            pltpu.VMEM((2, half, half), jnp.int16), pltpu.VMEM((2, 1, half), F32),
            pltpu.VMEM((2, traits, half), jnp.int16), pltpu.VMEM((2, 1, half), F32),
            state, coded, scales, coded, scales, chain_map, coded_map, scales,
            pltpu.VMEM((3 * half, half), BF16), pltpu.SemaphoreType.REGULAR,
            pltpu.SemaphoreType.DMA((25, chunks)), pltpu.SemaphoreType.DMA((15, chunks)),
            pltpu.SemaphoreType.DMA((2,)), pltpu.SemaphoreType.DMA((2,)),
        ],
        compiler_params=pltpu.CompilerParams(
            collective_id=0, has_side_effects=True, vmem_limit_bytes=int(53.25 * 1024 * 1024)),
    )(z_typed, diag_inverse[0], coupling[0], impute_coef, anchor.reshape(1, units))


def solution(mesh):
    shared = ("seg", "genome")
    in_specs = (P(None, shared), P(shared, None, None), P(shared, None, None),
                P(shared, None), P(shared))
    return jax.shard_map(
        functools.partial(per_device, mesh.shape["genome"]), mesh=mesh, in_specs=in_specs,
        out_specs=P(None, shared), check_vma=False)
```
